32 devices in a mesh: wide: 16 (over z, y, core), narrow: 2 (over x).
Axes of the slice: x: 2, y: 2, z: 4, core: 2. Of those that a mesh axis runs over, the one named last changes fastest.
Arguments:
- residual: bfloat16 [384, 5120], P(None, 'narrow'), may hold values from -70 to 70
- norm_gain: bfloat16 [5120], P('narrow'), may hold values from 0.5 to 1.5
- grad_out: bfloat16 [384, 5120], P(None, 'narrow'), may hold values from -6 to 6
- w_gate: bfloat16 [5120, 27648], P('narrow', 'wide'), may hold values from -0.078125 to 0.078125
- w_up: bfloat16 [5120, 27648], P('narrow', 'wide'), may hold values from -0.078125 to 0.078125
- w_down: bfloat16 [27648, 5120], P('wide', 'narrow'), may hold values from -0.0390625 to 0.0390625
- w_output: bfloat16 [5120, 5120], P('narrow', 'wide'), may hold values from -0.078125 to 0.078125
- query: bfloat16 [384, 5120], P('narrow'), may hold values from -6 to 6
- key: bfloat16 [384, 1024], P('narrow'), may hold values from -6 to 6
- value: bfloat16 [384, 1024], P('narrow'), may hold values from -6 to 6
- cache_key: bfloat16 [32768, 1024], P('wide', 'narrow'), may hold values from -10 to 10
- cache_value: bfloat16 [32768, 1024], P('wide', 'narrow'), may hold values from -6 to 6
- visible_from: int32 [384], replicated, may hold values from 0 to 16383
Outputs:
- grad_residual: bfloat16 [384, 5120], P(None, 'narrow')
- grad_gain: float32 [5120], P('narrow')
- grad_w_gate: bfloat16 [5120, 27648], P('narrow', 'wide')
- grad_w_up: bfloat16 [5120, 27648], P('narrow', 'wide')
- grad_w_down: bfloat16 [27648, 5120], P('wide', 'narrow')
- grad_w_output: bfloat16 [5120, 5120], P('narrow', 'wide')
- grad_query: bfloat16 [384, 5120], P(None, 'narrow')
The draws below stay inside these ranges and needn't reach their ends.
All inputs are finite; a program needn't handle non-finite values.
Results may differ from the reference program's by a relative error of at most 0.01.
Values may be sent and summed in bfloat16 or wider, within the bound.
A program may use at most 320 MiB of HBM per device.

```python
import math
import jax
import jax.numpy as jnp
from jax import lax

D = 5120
FF = 27648
HEADS = 40
KV_HEADS = 8
HEAD_DIM = 128
TOKENS = 384
CONTEXT = 32768


def draw_residual(key, part):
    first, second, third = jax.random.split(key, 3)
    rows = jnp.exp(jax.random.uniform(first, (TOKENS, 1), jnp.float32, math.log(0.3), math.log(3.0)))
    ramp = jnp.arange(D, dtype=jnp.float32) / D
    jitter = jnp.exp(jax.random.uniform(second, (1, D), jnp.float32, -0.3, 0.3))
    columns = (10.0 ** (ramp - 0.5))[None, :] * jitter
    base = jnp.clip(jax.random.normal(third, (TOKENS, D), jnp.float32), -5.0, 5.0)
    return (base * rows * columns).astype(jnp.bfloat16)


def attention_pair(key):
    base_seed = jax.random.fold_in(key, 11)
    query_seed, key_seed = jax.random.split(base_seed, 2)
    group = HEADS // KV_HEADS
    queries = jnp.clip(jax.random.normal(query_seed, (TOKENS, KV_HEADS, group, HEAD_DIM), jnp.float32), -5.0, 5.0)
    keys = jnp.clip(jax.random.normal(key_seed, (TOKENS, KV_HEADS, HEAD_DIM), jnp.float32), -5.0, 5.0)
    return (queries.reshape(TOKENS, HEADS * HEAD_DIM), keys.reshape(TOKENS, KV_HEADS * HEAD_DIM))


def draw_query(key, part):
    return attention_pair(key)[0].astype(jnp.bfloat16)


def draw_key(key, part):
    return attention_pair(key)[1].astype(jnp.bfloat16)


def draw_cache_key(key, part):
    ramp = jnp.arange(CONTEXT, dtype=jnp.float32) / CONTEXT
    factor = 10.0 ** (0.5 * ramp - 0.25)
    base = jnp.clip(jax.random.normal(key, (CONTEXT, KV_HEADS * HEAD_DIM), jnp.float32), -5.0, 5.0)
    return (base * factor[:, None]).astype(jnp.bfloat16)


def with_ends(result, rng, smallest, largest):
    longest = result.shape.index(max(result.shape))
    spots = []
    for shift in (0, 1):
        where = [jax.random.randint(jax.random.fold_in(rng, axis), (), 0, length) for axis, length in enumerate(result.shape)]
        where[longest] = (where[longest] + shift) % result.shape[longest]
        spots.append(tuple(where))
    return result.at[spots[0]].set(smallest).at[spots[1]].set(largest)


def block_levels(own_key, extent, cuts, least, largest):
    loudness = 1.0
    for axis_at, parts in cuts:
        heights = jax.random.uniform(jax.random.fold_in(jax.random.fold_in(own_key, 6), axis_at), (parts,), jnp.float32, least / len(cuts), largest / len(cuts))
        loudness = loudness * jnp.repeat(jnp.exp(heights), extent[axis_at] // parts).reshape((-1,) + (1,) * (len(extent) - 1 - axis_at))
    return loudness


def gaussian(key, shape, width, limit, pieces=(), kind=jnp.bfloat16):
    loudness = block_levels(key, shape, pieces, -0.22, 0.18) if pieces else 1.0
    result = jax.random.normal(key, shape, jnp.float32) * width * loudness
    return jnp.minimum(jnp.maximum(result, -limit), limit).astype(kind)


def setup_inputs(seed: int = 0) -> dict:
    arg_keys = jax.random.split(jax.random.key(seed), 14)
    return {
        "residual": draw_residual(jax.random.fold_in(arg_keys[13], 71), 0),
        "norm_gain": jnp.clip(1.0 + 0.1 * jax.random.normal(arg_keys[1], (D,), jnp.float32), 0.5, 1.5).astype(jnp.bfloat16),
        "grad_out": gaussian(arg_keys[2], (TOKENS, D), 1.0, 6.0, ((1, 2),)),
        "w_gate": gaussian(arg_keys[3], (D, FF), D ** -0.5, 0.078125, ((0, 2), (1, 16))),
        "w_up": gaussian(arg_keys[4], (D, FF), D ** -0.5, 0.078125, ((0, 2), (1, 16))),
        "w_down": gaussian(arg_keys[5], (FF, D), FF ** -0.5, 0.0390625, ((0, 16), (1, 2))),
        "w_output": gaussian(arg_keys[6], (HEADS * HEAD_DIM, D), (HEADS * HEAD_DIM) ** -0.5, 0.078125, ((0, 2), (1, 16))),
        "query": draw_query(jax.random.fold_in(arg_keys[13], 71), 0),
        "key": draw_key(jax.random.fold_in(arg_keys[13], 71), 0),
        "value": gaussian(arg_keys[9], (TOKENS, KV_HEADS * HEAD_DIM), 1.0, 6.0, ((0, 2),)),
        "cache_key": draw_cache_key(jax.random.fold_in(arg_keys[13], 71), 0),
        "cache_value": gaussian(arg_keys[11], (CONTEXT, KV_HEADS * HEAD_DIM), 1.0, 6.0, ((0, 16), (1, 2))),
        "visible_from": with_ends(jax.random.randint(arg_keys[12], (TOKENS,), 0, CONTEXT // 2), jax.random.fold_in(arg_keys[12], 1), 0, (CONTEXT // 2) - 1).astype(jnp.int32),
    }


EPSILON = 1e-06

def reference(residual, norm_gain, grad_out, w_gate, w_up, w_down, w_output, query, key, value, cache_key, cache_value, visible_from):
    stream = residual.astype(jnp.float32)
    gain = norm_gain.astype(jnp.float32)
    rstd = lax.rsqrt(lax.optimization_barrier(jnp.mean(stream * stream, axis=1, keepdims=True)) + EPSILON)
    scaled = stream * rstd
    normed = (scaled * gain).astype(jnp.bfloat16)
    gate = jnp.dot(normed, w_gate, preferred_element_type=jnp.float32)
    up = jnp.dot(normed, w_up, preferred_element_type=jnp.float32)
    hidden_grad = jnp.dot(grad_out, w_down.T, preferred_element_type=jnp.float32)
    sigmoid_gate = jax.nn.sigmoid(gate)
    silu_gate = gate * sigmoid_gate
    activated = (silu_gate * up).astype(jnp.bfloat16)
    d_gate = (hidden_grad * up * sigmoid_gate * (1.0 + gate * (1.0 - sigmoid_gate))).astype(jnp.bfloat16)
    d_up = (hidden_grad * silu_gate).astype(jnp.bfloat16)
    grad_w_down = jnp.dot(activated.T, grad_out, preferred_element_type=jnp.float32).astype(jnp.bfloat16)
    grad_w_gate = jnp.dot(normed.T, d_gate, preferred_element_type=jnp.float32).astype(jnp.bfloat16)
    grad_w_up = jnp.dot(normed.T, d_up, preferred_element_type=jnp.float32).astype(jnp.bfloat16)
    d_normed = jnp.dot(d_gate, w_gate.T, preferred_element_type=jnp.float32) + jnp.dot(d_up, w_up.T, preferred_element_type=jnp.float32)
    grad_gain = lax.optimization_barrier(jnp.sum(d_normed * scaled, axis=0))
    weighted = d_normed * gain
    inner = lax.optimization_barrier(jnp.mean(weighted * scaled, axis=1, keepdims=True))
    grad_residual = (grad_out.astype(jnp.float32) + rstd * (weighted - scaled * inner)).astype(jnp.bfloat16)
    d_attention = jnp.dot(grad_residual, w_output.T, preferred_element_type=jnp.float32).astype(jnp.bfloat16)
    group = HEADS // KV_HEADS
    every_key = jnp.concatenate([cache_key, key], axis=0).reshape(CONTEXT + TOKENS, KV_HEADS, HEAD_DIM).transpose(1, 0, 2)
    every_value = jnp.concatenate([cache_value, value], axis=0).reshape(CONTEXT + TOKENS, KV_HEADS, HEAD_DIM).transpose(1, 0, 2)
    queries = query.reshape(TOKENS, HEADS, HEAD_DIM).transpose(1, 0, 2)
    incoming = d_attention.reshape(TOKENS, HEADS, HEAD_DIM).transpose(1, 0, 2)
    position = jnp.arange(TOKENS, dtype=jnp.int32)[:, None]
    slots = jnp.arange(CONTEXT + TOKENS, dtype=jnp.int32)[None, :]
    usable = jnp.where(slots < CONTEXT, slots >= visible_from[:, None], slots - CONTEXT <= position)
    scale = 1.0 / math.sqrt(HEAD_DIM)

    def one_head(inputs):
        head_query, head_grad, index = inputs
        head_keys = lax.dynamic_index_in_dim(every_key, (index // group).astype(jnp.int32), 0, keepdims=False)
        head_values = lax.dynamic_index_in_dim(every_value, (index // group).astype(jnp.int32), 0, keepdims=False)
        scores = jnp.dot(head_query, head_keys.T, preferred_element_type=jnp.float32) * scale
        scores = jnp.where(usable, scores, -1e+30)
        highest = lax.optimization_barrier(jnp.max(scores, axis=1, keepdims=True))
        weights = jnp.where(usable, jnp.exp(scores - highest), 0.0)
        probs = weights / lax.optimization_barrier(jnp.sum(weights, axis=1, keepdims=True))
        probs_low = probs.astype(jnp.bfloat16)
        attended = jnp.dot(probs_low, head_values, preferred_element_type=jnp.float32).astype(jnp.bfloat16)
        prob_grad = jnp.dot(head_grad, head_values.T, preferred_element_type=jnp.float32)
        delta = lax.optimization_barrier(jnp.sum(head_grad.astype(jnp.float32) * attended.astype(jnp.float32), axis=1, keepdims=True))
        score_grad = (probs * (prob_grad - delta)).astype(jnp.bfloat16)
        head_query_grad = (jnp.dot(score_grad, head_keys, preferred_element_type=jnp.float32) * scale).astype(jnp.bfloat16)
        return (attended, head_query_grad)
    attended, query_grads = lax.map(one_head, (queries, incoming, jnp.arange(HEADS, dtype=jnp.int32)))
    attended = attended.transpose(1, 0, 2).reshape(TOKENS, HEADS * HEAD_DIM)
    grad_query = query_grads.transpose(1, 0, 2).reshape(TOKENS, HEADS * HEAD_DIM)
    grad_w_output = jnp.dot(attended.T, grad_residual, preferred_element_type=jnp.float32).astype(jnp.bfloat16)
    return (grad_residual, grad_gain, grad_w_gate, grad_w_up, grad_w_down, grad_w_output, grad_query)
```

```python
import functools
import math

import jax
import jax.numpy as jnp
from jax import lax
from jax.experimental import pallas as pl
from jax.experimental.pallas import tpu as pltpu
from jax.sharding import PartitionSpec as P

D = 5120
HEAD_DIM = 128


EPSILON = 1e-06


def contract_rows(left, right):
    return lax.dot_general(
        left, right, (((0,), (0,)), ((), ())), preferred_element_type=jnp.float32
    )


def contract_cols(left, right):
    return lax.dot_general(
        left, right, (((1,), (1,)), ((), ())), preferred_element_type=jnp.float32
    )


def swapped(array, axis, mask):
    size = lax.axis_size(axis)
    return lax.ppermute(array, axis, [(i, i ^ mask) for i in range(size)])


def wide_bits():
    return lax.axis_size("wide").bit_length() - 1


def bit_of(k):
    return (lax.axis_index("wide") >> k) & 1


def as_cube(array):
    count = lax.axis_size("wide")
    return array.reshape((2,) * wide_bits() + (array.shape[0] // count, array.shape[1]))


def masks(stage):
    found = [0]
    for k in stage:
        found += [mask | (1 << k) for mask in found]
    return found


def part_for(cube, stage, mask):
    for k in stage:
        cube = lax.dynamic_slice_in_dim(cube, bit_of(k) ^ ((mask >> k) & 1), 1, k)
    return cube


def scatter_sum(cube, stages):
    for stage in stages:
        low = cube.astype(jnp.bfloat16)
        total = part_for(cube, stage, 0).astype(jnp.float32)
        for mask in masks(stage)[1:]:
            got = swapped(part_for(low, stage, mask), "wide", mask)
            total = total + got.astype(jnp.float32)
        cube = total
    return cube.reshape(cube.shape[-2:])


def gathered(chunk, stages):
    cube = chunk.reshape((1,) * wide_bits() + chunk.shape)
    for stage in reversed(stages):
        held = {0: cube}
        for mask in masks(stage)[1:]:
            held[mask] = swapped(cube, "wide", mask)
        for k in stage:
            first = bit_of(k) == 0
            held = {
                mask: jnp.concatenate(
                    [
                        jnp.where(first, held[mask], held[mask | (1 << k)]),
                        jnp.where(first, held[mask | (1 << k)], held[mask]),
                    ],
                    axis=k,
                )
                for mask in held
                if not mask & (1 << k)
            }
        cube = held[0]
    return cube.reshape(-1, cube.shape[-1])


def own_rows(array):
    bits = wide_bits()
    rows = array.shape[0] // lax.axis_size("wide")
    at = sum(bit_of(k) << (bits - 1 - k) for k in range(bits))
    return lax.dynamic_slice_in_dim(array, at * rows, rows, 0)


def doubled(value, combine):
    for k in range(wide_bits()):
        value = combine(value, swapped(value, "wide", 1 << k))
    return value


def orders():
    core, side, line = (0,), (1,), tuple(range(2, wide_bits()))
    return ([core, side, line], [core, line, side])


def narrow_sum(part):
    if lax.axis_size("narrow") == 2:
        return part + swapped(part, "narrow", 1)
    return lax.psum(part, "narrow")


def narrow_total(part, low):
    if lax.axis_size("narrow") == 2:
        return part + swapped(low, "narrow", 1).astype(jnp.float32)
    return lax.psum(part, "narrow")


def after(arrays, *others):
    return lax.optimization_barrier((tuple(arrays), others))[0]


def to_heads(rows):
    if lax.axis_size("narrow") != 2:
        return lax.all_to_all(rows, "narrow", split_axis=1, concat_axis=0, tiled=True)
    place = lax.axis_index("narrow")
    half = rows.shape[1] // 2
    count = rows.shape[0] // 2
    bit = bit_of(0)
    kept = lax.dynamic_slice_in_dim(rows, place * half, half, 1)
    sent = lax.dynamic_slice(rows, (bit * count, (1 - place) * half), (count, half))
    got = swapped(sent, "narrow", 1)
    other = swapped(got, "wide", 1)
    first = bit == 0
    far = jnp.concatenate([jnp.where(first, got, other), jnp.where(first, other, got)], axis=0)
    low = place == 0
    return jnp.concatenate([jnp.where(low, kept, far), jnp.where(low, far, kept)], axis=0)


def merge_softmax(base, first, second):
    heads = first.shape[1] // 2
    top = jnp.maximum(first[:, :heads], second[:, :heads])
    total = first[:, heads:] * jnp.exp2((first[:, :heads] - top) * base) + second[
        :, heads:
    ] * jnp.exp2((second[:, :heads] - top) * base)
    return jnp.concatenate([top, total], axis=1)


def swiglu_back(gate, up, hidden_grad):
    sigmoid_gate = jax.nn.sigmoid(gate)
    silu_gate = gate * sigmoid_gate
    activated = (silu_gate * up).astype(jnp.bfloat16)
    d_gate = (hidden_grad * up * sigmoid_gate * (1.0 + gate * (1.0 - sigmoid_gate))).astype(
        jnp.bfloat16
    )
    d_up = (hidden_grad * silu_gate).astype(jnp.bfloat16)
    return (activated, d_gate, d_up)


LOG2E = 1.4426950408889634
MASKED = -1e30


def raw_scores(q, key_ref, own_key_ref, from_ref, own_ref):
    cached = contract_cols(q, key_ref[...])
    at = lax.broadcasted_iota(jnp.int32, cached.shape, 1)
    cached = jnp.where(at >= from_ref[...], cached, MASKED)
    own = contract_cols(q, own_key_ref[...])
    own_at = lax.broadcasted_iota(jnp.int32, own.shape, 1)
    own = jnp.where(own_at <= own_ref[...], own, MASKED)
    return (cached, own)


def pick_lane(stat_ref, head):
    lane = lax.broadcasted_iota(jnp.int32, stat_ref.shape, 1)
    return jnp.sum(jnp.where(lane == head, stat_ref[...], 0.0), axis=1, keepdims=True)


def forward_kernel(
    per_group, base, q_ref, key_ref, value_ref, own_key_ref, own_value_ref,
    from_ref, own_ref, out_ref, top_ref, total_ref,
):
    head = pl.program_id(0) * per_group + pl.program_id(1)

    @pl.when(head == 0)
    def _():
        top_ref[...] = jnp.zeros_like(top_ref)
        total_ref[...] = jnp.zeros_like(total_ref)

    cached, own = raw_scores(q_ref[...], key_ref, own_key_ref, from_ref, own_ref)
    top = jnp.maximum(
        jnp.max(cached, axis=1, keepdims=True), jnp.max(own, axis=1, keepdims=True)
    )
    cached = jnp.exp2((cached - top) * base)
    own = jnp.exp2((own - top) * base)
    total = jnp.sum(cached, axis=1, keepdims=True) + jnp.sum(own, axis=1, keepdims=True)
    out = jnp.dot(
        cached.astype(jnp.bfloat16), value_ref[...], preferred_element_type=jnp.float32
    ) + jnp.dot(
        own.astype(jnp.bfloat16), own_value_ref[...], preferred_element_type=jnp.float32
    )
    out_ref[...] = out.astype(out_ref.dtype)
    lane = lax.broadcasted_iota(jnp.int32, top_ref.shape, 1)
    top_ref[...] = jnp.where(lane == head, top, top_ref[...])
    total_ref[...] = jnp.where(lane == head, total, total_ref[...])


def backward_kernel(
    first_group, per_group, base, scale, q_ref, grad_ref, attended_ref, key_ref, value_ref,
    own_key_ref, own_value_ref, from_ref, own_ref, top_ref, inverse_ref, out_ref,
):
    head = (first_group + pl.program_id(0)) * per_group + pl.program_id(1)
    cached, own = raw_scores(q_ref[...], key_ref, own_key_ref, from_ref, own_ref)
    top = pick_lane(top_ref, head)
    inverse = pick_lane(inverse_ref, head)
    grad = grad_ref[...]
    delta = jnp.sum(
        grad.astype(jnp.float32) * attended_ref[...].astype(jnp.float32),
        axis=1,
        keepdims=True,
    )
    cached = jnp.exp2((cached - top) * base) * (contract_cols(grad, value_ref[...]) - delta)
    own = jnp.exp2((own - top) * base) * (contract_cols(grad, own_value_ref[...]) - delta)
    out = jnp.dot(
        cached.astype(jnp.bfloat16), key_ref[...], preferred_element_type=jnp.float32
    ) + jnp.dot(
        own.astype(jnp.bfloat16), own_key_ref[...], preferred_element_type=jnp.float32
    )
    out_ref[...] = (out * (inverse * scale)).astype(out_ref.dtype)


def blocks(tokens, cached, padded, per_group, first):
    head = pl.BlockSpec((tokens, HEAD_DIM), lambda g, p: (0, (first + g) * per_group + p))
    rows = pl.BlockSpec((cached, HEAD_DIM), lambda g, p: (0, first + g))
    own = pl.BlockSpec((padded, HEAD_DIM), lambda g, p: (0, first + g))
    bound = pl.BlockSpec((tokens, 1), lambda g, p: (0, 0))
    stat = pl.BlockSpec((tokens, HEAD_DIM), lambda g, p: (0, 0))
    here = pl.BlockSpec((tokens, HEAD_DIM), lambda g, p: (0, g * per_group + p))
    return (head, rows, own, bound, stat, here)


def forward(
    first, groups, per_group, base, queries, keys, values, own_keys, own_values, bounds
):
    tokens = queries.shape[0]
    cached, padded = keys.shape[0], own_keys.shape[0]
    head, rows, own, bound, stat, here = blocks(tokens, cached, padded, per_group, first)
    work = groups * per_group * tokens * (cached + padded)
    return pl.pallas_call(
        functools.partial(forward_kernel, per_group, base),
        grid=(groups, per_group),
        in_specs=[head, rows, rows, own, own, bound, bound],
        out_specs=[here, stat, stat],
        out_shape=[
            jax.ShapeDtypeStruct((tokens, groups * per_group * HEAD_DIM), jnp.float32),
            jax.ShapeDtypeStruct((tokens, HEAD_DIM), jnp.float32),
            jax.ShapeDtypeStruct((tokens, HEAD_DIM), jnp.float32),
        ],
        compiler_params=pltpu.CompilerParams(vmem_limit_bytes=40 << 20),
        cost_estimate=pl.CostEstimate(
            flops=16 * HEAD_DIM * work, bytes_accessed=20 << 20, transcendentals=work
        ),
    )(queries, keys, values, own_keys, own_values, *bounds)


def backward(
    first, groups, per_group, base, scale, queries, grads, attended, keys, values,
    own_keys, own_values, bounds, top, inverse,
):
    tokens = queries.shape[0]
    cached, padded = keys.shape[0], own_keys.shape[0]
    head, rows, own, bound, stat, here = blocks(tokens, cached, padded, per_group, first)
    work = groups * per_group * tokens * (cached + padded)
    return pl.pallas_call(
        functools.partial(backward_kernel, first, per_group, base, scale),
        grid=(groups, per_group),
        in_specs=[head, here, head, rows, rows, own, own, bound, bound, stat, stat],
        out_specs=here,
        out_shape=jax.ShapeDtypeStruct(grads.shape, jnp.float32),
        compiler_params=pltpu.CompilerParams(vmem_limit_bytes=48 << 20),
        cost_estimate=pl.CostEstimate(
            flops=16 * HEAD_DIM * work, bytes_accessed=12 << 20, transcendentals=work
        ),
    )(queries, grads, attended, keys, values, own_keys, own_values, *bounds, top, inverse)


def split_columns(array, pieces):
    width = array.shape[1] // pieces
    return [array[:, i * width : (i + 1) * width] for i in range(pieces)]


def per_device_general(
    residual,
    norm_gain,
    grad_out,
    w_gate,
    w_up,
    w_down,
    w_output,
    query,
    key,
    value,
    cache_key,
    cache_value,
    visible_from,
):
    wide_count = lax.axis_size("wide")
    wide_place = lax.axis_index("wide")
    tokens = residual.shape[0]
    scale = 1.0 / math.sqrt(HEAD_DIM)
    base = scale * LOG2E

    stream = residual.astype(jnp.float32)
    gain = norm_gain.astype(jnp.float32)
    hidden_part = contract_cols(grad_out, w_down)
    squares = narrow_sum(jnp.sum(stream * stream, axis=1))
    rstd = lax.rsqrt(squares / D + EPSILON)[:, None]
    normed = (stream * rstd * gain).astype(jnp.bfloat16)
    gate_part = jnp.dot(normed, w_gate, preferred_element_type=jnp.float32)
    up_part = jnp.dot(normed, w_up, preferred_element_type=jnp.float32)

    queries, stretch_keys, stretch_values = (to_heads(query), to_heads(key), to_heads(value))
    groups = stretch_keys.shape[1] // HEAD_DIM
    per_group = queries.shape[1] // stretch_keys.shape[1]
    heads = groups * per_group
    cached = cache_key.shape[0]
    span = tokens // wide_count
    start = wide_place * span
    padded = -(-span // HEAD_DIM) * HEAD_DIM
    filler = ((0, padded - span), (0, 0))
    own_keys = jnp.pad(lax.dynamic_slice_in_dim(stretch_keys, start, span, 0), filler)
    own_values = jnp.pad(lax.dynamic_slice_in_dim(stretch_values, start, span, 0), filler)
    position = jnp.arange(tokens, dtype=jnp.int32)[:, None]
    bounds = (
        visible_from[:, None] - wide_place * cached,
        jnp.minimum(position - start, span - 1),
    )

    lows = [part.astype(jnp.bfloat16) for part in (hidden_part, gate_part, up_part)]
    hidden_grad = narrow_total(hidden_part, lows[0])
    gate = narrow_total(gate_part, lows[1])
    up = narrow_total(up_part, lows[2])

    queries, own_keys, own_values = after((queries, own_keys, own_values), *lows)
    early = groups - groups // 4
    outs, tops, totals = [], [], []
    for first, count in ((0, early), (early, groups - early)):
        if count == 0:
            continue
        if first:
            (queries,) = after((queries,), hidden_grad, gate, up)
        out, top, total = forward(
            first, count, per_group, base, queries, cache_key, cache_value, own_keys,
            own_values, bounds,
        )
        outs.append(out)
        tops.append(top[:, : count * per_group])
        totals.append(total[:, : count * per_group])
    local_out = jnp.concatenate(outs, axis=1)
    local_top = jnp.concatenate(tops, axis=1)
    stats = doubled(
        jnp.concatenate([local_top] + totals, axis=1), functools.partial(merge_softmax, base)
    )
    top, inverse = stats[:, :heads], 1.0 / stats[:, heads:]
    factor = jnp.exp2((local_top - top) * base) * inverse
    owner = jnp.arange(heads * HEAD_DIM, dtype=jnp.int32)[None, :] // HEAD_DIM
    choose = (owner == jnp.arange(heads, dtype=jnp.int32)[:, None]).astype(jnp.float32)
    attended_part = local_out * jnp.dot(factor, choose, precision=lax.Precision.HIGHEST)
    side = ((0, 0), (0, HEAD_DIM - heads))
    top, inverse = jnp.pad(top, side), jnp.pad(inverse, side)
    ways = orders()
    attended = jnp.concatenate(
        [
            gathered(scatter_sum(as_cube(part), way).astype(jnp.bfloat16), way)
            for part, way in zip(split_columns(attended_part, 2), ways)
        ],
        axis=1,
    )

    activated, d_gate, d_up = swiglu_back(gate, up, hidden_grad)
    d_normed_part = contract_cols(d_gate, w_gate) + contract_cols(d_up, w_up)
    d_normed = jnp.concatenate(
        [
            scatter_sum(as_cube(part), way)
            for part, way in zip(split_columns(d_normed_part, 2), ways)
        ],
        axis=1,
    )
    rstd_rows = own_rows(rstd)
    scaled = own_rows(residual).astype(jnp.float32) * rstd_rows
    grad_gain = doubled(jnp.sum(d_normed * scaled, axis=0), jnp.add)
    weighted = d_normed * gain
    inner = narrow_sum(jnp.sum(weighted * scaled, axis=1)) / D
    grad_rows = (
        own_rows(grad_out).astype(jnp.float32)
        + rstd_rows * (weighted - scaled * inner[:, None])
    ).astype(jnp.bfloat16)
    grad_residual = jnp.concatenate(
        [gathered(part, way) for part, way in zip(split_columns(grad_rows, 2), ways)], axis=1
    )

    columns = w_output.shape[1]
    width = grad_residual.shape[1]
    if lax.axis_size("narrow") == 2:
        own_panel = lax.dynamic_slice_in_dim(
            grad_residual, (wide_place * columns) % width, columns, 1
        )
        holder = (wide_place * columns) // width == lax.axis_index("narrow")
        panel = jnp.where(holder, own_panel, swapped(own_panel, "narrow", 1))
    else:
        whole = lax.all_gather(grad_residual, "narrow", axis=1, tiled=True)
        panel = lax.dynamic_slice_in_dim(whole, wide_place * columns, columns, 1)
    pieces = 2 if groups % 2 == 0 else 1
    group_count = groups // pieces
    query_grads, query_parts = [], []
    for piece in range(pieces):
        way = ways[piece]
        wide_rows = group_count * per_group * HEAD_DIM
        rows = w_output[piece * wide_rows : (piece + 1) * wide_rows]
        d_attention = gathered(
            scatter_sum(as_cube(contract_cols(panel, rows)), way).astype(jnp.bfloat16), way
        )
        query_part = backward(
            piece * group_count, group_count, per_group, base, scale, queries, d_attention,
            attended, cache_key, cache_value, own_keys, own_values, bounds, top, inverse,
        )
        query_parts.append(query_part)
        query_grads.append(
            gathered(scatter_sum(as_cube(query_part), way).astype(jnp.bfloat16), way)
        )
    grad_query = jnp.concatenate(query_grads, axis=1)
    activated, d_gate, d_up, panel = after((activated, d_gate, d_up, panel), *query_parts)
    grad_w_down = contract_rows(activated, grad_out).astype(jnp.bfloat16)
    grad_w_gate = contract_rows(normed, d_gate).astype(jnp.bfloat16)
    grad_w_up = contract_rows(normed, d_up).astype(jnp.bfloat16)
    grad_w_output = contract_rows(attended, panel).astype(jnp.bfloat16)
    return (
        grad_residual,
        grad_gain,
        grad_w_gate,
        grad_w_up,
        grad_w_down,
        grad_w_output,
        grad_query,
    )


def block_scores(q, pair_ref, from_ref, block):
    rows = pair_ref.shape[0] // 2
    cached = contract_cols(q, pair_ref[:rows, :])
    at = lax.broadcasted_iota(jnp.int32, cached.shape, 1)
    return jnp.where(at >= from_ref[:, block : block + 1], cached, MASKED)


def own_scores(q, pair_ref, own_ref):
    own = contract_cols(q, pair_ref[: pair_ref.shape[0] // 2, :])
    own_at = lax.broadcasted_iota(jnp.int32, own.shape, 1)
    return jnp.where(own_at <= own_ref[...], own, MASKED)


STATS = HEAD_DIM // 2


def online_kernel(base, first, count, has_own, q_ref, from_ref, own_ref, *refs):
    pairs = refs[: count + has_own]
    rest = refs[count + has_own :]
    earlier, (out_ref, stat_ref) = rest[:-2], rest[-2:]
    head = pl.program_id(0)

    @pl.when(head == 0)
    def _():
        stat_ref[...] = jnp.zeros_like(stat_ref)

    q = q_ref[...]
    top = total = out = None
    if earlier:
        out_before, stat_before = earlier
        top, total = pick_lane(stat_before, head), pick_lane(stat_before, head + STATS)
        out = out_before[...]
    for at, pair in enumerate(pairs):
        rows = pair.shape[0] // 2
        if at < count:
            scores = block_scores(q, pair, from_ref, first + at)
        else:
            scores = own_scores(q, pair, own_ref)
        later = jnp.max(scores, axis=1, keepdims=True)
        if top is not None:
            later = jnp.maximum(top, later)
            shrink = jnp.exp2((top - later) * base)
            total, out = total * shrink, out * shrink
        scores = jnp.exp2((scores - later) * base)
        added = jnp.sum(scores, axis=1, keepdims=True)
        product = jnp.dot(
            scores.astype(jnp.bfloat16), pair[rows:, :], preferred_element_type=jnp.float32
        )
        total = added if top is None else total + added
        out = product if top is None else out + product
        top = later
    out_ref[...] = (out / total if earlier else out).astype(out_ref.dtype)
    lane = lax.broadcasted_iota(jnp.int32, stat_ref.shape, 1)
    stat_ref[...] = jnp.where(
        lane == head, top, jnp.where(lane == head + STATS, total, stat_ref[...])
    )


def online_forward(base, first, heads, queries, bounds, blocks, own, earlier):
    tokens = queries.shape[0]
    whole = lambda array: pl.BlockSpec(array.shape, lambda h: (0, 0))
    here = pl.BlockSpec((tokens, HEAD_DIM), lambda h: (0, h))
    stat = pl.BlockSpec((tokens, HEAD_DIM), lambda h: (0, 0))
    pairs = list(blocks) + ([] if own is None else [own])
    work = heads * tokens * sum(pair.shape[0] // 2 for pair in pairs)
    rest = (*bounds, *pairs)
    kind = jnp.bfloat16 if earlier else jnp.float32
    return pl.pallas_call(
        functools.partial(online_kernel, base, first, len(blocks), int(own is not None)),
        grid=(heads,),
        in_specs=[here] + [whole(array) for array in rest] + ([here, stat] if earlier else []),
        out_specs=[here, stat],
        out_shape=[
            jax.ShapeDtypeStruct((tokens, heads * HEAD_DIM), kind),
            jax.ShapeDtypeStruct((tokens, HEAD_DIM), jnp.float32),
        ],
        compiler_params=pltpu.CompilerParams(vmem_limit_bytes=48 << 20),
        cost_estimate=pl.CostEstimate(
            flops=HEAD_DIM * work, bytes_accessed=1 << 20, transcendentals=work // 8
        ),
    )(queries, *rest, *earlier)


def query_kernel(base, scale, count, q_ref, grad_ref, attended_ref, from_ref, own_ref, *refs):
    pairs = refs[: count + 1]
    stat_ref, out_ref = refs[count + 1 :]
    head = pl.program_id(0)
    top = pick_lane(stat_ref, head)
    inverse = pick_lane(stat_ref, head + STATS)
    q, grad = q_ref[...], grad_ref[...]
    delta = jnp.sum(
        grad.astype(jnp.float32) * attended_ref[...].astype(jnp.float32), axis=1, keepdims=True
    )
    out = None
    for at, pair in enumerate(pairs):
        rows = pair.shape[0] // 2
        if at < count:
            scores = block_scores(q, pair, from_ref, at)
        else:
            scores = own_scores(q, pair, own_ref)
        scores = jnp.exp2((scores - top) * base) * (contract_cols(grad, pair[rows:, :]) - delta)
        product = jnp.dot(
            scores.astype(jnp.bfloat16), pair[:rows, :], preferred_element_type=jnp.float32
        )
        out = out + product if at else product
    out_ref[...] = out * (inverse * scale)


def query_backward(
    base, scale, heads, queries, grads, attended, bounds, blocks, own, stats
):
    tokens = queries.shape[0]
    whole = lambda array: pl.BlockSpec(array.shape, lambda h: (0, 0))
    head = pl.BlockSpec((tokens, HEAD_DIM), lambda h: (0, h))
    pairs = list(blocks) + [own]
    work = heads * tokens * sum(pair.shape[0] // 2 for pair in pairs)
    rest = (*bounds, *pairs, stats)
    return pl.pallas_call(
        functools.partial(query_kernel, base, scale, len(blocks)),
        grid=(heads,),
        in_specs=[head, head, head] + [whole(array) for array in rest],
        out_specs=head,
        out_shape=jax.ShapeDtypeStruct((tokens, heads * HEAD_DIM), jnp.float32),
        compiler_params=pltpu.CompilerParams(vmem_limit_bytes=48 << 20),
        cost_estimate=pl.CostEstimate(
            flops=12 * HEAD_DIM * work, bytes_accessed=12 << 20, transcendentals=work
        ),
    )(queries, grads, attended, *rest)


def placed(near, far, first):
    low = first == 0
    return jnp.concatenate([jnp.where(low, near, far), jnp.where(low, far, near)], axis=0)


def joined(near, far, bit, axis):
    low = bit == 0
    return jnp.concatenate([jnp.where(low, near, far), jnp.where(low, far, near)], axis=axis)


def line_scatter(part, line):
    rows = part.shape[0] // 4
    low = part.astype(jnp.bfloat16)
    total = lax.dynamic_slice_in_dim(part, line * rows, rows, 0)
    for m in (1, 2, 3):
        sent = lax.dynamic_slice_in_dim(low, (line ^ m) * rows, rows, 0)
        total = total + swapped(sent, "wide", m << 2).astype(jnp.float32)
    return total


def line_gather(chunk, line):
    held = [chunk if m == 0 else swapped(chunk, "wide", m << 2) for m in range(4)]
    return joined(
        joined(held[0], held[1], line & 1, 0), joined(held[2], held[3], line & 1, 0), line >> 1, 0
    )


def side_gather(block, group):
    return joined(block, swapped(block, "wide", 2), group >> 1, 1)


def core_gather(block, group):
    return joined(block, swapped(block, "wide", 1), group & 1, 1)


PIECES = 5
MESH = pl.DeviceIdType.MESH


def exchange_kernel(
    base, d_gate_ref, d_up_ref, out_ref, stat_ref,
    every_gate, every_up, attended_ref, stats_ref,
    outs, stats, rows, row_stats, all_rows, all_stats,
    local_sem, x_send, x_recv, send_sem, recv_sem,
):
    place = lax.axis_index("wide")
    x = lax.axis_index("narrow")
    line, group = place // 4, place % 4
    count = d_gate_ref.shape[0]
    lines = [place + 4 * (1 - 2 * (line % 2)), place + 8 * (1 - 2 * (line // 2))]
    lines.append(lines[0] + lines[1] - place)
    at_line = [at // 4 for at in lines]
    barrier = pltpu.get_barrier_semaphore()
    pl.semaphore_signal(barrier, inc=1, device_id=(place, 1 - x), device_id_type=MESH)
    for peer in lines:
        pl.semaphore_signal(barrier, inc=1, device_id=(peer, x), device_id_type=MESH)
    pl.semaphore_wait(barrier, 4)

    here = pl.ds(pl.multiple_of(x * count, 16), count)
    moves = []
    for at, (src, dst) in enumerate(((d_gate_ref, every_gate), (d_up_ref, every_up))):
        far = pltpu.make_async_remote_copy(
            src_ref=src, dst_ref=dst.at[here], send_sem=x_send.at[at], recv_sem=x_recv.at[at],
            device_id=(place, 1 - x), device_id_type=MESH,
        )
        near = pltpu.make_async_copy(src, dst.at[here], local_sem.at[at])
        far.start()
        near.start()
        moves += [far, near]

    def line_copy(src, dst, at, m):
        return pltpu.make_async_remote_copy(
            src_ref=src, dst_ref=dst, send_sem=send_sem.at[at, m], recv_sem=recv_sem.at[at, m],
            device_id=(lines[m], x), device_id_type=MESH,
        )

    def scattered(m):
        return (
            line_copy(out_ref.at[at_line[m]], outs.at[m], 0, m),
            line_copy(stat_ref.at[at_line[m]], stats.at[m], 1, m),
        )

    for m in range(3):
        for sending in scattered(m):
            sending.start()
    for m in range(3):
        for sending in scattered(m):
            sending.wait_recv()
    parts = [stat_ref[line]] + [stats[m] for m in range(3)]
    top = functools.reduce(jnp.maximum, parts)
    lane = lax.broadcasted_iota(jnp.int32, top.shape, 1)
    weights = [
        jnp.where(
            lane < STATS, 0.0, pltpu.roll(jnp.exp2((part - top) * base), STATS, 1) * part
        )
        for part in parts
    ]
    total = functools.reduce(jnp.add, weights)
    inverse = 1.0 / jnp.where(total > 0.0, total, 1.0)
    row_stats[...] = jnp.where(lane < STATS, top, inverse)
    all_stats[line] = row_stats[...]
    weights = [weight * inverse for weight in weights]
    for h in range(rows.shape[1] // HEAD_DIM):
        cols = slice(h * HEAD_DIM, (h + 1) * HEAD_DIM)
        pieces = [out_ref[line, :, cols]] + [outs[m, :, cols] for m in range(3)]
        value = functools.reduce(
            jnp.add,
            [
                piece.astype(jnp.float32) * weight[:, STATS + h : STATS + h + 1]
                for piece, weight in zip(pieces, weights)
            ],
        )
        rows[:, cols] = value.astype(jnp.bfloat16)
    all_rows[line] = rows[...]

    def spread(m, where):
        return (
            line_copy(rows, all_rows.at[where], 2, m),
            line_copy(row_stats, all_stats.at[where], 3, m),
        )

    for m in range(3):
        for sending in spread(m, line):
            sending.start()
    for m in range(3):
        for sending in spread(m, at_line[m]):
            sending.wait_recv()
    attended_ref[...] = all_rows[...]
    stats_ref[...] = all_stats[...]
    for m in range(3):
        for sending in scattered(m) + spread(m, line):
            sending.wait_send()
    for move in moves:
        move.wait()


def exchange(base, d_gate, d_up, out, stat):
    tokens, width = out.shape
    span = tokens // 4
    low, full = jnp.bfloat16, jnp.float32
    vmem = pl.BlockSpec(memory_space=pltpu.VMEM)
    hbm = pl.BlockSpec(memory_space=pl.ANY)
    dma = pltpu.SemaphoreType.DMA
    every = jax.ShapeDtypeStruct((2 * d_gate.shape[0], d_gate.shape[1]), low)
    every_gate, every_up, attended, stats = pl.pallas_call(
        functools.partial(exchange_kernel, base),
        out_shape=[
            every,
            every,
            jax.ShapeDtypeStruct((4, span, width), low),
            jax.ShapeDtypeStruct((4, span, HEAD_DIM), full),
        ],
        in_specs=[hbm, hbm, vmem, vmem],
        out_specs=[hbm, hbm, vmem, vmem],
        scratch_shapes=[
            pltpu.VMEM((3, span, width), low),
            pltpu.VMEM((3, span, HEAD_DIM), full),
            pltpu.VMEM((span, width), low),
            pltpu.VMEM((span, HEAD_DIM), full),
            pltpu.VMEM((4, span, width), low),
            pltpu.VMEM((4, span, HEAD_DIM), full),
            dma((2,)), dma((2,)), dma((2,)), dma((4, 3)), dma((4, 3)),
        ],
        compiler_params=pltpu.CompilerParams(
            collective_id=1, has_side_effects=True, vmem_limit_bytes=40 << 20
        ),
        cost_estimate=pl.CostEstimate(
            flops=20_000_000_000, bytes_accessed=8 << 20, transcendentals=0
        ),
    )(d_gate, d_up, out.reshape(4, span, width), stat.reshape(4, span, HEAD_DIM))
    return every_gate, every_up, attended.reshape(tokens, width), stats.reshape(tokens, HEAD_DIM)


def middle_kernel(
    part_ref, scaled_ref, rstd_ref, out_grad_ref, gain_ref, w_ref,
    rows_ref, gain_grad_ref, window_ref, d_attention_ref,
    from_core, to_side, from_side, to_near, from_near, kept, to_far, from_far, summed,
    da_send, da_own, da_core, da_to_side, da_side, da_to_near, da_near, da_kept, da_to_far, da_far,
    inner_to, inner_from, grad_rows, panels, gathered_ref,
    send_sem, recv_sem, da_send_sem, da_recv_sem, inner_send, inner_recv,
    panel_send, panel_recv, gather_send, gather_recv,
):
    place = lax.axis_index("wide")
    x = lax.axis_index("narrow")
    line, group = place // 4, place % 4
    y, core = group // 2, group % 2
    hi, lo = line // 2, line % 2
    width = rows_ref.shape[1]
    step = width // PIECES

    def flip(bit):
        weight = 1 << bit
        at = (place // weight) % 2
        return (place + weight - 2 * weight * at, x)

    peers = {"core": flip(0), "side": flip(1), "near": flip(2), "far": flip(3), "x": (place, 1 - x)}
    panel_block = 2 * core + y
    targets = [(8 * x + 2 * panel_block + j, nx) for j in (0, 1) for nx in (0, 1)]
    source_x, source_block = place // 8, (place % 8) // 2
    source_group = 2 * (source_block % 2) + source_block // 2
    sources = [(4 * s + source_group, source_x) for s in range(4)]

    def is_me(device):
        return jnp.logical_and(device[0] == place, device[1] == x)

    def not_me(device):
        return jnp.logical_not(is_me(device))

    barrier = pltpu.get_barrier_semaphore()
    for device in peers.values():
        pl.semaphore_signal(barrier, inc=1, device_id=device, device_id_type=MESH)
    for device in targets + sources:
        @pl.when(not_me(device))
        def _(device=device):
            pl.semaphore_signal(barrier, inc=1, device_id=device, device_id_type=MESH)
    mine = jnp.logical_and(place // 8 == x, source_group == group).astype(jnp.int32)
    pl.semaphore_wait(barrier, 13 - 2 * mine)

    def copy(src, dst, sends, recvs, at, device):
        return pltpu.make_async_remote_copy(
            src_ref=src, dst_ref=dst, send_sem=sends.at[at], recv_sem=recvs.at[at],
            device_id=device, device_id_type=MESH,
        )

    def scatter(outgoing, own, bufs, sends, recvs, finish):
        core_buf, side_out, side_in, near_out, near_in, keep, far_out, far_in = bufs

        def cols(p):
            return pl.ds(p * step, step)

        def core_copy(yp, p):
            return copy(
                outgoing(yp, p), core_buf.at[yp, :, :, :, cols(p)], sends, recvs,
                (yp, p), peers["core"],
            )

        def side_copy(p):
            return copy(
                side_out.at[:, :, :, cols(p)], side_in.at[:, :, :, cols(p)], sends, recvs,
                (2, p), peers["side"],
            )

        def near_copy(p):
            return copy(
                near_out.at[:, :, cols(p)], near_in.at[:, :, cols(p)], sends, recvs,
                (3, p), peers["near"],
            )

        def far_copy(p):
            return copy(
                far_out.at[:, cols(p)], far_in.at[:, cols(p)], sends, recvs,
                (4, p), peers["far"],
            )

        def stage(s, p):
            if s == 0:
                core_copy(0, p).start()
                core_copy(1, p).start()
            elif s == 1:
                core_copy(0, p).wait_recv()
                core_copy(1, p).wait_recv()
                for h in range(2):
                    for l in range(2):
                        value = own(1 - y, h, l, p) + core_buf[1 - y, h, l, :, cols(p)].astype(
                            jnp.float32
                        )
                        side_out[h, l, :, cols(p)] = value.astype(jnp.bfloat16)
                side_copy(p).start()
            elif s == 2:
                side_copy(p).wait_recv()

                def total(h, l):
                    return (
                        own(y, h, l, p)
                        + core_buf[y, h, l, :, cols(p)].astype(jnp.float32)
                        + side_in[h, l, :, cols(p)].astype(jnp.float32)
                    )

                for h in range(2):
                    near_out[h, :, cols(p)] = total(h, 1 - lo).astype(jnp.bfloat16)
                near_copy(p).start()
                for h in range(2):
                    keep[h, :, cols(p)] = total(h, lo)
            elif s == 3:
                near_copy(p).wait_recv()

                def total(h):
                    return keep[h, :, cols(p)] + near_in[h, :, cols(p)].astype(jnp.float32)

                far_out[:, cols(p)] = total(1 - hi).astype(jnp.bfloat16)
                far_copy(p).start()
            else:
                far_copy(p).wait_recv()
                finish(
                    p,
                    keep[hi, :, cols(p)]
                    + near_in[hi, :, cols(p)].astype(jnp.float32)
                    + far_in[:, cols(p)].astype(jnp.float32),
                )

        for p in range(PIECES):
            stage(0, p)
        for t in range(-2, PIECES + 2):
            for s, p in ((2, t), (1, t + 2), (3, t - 1), (4, t - 2)):
                if 0 <= p < PIECES:
                    stage(s, p)

        def drain():
            for p in range(PIECES):
                core_copy(0, p).wait_send()
                core_copy(1, p).wait_send()
                side_copy(p).wait_send()
                near_copy(p).wait_send()
                far_copy(p).wait_send()

        return drain

    def part_cols(yp, cp, p):
        return pl.ds(pl.multiple_of((2 * cp + yp) * width + p * step, HEAD_DIM), step)

    def part_finish(p, value):
        summed[:, pl.ds(p * step, step)] = value

    drain_parts = scatter(
        lambda yp, p: part_ref.at[:, :, :, part_cols(yp, 1 - core, p)],
        lambda yp, h, l, p: part_ref[h, l, :, part_cols(yp, core, p)].astype(jnp.float32),
        (from_core, to_side, from_side, to_near, from_near, kept, to_far, from_far),
        send_sem, recv_sem, part_finish,
    )

    d_normed = summed[...]
    scaled = scaled_ref[...]
    weighted = d_normed * gain_ref[...]
    inner = jnp.sum(weighted * scaled, axis=1, keepdims=True)
    inner = jnp.broadcast_to(inner, inner_to.shape[1:])
    inner_copies = []
    for at, name in enumerate(("core", "side", "x")):
        inner_to[at] = inner
        sending = copy(
            inner_to.at[at], inner_from.at[at], inner_send, inner_recv, at, peers[name]
        )
        sending.start()
        inner_copies.append(sending)
        if at == 0:
            gain_grad_ref[...] = jnp.broadcast_to(
                jnp.sum(d_normed * scaled, axis=0, keepdims=True), gain_grad_ref.shape
            )
        sending.wait_recv()
        inner = inner + inner_from[at]
    inner = inner[:, :1] * (1.0 / D)
    rows = (
        out_grad_ref[...] + rstd_ref[:, :1] * (weighted - scaled * inner)
    ).astype(jnp.bfloat16)
    grad_rows[...] = rows
    span = panels.shape[3]
    starts = (0, width - span)

    def panel_copy(at):
        j = at // 2
        return pltpu.make_async_remote_copy(
            src_ref=grad_rows.at[:, pl.ds(starts[j], span)], dst_ref=panels.at[hi, lo],
            send_sem=panel_send.at[at], recv_sem=panel_recv.at[line],
            device_id=targets[at], device_id_type=MESH,
        )

    for at, device in enumerate(targets):
        @pl.when(not_me(device))
        def _(at=at):
            panel_copy(at).start()

        @pl.when(is_me(device))
        def _(at=at):
            begin = starts[at // 2]
            panels[hi, lo] = grad_rows[:, begin : begin + span]
    rows_ref[...] = rows
    for s, device in enumerate(sources):
        @pl.when(not_me(device))
        def _(s=s, device=device):
            pltpu.make_async_remote_copy(
                src_ref=grad_rows.at[:, pl.ds(0, span)], dst_ref=panels.at[s // 2, s % 2],
                send_sem=panel_send.at[0], recv_sem=panel_recv.at[s],
                device_id=device, device_id_type=MESH,
            ).wait_recv()

    panel = panels[...]
    window_ref[...] = panel
    panel = panel.reshape(-1, span)
    shape = (2, 2, grad_rows.shape[0], width)

    def product(yp, cp):
        block = w_ref[pl.ds(pl.multiple_of((2 * yp + cp) * width, HEAD_DIM), width), :]
        return contract_cols(panel, block).reshape(shape)

    for yp in range(2):
        da_send[yp] = product(yp, 1 - core).astype(jnp.bfloat16)
        da_own[yp] = product(yp, core)

    def gather_far(p):
        at = pl.ds(p * step, step)
        return copy(
            gathered_ref.at[hi, lo, :, at], gathered_ref.at[hi, lo, :, at],
            gather_send, gather_recv, (0, p), peers["far"],
        )

    def gather_near(p):
        at = pl.ds(p * step, step)
        return copy(
            gathered_ref.at[:, lo, :, at], gathered_ref.at[:, lo, :, at],
            gather_send, gather_recv, (1, p), peers["near"],
        )

    def da_finish(p, value):
        gathered_ref[hi, lo, :, pl.ds(p * step, step)] = value.astype(jnp.bfloat16)
        gather_far(p).start()
        if p > 0:
            gather_far(p - 1).wait_recv()
            gather_near(p - 1).start()

    drain_da = scatter(
        lambda yp, p: da_send.at[yp, :, :, :, pl.ds(p * step, step)],
        lambda yp, h, l, p: da_own[yp, h, l, :, pl.ds(p * step, step)],
        (da_core, da_to_side, da_side, da_to_near, da_near, da_kept, da_to_far, da_far),
        da_send_sem, da_recv_sem, da_finish,
    )
    gather_far(PIECES - 1).wait_recv()
    gather_near(PIECES - 1).start()
    for p in range(PIECES):
        gather_near(p).wait_recv()
    d_attention_ref[...] = gathered_ref[...]

    drain_parts()
    for sending in inner_copies:
        sending.wait_send()
    for at, device in enumerate(targets):
        @pl.when(not_me(device))
        def _(at=at):
            panel_copy(at).wait_send()
    drain_da()
    for p in range(PIECES):
        gather_far(p).wait_send()
        gather_near(p).wait_send()


def middle(part, scaled, rstd, out_grad, gain, weights):
    rows, width = scaled.shape
    span = weights.shape[1]
    low, full = jnp.bfloat16, jnp.float32
    chunk = (2, 2, rows, width)
    stages = [
        pltpu.VMEM((2,) + chunk, low),
        pltpu.VMEM(chunk, low),
        pltpu.VMEM(chunk, low),
        pltpu.VMEM((2, rows, width), low),
        pltpu.VMEM((2, rows, width), low),
        pltpu.VMEM((2, rows, width), full),
        pltpu.VMEM((rows, width), low),
        pltpu.VMEM((rows, width), low),
    ]
    vmem = pl.BlockSpec(memory_space=pltpu.VMEM)
    dma = pltpu.SemaphoreType.DMA
    return pl.pallas_call(
        middle_kernel,
        out_shape=[
            jax.ShapeDtypeStruct((rows, width), low),
            jax.ShapeDtypeStruct((8, width), full),
            jax.ShapeDtypeStruct((2, 2, rows, span), low),
            jax.ShapeDtypeStruct(chunk, low),
        ],
        in_specs=[vmem] * 6,
        out_specs=[vmem] * 4,
        scratch_shapes=stages
        + [pltpu.VMEM((rows, width), full)]
        + [pltpu.VMEM((2,) + chunk, low), pltpu.VMEM((2,) + chunk, full)]
        + stages
        + [
            pltpu.VMEM((3, rows, HEAD_DIM), full),
            pltpu.VMEM((3, rows, HEAD_DIM), full),
            pltpu.VMEM((rows, width), low),
            pltpu.VMEM((2, 2, rows, span), low),
            pltpu.VMEM(chunk, low),
            dma((5, PIECES)), dma((5, PIECES)), dma((5, PIECES)), dma((5, PIECES)),
            dma((3,)), dma((3,)), dma((4,)), dma((4,)), dma((2, PIECES)), dma((2, PIECES)),
        ],
        compiler_params=pltpu.CompilerParams(
            collective_id=0, has_side_effects=True, vmem_limit_bytes=40 << 20
        ),
        cost_estimate=pl.CostEstimate(
            flops=60_000_000_000, bytes_accessed=8 << 20, transcendentals=0
        ),
    )(part.reshape(2, 2, rows, -1), scaled, rstd, out_grad, gain, weights)


def per_device(
    residual,
    norm_gain,
    grad_out,
    w_gate,
    w_up,
    w_down,
    w_output,
    query,
    key,
    value,
    cache_key,
    cache_value,
    visible_from,
):
    wide_place = lax.axis_index("wide")
    side = lax.axis_index("narrow")
    line, group = wide_place >> 2, wide_place & 3
    tokens = residual.shape[0]
    cached = cache_key.shape[0]
    hidden = w_down.shape[0]
    scale = 1.0 / math.sqrt(HEAD_DIM)
    base = scale * LOG2E
    heads = query.shape[1] // (8 * HEAD_DIM)
    group_width = heads * HEAD_DIM
    span = tokens // 4

    def for_side(array, place):
        count = array.shape[0] // 2
        return lax.dynamic_slice_in_dim(array, place * count, count, 0)

    def for_heads(array, place):
        width = array.shape[1] // 8
        return lax.dynamic_slice_in_dim(array, (place * 4 + group) * width, width, 1)

    block = 2 * (group & 1) + (group >> 1)

    def own_chunk(array):
        return lax.dynamic_slice(
            array, (line * span, block * group_width), (span, group_width)
        )

    stream = residual.astype(jnp.float32)
    gain = norm_gain.astype(jnp.float32)
    squares = narrow_sum(jnp.sum(stream * stream, axis=1))

    near = jnp.concatenate([for_heads(array, side) for array in (query, key, value)], axis=1)
    sent = jnp.concatenate([for_heads(array, 1 - side) for array in (query, key, value)], axis=1)
    stretch = placed(near, swapped(sent, "narrow", 1), side)
    queries = stretch[:, :group_width]
    own = lax.dynamic_slice_in_dim(stretch[:, group_width:], line * span, span, 0)
    own = jnp.pad(own, ((0, HEAD_DIM - span), (0, 0)))
    own = jnp.concatenate([own[:, :HEAD_DIM], own[:, HEAD_DIM:]], axis=0)

    def stacked(m):
        at = (group ^ m) * HEAD_DIM
        return jnp.concatenate(
            [
                lax.dynamic_slice_in_dim(cache, at, HEAD_DIM, 1)
                for cache in (cache_key, cache_value)
            ],
            axis=0,
        )

    cache_blocks = [
        stacked(m) if m == 0 else swapped(stacked(m), "wide", m) for m in range(4)
    ]
    position = jnp.arange(tokens, dtype=jnp.int32)[:, None]
    starts = jnp.stack([((line << 2) | (group ^ m)) * cached for m in range(4)])
    bounds = (
        visible_from[:, None] - starts[None, :],
        jnp.minimum(position - line * span, span - 1),
    )

    def halves(part):
        sent = for_side(part, 1 - side).astype(jnp.bfloat16)
        return sent, swapped(sent, "narrow", 1)

    def across(weights, rows, dim):
        return lax.dot_general(
            weights, rows, (((dim,), (1,)), ((), ())), preferred_element_type=jnp.float32
        )

    hidden_part = across(w_down, grad_out, 1)
    rstd = lax.rsqrt(squares / D + EPSILON)[:, None]
    normed = (stream * rstd * gain).astype(jnp.bfloat16)
    gate_part = across(w_gate, normed, 0)
    up_part = across(w_up, normed, 0)
    matmuls = (hidden_part, gate_part, up_part)
    exchanged = [halves(part) for part in matmuls]
    (early_queries,) = after((queries,), *[sent for sent, _ in exchanged])
    early = online_forward(base, 0, heads, early_queries, bounds, cache_blocks[:2], own, ())
    local_out, local_stat = online_forward(
        base, 2, heads, queries, bounds, cache_blocks[2:], None, early
    )
    gots = after([got for _, got in exchanged], local_out)
    hidden_grad, gate, up = [
        for_side(part, side) + got.astype(jnp.float32) for part, got in zip(matmuls, gots)
    ]
    activated_near, d_gate_near, d_up_near = swiglu_back(gate, up, hidden_grad)
    d_gate, d_up, attended, stats = exchange(
        base, d_gate_near, d_up_near, local_out, local_stat
    )
    (activated_sent,) = after((activated_near,), d_gate)
    activated_far = swapped(activated_sent, "narrow", 1)

    def back(grads, weights):
        return lax.dot_general(
            grads, weights, (((0,), (1,)), ((), ())), preferred_element_type=jnp.float32
        )

    d_normed_part = (back(d_gate, w_gate) + back(d_up, w_up)).astype(jnp.bfloat16)

    rstd_rows = lax.dynamic_slice_in_dim(rstd, line * span, span, 0)
    columns = w_output.shape[1]
    slack = -(-columns // HEAD_DIM) * HEAD_DIM - columns
    even = wide_place % 2 == 0
    weights = jnp.where(
        even, jnp.pad(w_output, ((0, 0), (0, slack))), jnp.pad(w_output, ((0, 0), (slack, 0)))
    )
    grad_rows, gain_rows, window, d_attention = middle(
        d_normed_part,
        own_chunk(residual).astype(jnp.float32) * rstd_rows,
        jnp.broadcast_to(rstd_rows, (span, HEAD_DIM)),
        own_chunk(grad_out).astype(jnp.float32),
        lax.dynamic_slice_in_dim(gain, block * group_width, group_width, 0)[None, :],
        weights,
    )
    d_attention = d_attention.reshape(tokens, group_width)
    window = window.reshape(tokens, -1)
    panel = jnp.where(even, window[:, :columns], window[:, slack:])
    def by_block(rows):
        return core_gather(side_gather(rows, group), group)

    grad_residual = by_block(line_gather(grad_rows, line))
    gain_sum = gain_rows[:1]
    for m in (4, 8):
        gain_sum = gain_sum + swapped(gain_sum, "wide", m)
    grad_gain = by_block(gain_sum)[0]

    def interleaved(pair, other):
        low = (group & 1) == 0
        width = group_width
        first, second = jnp.where(low, pair, other), jnp.where(low, other, pair)
        return jnp.concatenate(
            [first[:, :width], second[:, :width], first[:, width:], second[:, width:]], axis=1
        )

    def by_group(rows):
        pair = side_gather(rows, group)
        return interleaved(pair, swapped(pair, "wide", 1))

    query_part = query_backward(
        base, scale, heads, queries, d_attention, attended, bounds, cache_blocks, own, stats
    )
    every_attended = by_group(attended)
    activated = placed(activated_near, activated_far, side)

    def outer(grads):
        return lax.dot_general(
            normed, grads, (((0,), (1,)), ((), ())), preferred_element_type=jnp.float32
        ).astype(jnp.bfloat16)

    query_low = query_part.astype(jnp.bfloat16)

    def query_rows(array, at):
        return lax.dynamic_slice_in_dim(array, at * span, span, 0)

    d_gate, d_up, activated, panel = after((d_gate, d_up, activated, panel), query_part)
    got = [swapped(query_rows(query_low, line ^ m), "wide", m << 2) for m in (1, 2, 3)]
    grad_w_gate = outer(d_gate)
    got = after(got, grad_w_gate)
    total = query_rows(query_part, line)
    for piece in got:
        total = total + piece.astype(jnp.float32)
    total = total.astype(jnp.bfloat16)
    held = [total] + [swapped(total, "wide", m << 2) for m in (1, 2, 3)]
    (d_up,) = after((d_up,), grad_w_gate)
    grad_w_up = outer(d_up)
    held = after(held, grad_w_up)
    own_query = joined(
        joined(held[0], held[1], line & 1, 0), joined(held[2], held[3], line & 1, 0), line >> 1, 0
    )
    side_query = swapped(own_query, "wide", 2)
    (activated,) = after((activated,), grad_w_up)
    grad_w_down = jnp.dot(
        activated, grad_out, preferred_element_type=jnp.float32
    ).astype(jnp.bfloat16)
    (side_query,) = after((side_query,), grad_w_down)
    pair = joined(own_query, side_query, group >> 1, 1)
    core_query = swapped(pair, "wide", 1)
    (panel,) = after((panel,), grad_w_down)
    grad_w_output = contract_rows(every_attended, panel).astype(jnp.bfloat16)
    (core_query,) = after((core_query,), grad_w_output)
    grad_query = interleaved(pair, core_query)
    return (
        grad_residual,
        grad_gain,
        grad_w_gate,
        grad_w_up,
        grad_w_down,
        grad_w_output,
        grad_query,
    )


def solution(mesh):
    in_specs = (
        P(None, "narrow"),
        P("narrow"),
        P(None, "narrow"),
        P("narrow", "wide"),
        P("narrow", "wide"),
        P("wide", "narrow"),
        P("narrow", "wide"),
        P("narrow", None),
        P("narrow", None),
        P("narrow", None),
        P("wide", "narrow"),
        P("wide", "narrow"),
        P(),
    )
    out_specs = (
        P(None, "narrow"),
        P("narrow"),
        P("narrow", "wide"),
        P("narrow", "wide"),
        P("wide", "narrow"),
        P("narrow", "wide"),
        P(None, "narrow"),
    )
    planes = mesh.shape["wide"] == 16 and mesh.shape["narrow"] == 2
    body = per_device if planes else per_device_general
    return jax.shard_map(
        body, mesh=mesh, in_specs=in_specs, out_specs=out_specs, check_vma=False
    )
```

```python
import functools
import math

import jax
import jax.numpy as jnp
from jax import lax
from jax.experimental import pallas as pl
from jax.experimental.pallas import tpu as pltpu
from jax.sharding import PartitionSpec as P

D = 5120
HEAD_DIM = 128


EPSILON = 1e-06


def contract_rows(left, right):
    return lax.dot_general(
        left, right, (((0,), (0,)), ((), ())), preferred_element_type=jnp.float32
    )


def contract_cols(left, right):
    return lax.dot_general(
        left, right, (((1,), (1,)), ((), ())), preferred_element_type=jnp.float32
    )


def swapped(array, axis, mask):
    size = lax.axis_size(axis)
    return lax.ppermute(array, axis, [(i, i ^ mask) for i in range(size)])


def wide_bits():
    return lax.axis_size("wide").bit_length() - 1


def bit_of(k):
    return (lax.axis_index("wide") >> k) & 1


def as_cube(array):
    count = lax.axis_size("wide")
    return array.reshape((2,) * wide_bits() + (array.shape[0] // count, array.shape[1]))


def masks(stage):
    found = [0]
    for k in stage:
        found += [mask | (1 << k) for mask in found]
    return found


def part_for(cube, stage, mask):
    for k in stage:
        cube = lax.dynamic_slice_in_dim(cube, bit_of(k) ^ ((mask >> k) & 1), 1, k)
    return cube


def scatter_sum(cube, stages):
    for stage in stages:
        low = cube.astype(jnp.bfloat16)
        total = part_for(cube, stage, 0).astype(jnp.float32)
        for mask in masks(stage)[1:]:
            got = swapped(part_for(low, stage, mask), "wide", mask)
            total = total + got.astype(jnp.float32)
        cube = total
    return cube.reshape(cube.shape[-2:])


def gathered(chunk, stages):
    cube = chunk.reshape((1,) * wide_bits() + chunk.shape)
    for stage in reversed(stages):
        held = {0: cube}
        for mask in masks(stage)[1:]:
            held[mask] = swapped(cube, "wide", mask)
        for k in stage:
            first = bit_of(k) == 0
            held = {
                mask: jnp.concatenate(
                    [
                        jnp.where(first, held[mask], held[mask | (1 << k)]),
                        jnp.where(first, held[mask | (1 << k)], held[mask]),
                    ],
                    axis=k,
                )
                for mask in held
                if not mask & (1 << k)
            }
        cube = held[0]
    return cube.reshape(-1, cube.shape[-1])


def own_rows(array):
    bits = wide_bits()
    rows = array.shape[0] // lax.axis_size("wide")
    at = sum(bit_of(k) << (bits - 1 - k) for k in range(bits))
    return lax.dynamic_slice_in_dim(array, at * rows, rows, 0)


def doubled(value, combine):
    for k in range(wide_bits()):
        value = combine(value, swapped(value, "wide", 1 << k))
    return value


def orders():
    core, side, line = (0,), (1,), tuple(range(2, wide_bits()))
    return ([core, side, line], [core, line, side])


def narrow_sum(part):
    if lax.axis_size("narrow") == 2:
        return part + swapped(part, "narrow", 1)
    return lax.psum(part, "narrow")


def narrow_total(part, low):
    if lax.axis_size("narrow") == 2:
        return part + swapped(low, "narrow", 1).astype(jnp.float32)
    return lax.psum(part, "narrow")


def after(arrays, *others):
    return lax.optimization_barrier((tuple(arrays), others))[0]


def to_heads(rows):
    if lax.axis_size("narrow") != 2:
        return lax.all_to_all(rows, "narrow", split_axis=1, concat_axis=0, tiled=True)
    place = lax.axis_index("narrow")
    half = rows.shape[1] // 2
    count = rows.shape[0] // 2
    bit = bit_of(0)
    kept = lax.dynamic_slice_in_dim(rows, place * half, half, 1)
    sent = lax.dynamic_slice(rows, (bit * count, (1 - place) * half), (count, half))
    got = swapped(sent, "narrow", 1)
    other = swapped(got, "wide", 1)
    first = bit == 0
    far = jnp.concatenate([jnp.where(first, got, other), jnp.where(first, other, got)], axis=0)
    low = place == 0
    return jnp.concatenate([jnp.where(low, kept, far), jnp.where(low, far, kept)], axis=0)


def merge_softmax(base, first, second):
    heads = first.shape[1] // 2
    top = jnp.maximum(first[:, :heads], second[:, :heads])
    total = first[:, heads:] * jnp.exp2((first[:, :heads] - top) * base) + second[
        :, heads:
    ] * jnp.exp2((second[:, :heads] - top) * base)
    return jnp.concatenate([top, total], axis=1)


def swiglu_back(gate, up, hidden_grad):
    sigmoid_gate = jax.nn.sigmoid(gate)
    silu_gate = gate * sigmoid_gate
    activated = (silu_gate * up).astype(jnp.bfloat16)
    d_gate = (hidden_grad * up * sigmoid_gate * (1.0 + gate * (1.0 - sigmoid_gate))).astype(
        jnp.bfloat16
    )
    d_up = (hidden_grad * silu_gate).astype(jnp.bfloat16)
    return (activated, d_gate, d_up)


LOG2E = 1.4426950408889634
MASKED = -1e30


def raw_scores(q, key_ref, own_key_ref, from_ref, own_ref):
    cached = contract_cols(q, key_ref[...])
    at = lax.broadcasted_iota(jnp.int32, cached.shape, 1)
    cached = jnp.where(at >= from_ref[...], cached, MASKED)
    own = contract_cols(q, own_key_ref[...])
    own_at = lax.broadcasted_iota(jnp.int32, own.shape, 1)
    own = jnp.where(own_at <= own_ref[...], own, MASKED)
    return (cached, own)


def pick_lane(stat_ref, head):
    lane = lax.broadcasted_iota(jnp.int32, stat_ref.shape, 1)
    return jnp.sum(jnp.where(lane == head, stat_ref[...], 0.0), axis=1, keepdims=True)


def forward_kernel(
    per_group, base, q_ref, key_ref, value_ref, own_key_ref, own_value_ref,
    from_ref, own_ref, out_ref, top_ref, total_ref,
):
    head = pl.program_id(0) * per_group + pl.program_id(1)

    @pl.when(head == 0)
    def _():
        top_ref[...] = jnp.zeros_like(top_ref)
        total_ref[...] = jnp.zeros_like(total_ref)

    cached, own = raw_scores(q_ref[...], key_ref, own_key_ref, from_ref, own_ref)
    top = jnp.maximum(
        jnp.max(cached, axis=1, keepdims=True), jnp.max(own, axis=1, keepdims=True)
    )
    cached = jnp.exp2((cached - top) * base)
    own = jnp.exp2((own - top) * base)
    total = jnp.sum(cached, axis=1, keepdims=True) + jnp.sum(own, axis=1, keepdims=True)
    out = jnp.dot(
        cached.astype(jnp.bfloat16), value_ref[...], preferred_element_type=jnp.float32
    ) + jnp.dot(
        own.astype(jnp.bfloat16), own_value_ref[...], preferred_element_type=jnp.float32
    )
    out_ref[...] = out.astype(out_ref.dtype)
    lane = lax.broadcasted_iota(jnp.int32, top_ref.shape, 1)
    top_ref[...] = jnp.where(lane == head, top, top_ref[...])
    total_ref[...] = jnp.where(lane == head, total, total_ref[...])


def backward_kernel(
    first_group, per_group, base, scale, q_ref, grad_ref, attended_ref, key_ref, value_ref,
    own_key_ref, own_value_ref, from_ref, own_ref, top_ref, inverse_ref, out_ref,
):
    head = (first_group + pl.program_id(0)) * per_group + pl.program_id(1)
    cached, own = raw_scores(q_ref[...], key_ref, own_key_ref, from_ref, own_ref)
    top = pick_lane(top_ref, head)
    inverse = pick_lane(inverse_ref, head)
    grad = grad_ref[...]
    delta = jnp.sum(
        grad.astype(jnp.float32) * attended_ref[...].astype(jnp.float32),
        axis=1,
        keepdims=True,
    )
    cached = jnp.exp2((cached - top) * base) * (contract_cols(grad, value_ref[...]) - delta)
    own = jnp.exp2((own - top) * base) * (contract_cols(grad, own_value_ref[...]) - delta)
    out = jnp.dot(
        cached.astype(jnp.bfloat16), key_ref[...], preferred_element_type=jnp.float32
    ) + jnp.dot(
        own.astype(jnp.bfloat16), own_key_ref[...], preferred_element_type=jnp.float32
    )
    out_ref[...] = (out * (inverse * scale)).astype(out_ref.dtype)


def blocks(tokens, cached, padded, per_group, first):
    head = pl.BlockSpec((tokens, HEAD_DIM), lambda g, p: (0, (first + g) * per_group + p))
    rows = pl.BlockSpec((cached, HEAD_DIM), lambda g, p: (0, first + g))
    own = pl.BlockSpec((padded, HEAD_DIM), lambda g, p: (0, first + g))
    bound = pl.BlockSpec((tokens, 1), lambda g, p: (0, 0))
    stat = pl.BlockSpec((tokens, HEAD_DIM), lambda g, p: (0, 0))
    here = pl.BlockSpec((tokens, HEAD_DIM), lambda g, p: (0, g * per_group + p))
    return (head, rows, own, bound, stat, here)


def forward(
    first, groups, per_group, base, queries, keys, values, own_keys, own_values, bounds
):
    tokens = queries.shape[0]
    cached, padded = keys.shape[0], own_keys.shape[0]
    head, rows, own, bound, stat, here = blocks(tokens, cached, padded, per_group, first)
    work = groups * per_group * tokens * (cached + padded)
    return pl.pallas_call(
        functools.partial(forward_kernel, per_group, base),
        grid=(groups, per_group),
        in_specs=[head, rows, rows, own, own, bound, bound],
        out_specs=[here, stat, stat],
        out_shape=[
            jax.ShapeDtypeStruct((tokens, groups * per_group * HEAD_DIM), jnp.float32),
            jax.ShapeDtypeStruct((tokens, HEAD_DIM), jnp.float32),
            jax.ShapeDtypeStruct((tokens, HEAD_DIM), jnp.float32),
        ],
        compiler_params=pltpu.CompilerParams(vmem_limit_bytes=40 << 20),
        cost_estimate=pl.CostEstimate(
            flops=16 * HEAD_DIM * work, bytes_accessed=20 << 20, transcendentals=work
        ),
    )(queries, keys, values, own_keys, own_values, *bounds)


def backward(
    first, groups, per_group, base, scale, queries, grads, attended, keys, values,
    own_keys, own_values, bounds, top, inverse,
):
    tokens = queries.shape[0]
    cached, padded = keys.shape[0], own_keys.shape[0]
    head, rows, own, bound, stat, here = blocks(tokens, cached, padded, per_group, first)
    work = groups * per_group * tokens * (cached + padded)
    return pl.pallas_call(
        functools.partial(backward_kernel, first, per_group, base, scale),
        grid=(groups, per_group),
        in_specs=[head, here, head, rows, rows, own, own, bound, bound, stat, stat],
        out_specs=here,
        out_shape=jax.ShapeDtypeStruct(grads.shape, jnp.float32),
        compiler_params=pltpu.CompilerParams(vmem_limit_bytes=58 << 20),
        cost_estimate=pl.CostEstimate(
            flops=16 * HEAD_DIM * work, bytes_accessed=12 << 20, transcendentals=work
        ),
    )(queries, grads, attended, keys, values, own_keys, own_values, *bounds, top, inverse)


def split_columns(array, pieces):
    width = array.shape[1] // pieces
    return [array[:, i * width : (i + 1) * width] for i in range(pieces)]


def per_device_general(
    residual,
    norm_gain,
    grad_out,
    w_gate,
    w_up,
    w_down,
    w_output,
    query,
    key,
    value,
    cache_key,
    cache_value,
    visible_from,
):
    wide_count = lax.axis_size("wide")
    wide_place = lax.axis_index("wide")
    tokens = residual.shape[0]
    scale = 1.0 / math.sqrt(HEAD_DIM)
    base = scale * LOG2E

    stream = residual.astype(jnp.float32)
    gain = norm_gain.astype(jnp.float32)
    hidden_part = contract_cols(grad_out, w_down)
    squares = narrow_sum(jnp.sum(stream * stream, axis=1))
    rstd = lax.rsqrt(squares / D + EPSILON)[:, None]
    normed = (stream * rstd * gain).astype(jnp.bfloat16)
    gate_part = jnp.dot(normed, w_gate, preferred_element_type=jnp.float32)
    up_part = jnp.dot(normed, w_up, preferred_element_type=jnp.float32)

    queries, stretch_keys, stretch_values = (to_heads(query), to_heads(key), to_heads(value))
    groups = stretch_keys.shape[1] // HEAD_DIM
    per_group = queries.shape[1] // stretch_keys.shape[1]
    heads = groups * per_group
    cached = cache_key.shape[0]
    span = tokens // wide_count
    start = wide_place * span
    padded = -(-span // HEAD_DIM) * HEAD_DIM
    filler = ((0, padded - span), (0, 0))
    own_keys = jnp.pad(lax.dynamic_slice_in_dim(stretch_keys, start, span, 0), filler)
    own_values = jnp.pad(lax.dynamic_slice_in_dim(stretch_values, start, span, 0), filler)
    position = jnp.arange(tokens, dtype=jnp.int32)[:, None]
    bounds = (
        visible_from[:, None] - wide_place * cached,
        jnp.minimum(position - start, span - 1),
    )

    lows = [part.astype(jnp.bfloat16) for part in (hidden_part, gate_part, up_part)]
    hidden_grad = narrow_total(hidden_part, lows[0])
    gate = narrow_total(gate_part, lows[1])
    up = narrow_total(up_part, lows[2])

    queries, own_keys, own_values = after((queries, own_keys, own_values), *lows)
    early = groups - groups // 4
    outs, tops, totals = [], [], []
    for first, count in ((0, early), (early, groups - early)):
        if count == 0:
            continue
        if first:
            (queries,) = after((queries,), hidden_grad, gate, up)
        out, top, total = forward(
            first, count, per_group, base, queries, cache_key, cache_value, own_keys,
            own_values, bounds,
        )
        outs.append(out)
        tops.append(top[:, : count * per_group])
        totals.append(total[:, : count * per_group])
    local_out = jnp.concatenate(outs, axis=1)
    local_top = jnp.concatenate(tops, axis=1)
    stats = doubled(
        jnp.concatenate([local_top] + totals, axis=1), functools.partial(merge_softmax, base)
    )
    top, inverse = stats[:, :heads], 1.0 / stats[:, heads:]
    factor = jnp.exp2((local_top - top) * base) * inverse
    owner = jnp.arange(heads * HEAD_DIM, dtype=jnp.int32)[None, :] // HEAD_DIM
    choose = (owner == jnp.arange(heads, dtype=jnp.int32)[:, None]).astype(jnp.float32)
    attended_part = local_out * jnp.dot(factor, choose, precision=lax.Precision.HIGHEST)
    side = ((0, 0), (0, HEAD_DIM - heads))
    top, inverse = jnp.pad(top, side), jnp.pad(inverse, side)
    ways = orders()
    attended = jnp.concatenate(
        [
            gathered(scatter_sum(as_cube(part), way).astype(jnp.bfloat16), way)
            for part, way in zip(split_columns(attended_part, 2), ways)
        ],
        axis=1,
    )

    activated, d_gate, d_up = swiglu_back(gate, up, hidden_grad)
    d_normed_part = contract_cols(d_gate, w_gate) + contract_cols(d_up, w_up)
    d_normed = jnp.concatenate(
        [
            scatter_sum(as_cube(part), way)
            for part, way in zip(split_columns(d_normed_part, 2), ways)
        ],
        axis=1,
    )
    rstd_rows = own_rows(rstd)
    scaled = own_rows(residual).astype(jnp.float32) * rstd_rows
    grad_gain = doubled(jnp.sum(d_normed * scaled, axis=0), jnp.add)
    weighted = d_normed * gain
    inner = narrow_sum(jnp.sum(weighted * scaled, axis=1)) / D
    grad_rows = (
        own_rows(grad_out).astype(jnp.float32)
        + rstd_rows * (weighted - scaled * inner[:, None])
    ).astype(jnp.bfloat16)
    grad_residual = jnp.concatenate(
        [gathered(part, way) for part, way in zip(split_columns(grad_rows, 2), ways)], axis=1
    )

    columns = w_output.shape[1]
    width = grad_residual.shape[1]
    if lax.axis_size("narrow") == 2:
        own_panel = lax.dynamic_slice_in_dim(
            grad_residual, (wide_place * columns) % width, columns, 1
        )
        holder = (wide_place * columns) // width == lax.axis_index("narrow")
        panel = jnp.where(holder, own_panel, swapped(own_panel, "narrow", 1))
    else:
        whole = lax.all_gather(grad_residual, "narrow", axis=1, tiled=True)
        panel = lax.dynamic_slice_in_dim(whole, wide_place * columns, columns, 1)
    pieces = 2 if groups % 2 == 0 else 1
    group_count = groups // pieces
    query_grads, query_parts = [], []
    for piece in range(pieces):
        way = ways[piece]
        wide_rows = group_count * per_group * HEAD_DIM
        rows = w_output[piece * wide_rows : (piece + 1) * wide_rows]
        d_attention = gathered(
            scatter_sum(as_cube(contract_cols(panel, rows)), way).astype(jnp.bfloat16), way
        )
        query_part = backward(
            piece * group_count, group_count, per_group, base, scale, queries, d_attention,
            attended, cache_key, cache_value, own_keys, own_values, bounds, top, inverse,
        )
        query_parts.append(query_part)
        query_grads.append(
            gathered(scatter_sum(as_cube(query_part), way).astype(jnp.bfloat16), way)
        )
    grad_query = jnp.concatenate(query_grads, axis=1)
    activated, d_gate, d_up, panel = after((activated, d_gate, d_up, panel), *query_parts)
    grad_w_down = contract_rows(activated, grad_out).astype(jnp.bfloat16)
    grad_w_gate = contract_rows(normed, d_gate).astype(jnp.bfloat16)
    grad_w_up = contract_rows(normed, d_up).astype(jnp.bfloat16)
    grad_w_output = contract_rows(attended, panel).astype(jnp.bfloat16)
    return (
        grad_residual,
        grad_gain,
        grad_w_gate,
        grad_w_up,
        grad_w_down,
        grad_w_output,
        grad_query,
    )


def block_scores(q, pair_ref, from_ref, block):
    rows = pair_ref.shape[0] // 2
    cached = contract_cols(q, pair_ref[:rows, :])
    at = lax.broadcasted_iota(jnp.int32, cached.shape, 1)
    return jnp.where(at >= from_ref[:, block : block + 1], cached, MASKED)


def own_scores(q, pair_ref, own_ref):
    own = contract_cols(q, pair_ref[: pair_ref.shape[0] // 2, :])
    own_at = lax.broadcasted_iota(jnp.int32, own.shape, 1)
    return jnp.where(own_at <= own_ref[...], own, MASKED)


STATS = HEAD_DIM // 2
MESH = pl.DeviceIdType.MESH


def online_kernel(base, first, count, has_own, q_ref, from_ref, own_ref, *refs):
    pairs = refs[: count + has_own]
    rest = refs[count + has_own :]
    earlier, (out_ref, stat_ref) = rest[:-2], rest[-2:]
    head = pl.program_id(0)

    @pl.when(head == 0)
    def _():
        stat_ref[...] = jnp.zeros_like(stat_ref)

    q = q_ref[...]
    top = total = out = None
    if earlier:
        out_before, stat_before = earlier
        top, total = pick_lane(stat_before, head), pick_lane(stat_before, head + STATS)
        out = out_before[...]
    for at, pair in enumerate(pairs):
        rows = pair.shape[0] // 2
        if at < count:
            scores = block_scores(q, pair, from_ref, first + at)
        else:
            scores = own_scores(q, pair, own_ref)
        later = jnp.max(scores, axis=1, keepdims=True)
        if top is not None:
            later = jnp.maximum(top, later)
            shrink = jnp.exp2((top - later) * base)
            total, out = total * shrink, out * shrink
        scores = jnp.exp2((scores - later) * base)
        added = jnp.sum(scores, axis=1, keepdims=True)
        product = jnp.dot(
            scores.astype(jnp.bfloat16), pair[rows:, :], preferred_element_type=jnp.float32
        )
        total = added if top is None else total + added
        out = product if top is None else out + product
        top = later
    out_ref[...] = (out / total if earlier else out).astype(out_ref.dtype)
    lane = lax.broadcasted_iota(jnp.int32, stat_ref.shape, 1)
    stat_ref[...] = jnp.where(
        lane == head, top, jnp.where(lane == head + STATS, total, stat_ref[...])
    )


def online_forward(base, first, heads, queries, bounds, blocks, own, earlier):
    tokens = queries.shape[0]
    whole = lambda array: pl.BlockSpec(array.shape, lambda h: (0, 0))
    here = pl.BlockSpec((tokens, HEAD_DIM), lambda h: (0, h))
    stat = pl.BlockSpec((tokens, HEAD_DIM), lambda h: (0, 0))
    pairs = list(blocks) + ([] if own is None else [own])
    work = heads * tokens * sum(pair.shape[0] // 2 for pair in pairs)
    rest = (*bounds, *pairs)
    kind = jnp.bfloat16 if earlier else jnp.float32
    return pl.pallas_call(
        functools.partial(online_kernel, base, first, len(blocks), int(own is not None)),
        grid=(heads,),
        in_specs=[here] + [whole(array) for array in rest] + ([here, stat] if earlier else []),
        out_specs=[here, stat],
        out_shape=[
            jax.ShapeDtypeStruct((tokens, heads * HEAD_DIM), kind),
            jax.ShapeDtypeStruct((tokens, HEAD_DIM), jnp.float32),
        ],
        compiler_params=pltpu.CompilerParams(vmem_limit_bytes=58 << 20),
        cost_estimate=pl.CostEstimate(
            flops=HEAD_DIM * work, bytes_accessed=1 << 20, transcendentals=work // 8
        ),
    )(queries, *rest, *earlier)


def query_kernel(
    base, scale, count, q_ref, grad_ref, attended_ref, from_ref, own_ref, *refs
):
    pairs = refs[: count + 1]
    stat_ref, rows_ref, out_ref, grad_residual_ref, residuals, row_send, row_recv = refs[
        count + 1 :
    ]
    head = pl.program_id(0)
    place = lax.axis_index("wide")
    x = lax.axis_index("narrow")
    line, group = place // 4, place % 4
    y, core = group // 2, group % 2
    hi, lo = line // 2, line % 2

    def flip(bit):
        weight = 1 << bit
        return (place + weight - 2 * weight * ((place // weight) % 2), x)

    peers = [flip(bit) for bit in (3, 2, 1, 0)]

    def sending(stage):
        ref = (
            residuals.at[core, y, hi, lo],
            residuals.at[core, y, :, lo],
            residuals.at[core, y],
            residuals.at[core],
        )[stage]
        return pltpu.make_async_remote_copy(
            src_ref=ref, dst_ref=ref, send_sem=row_send.at[stage], recv_sem=row_recv.at[stage],
            device_id=peers[stage], device_id_type=MESH,
        )

    @pl.when(head == 0)
    def _():
        barrier = pltpu.get_barrier_semaphore()
        for device in peers:
            pl.semaphore_signal(barrier, inc=1, device_id=device, device_id_type=MESH)
        pl.semaphore_wait(barrier, 4)
        residuals[core, y, hi, lo] = rows_ref[...]
        sending(0).start()

    for stage, step in ((1, 1), (2, 2), (3, 4)):
        @pl.when(head == step)
        def _(stage=stage):
            sending(stage - 1).wait_recv()
            sending(stage).start()

    top = pick_lane(stat_ref, head)
    inverse = pick_lane(stat_ref, head + STATS)
    q, grad = q_ref[...], grad_ref[...]
    delta = jnp.sum(
        grad.astype(jnp.float32) * attended_ref[...].astype(jnp.float32), axis=1, keepdims=True
    )
    out = None
    for at, pair in enumerate(pairs):
        rows = pair.shape[0] // 2
        if at < count:
            scores = block_scores(q, pair, from_ref, at)
        else:
            scores = own_scores(q, pair, own_ref)
        scores = jnp.exp2((scores - top) * base) * (contract_cols(grad, pair[rows:, :]) - delta)
        product = jnp.dot(
            scores.astype(jnp.bfloat16), pair[:rows, :], preferred_element_type=jnp.float32
        )
        out = out + product if at else product
    out_ref[...] = out * (inverse * scale)

    @pl.when(head == pl.num_programs(0) - 1)
    def _():
        sending(3).wait_recv()
        width = rows_ref.shape[1]
        for cp in range(2):
            for yp in range(2):
                at = (2 * cp + yp) * width
                grad_residual_ref[:, :, :, at : at + width] = residuals[cp, yp]
        for stage in range(4):
            sending(stage).wait_send()


def query_backward(
    base, scale, heads, queries, grads, attended, bounds, blocks, own, stats, grad_rows
):
    tokens = queries.shape[0]
    span, width = grad_rows.shape
    whole = lambda array: pl.BlockSpec(array.shape, lambda h: (0, 0))
    head = pl.BlockSpec((tokens, HEAD_DIM), lambda h: (0, h))
    pairs = list(blocks) + [own]
    work = heads * tokens * sum(pair.shape[0] // 2 for pair in pairs)
    rest = (*bounds, *pairs, stats, grad_rows)
    result = (2, 2, span, 4 * width)
    dma = pltpu.SemaphoreType.DMA
    query_part, grad_residual = pl.pallas_call(
        functools.partial(query_kernel, base, scale, len(blocks)),
        grid=(heads,),
        in_specs=[head, head, head] + [whole(array) for array in rest],
        out_specs=[head, pl.BlockSpec(result, lambda h: (0, 0, 0, 0))],
        out_shape=[
            jax.ShapeDtypeStruct((tokens, width), jnp.float32),
            jax.ShapeDtypeStruct(result, jnp.bfloat16),
        ],
        scratch_shapes=[
            pltpu.VMEM((2, 2, 2, 2, span, width), jnp.bfloat16),
            dma((4,)), dma((4,)),
        ],
        compiler_params=pltpu.CompilerParams(
            collective_id=2, has_side_effects=True, vmem_limit_bytes=58 << 20
        ),
        cost_estimate=pl.CostEstimate(
            flops=12 * HEAD_DIM * work, bytes_accessed=12 << 20, transcendentals=work
        ),
    )(queries, grads, attended, *rest)
    return query_part, grad_residual.reshape(tokens, -1)


def placed(near, far, first):
    low = first == 0
    return jnp.concatenate([jnp.where(low, near, far), jnp.where(low, far, near)], axis=0)


def joined(near, far, bit, axis):
    low = bit == 0
    return jnp.concatenate([jnp.where(low, near, far), jnp.where(low, far, near)], axis=axis)


def line_scatter(part, line):
    rows = part.shape[0] // 4
    low = part.astype(jnp.bfloat16)
    total = lax.dynamic_slice_in_dim(part, line * rows, rows, 0)
    for m in (1, 2, 3):
        sent = lax.dynamic_slice_in_dim(low, (line ^ m) * rows, rows, 0)
        total = total + swapped(sent, "wide", m << 2).astype(jnp.float32)
    return total


def line_gather(chunk, line):
    held = [chunk if m == 0 else swapped(chunk, "wide", m << 2) for m in range(4)]
    return joined(
        joined(held[0], held[1], line & 1, 0), joined(held[2], held[3], line & 1, 0), line >> 1, 0
    )


def side_gather(block, group):
    return joined(block, swapped(block, "wide", 2), group >> 1, 1)


def core_gather(block, group):
    return joined(block, swapped(block, "wide", 1), group & 1, 1)


PIECES = 5
def exchange_kernel(
    base, d_gate_ref, d_up_ref, out_ref, stat_ref,
    every_gate, every_up, attended_ref, stats_ref,
    outs, stats, rows, row_stats, all_rows, all_stats,
    local_sem, x_send, x_recv, send_sem, recv_sem,
):
    place = lax.axis_index("wide")
    x = lax.axis_index("narrow")
    line, group = place // 4, place % 4
    count = d_gate_ref.shape[0]
    lines = [place + 4 * (1 - 2 * (line % 2)), place + 8 * (1 - 2 * (line // 2))]
    lines.append(lines[0] + lines[1] - place)
    at_line = [at // 4 for at in lines]
    barrier = pltpu.get_barrier_semaphore()
    pl.semaphore_signal(barrier, inc=1, device_id=(place, 1 - x), device_id_type=MESH)
    for peer in lines:
        pl.semaphore_signal(barrier, inc=1, device_id=(peer, x), device_id_type=MESH)
    pl.semaphore_wait(barrier, 4)

    here = pl.ds(pl.multiple_of(x * count, 16), count)
    moves = []
    for at, (src, dst) in enumerate(((d_gate_ref, every_gate), (d_up_ref, every_up))):
        far = pltpu.make_async_remote_copy(
            src_ref=src, dst_ref=dst.at[here], send_sem=x_send.at[at], recv_sem=x_recv.at[at],
            device_id=(place, 1 - x), device_id_type=MESH,
        )
        near = pltpu.make_async_copy(src, dst.at[here], local_sem.at[at])
        far.start()
        near.start()
        moves += [far, near]

    def line_copy(src, dst, at, m):
        return pltpu.make_async_remote_copy(
            src_ref=src, dst_ref=dst, send_sem=send_sem.at[at, m], recv_sem=recv_sem.at[at, m],
            device_id=(lines[m], x), device_id_type=MESH,
        )

    def scattered(m):
        return (
            line_copy(out_ref.at[at_line[m]], outs.at[m], 0, m),
            line_copy(stat_ref.at[at_line[m]], stats.at[m], 1, m),
        )

    for m in range(3):
        for sending in scattered(m):
            sending.start()
    for m in range(3):
        for sending in scattered(m):
            sending.wait_recv()
    parts = [stat_ref[line]] + [stats[m] for m in range(3)]
    top = functools.reduce(jnp.maximum, parts)
    lane = lax.broadcasted_iota(jnp.int32, top.shape, 1)
    weights = [
        jnp.where(
            lane < STATS, 0.0, pltpu.roll(jnp.exp2((part - top) * base), STATS, 1) * part
        )
        for part in parts
    ]
    total = functools.reduce(jnp.add, weights)
    inverse = 1.0 / jnp.where(total > 0.0, total, 1.0)
    row_stats[...] = jnp.where(lane < STATS, top, inverse)
    all_stats[line] = row_stats[...]
    weights = [weight * inverse for weight in weights]
    for h in range(rows.shape[1] // HEAD_DIM):
        cols = slice(h * HEAD_DIM, (h + 1) * HEAD_DIM)
        pieces = [out_ref[line, :, cols]] + [outs[m, :, cols] for m in range(3)]
        value = functools.reduce(
            jnp.add,
            [
                piece.astype(jnp.float32) * weight[:, STATS + h : STATS + h + 1]
                for piece, weight in zip(pieces, weights)
            ],
        )
        rows[:, cols] = value.astype(jnp.bfloat16)
    all_rows[line] = rows[...]

    def spread(m, where):
        return (
            line_copy(rows, all_rows.at[where], 2, m),
            line_copy(row_stats, all_stats.at[where], 3, m),
        )

    for m in range(3):
        for sending in spread(m, line):
            sending.start()
    for m in range(3):
        for sending in spread(m, at_line[m]):
            sending.wait_recv()
    attended_ref[...] = all_rows[...]
    stats_ref[...] = all_stats[...]
    for m in range(3):
        for sending in scattered(m) + spread(m, line):
            sending.wait_send()
    for move in moves:
        move.wait()


def exchange(base, d_gate, d_up, out, stat):
    tokens, width = out.shape
    span = tokens // 4
    low, full = jnp.bfloat16, jnp.float32
    vmem = pl.BlockSpec(memory_space=pltpu.VMEM)
    hbm = pl.BlockSpec(memory_space=pl.ANY)
    dma = pltpu.SemaphoreType.DMA
    every = jax.ShapeDtypeStruct((2 * d_gate.shape[0], d_gate.shape[1]), low)
    every_gate, every_up, attended, stats = pl.pallas_call(
        functools.partial(exchange_kernel, base),
        out_shape=[
            every,
            every,
            jax.ShapeDtypeStruct((4, span, width), low),
            jax.ShapeDtypeStruct((4, span, HEAD_DIM), full),
        ],
        in_specs=[hbm, hbm, vmem, vmem],
        out_specs=[hbm, hbm, vmem, vmem],
        scratch_shapes=[
            pltpu.VMEM((3, span, width), low),
            pltpu.VMEM((3, span, HEAD_DIM), full),
            pltpu.VMEM((span, width), low),
            pltpu.VMEM((span, HEAD_DIM), full),
            pltpu.VMEM((4, span, width), low),
            pltpu.VMEM((4, span, HEAD_DIM), full),
            dma((2,)), dma((2,)), dma((2,)), dma((4, 3)), dma((4, 3)),
        ],
        compiler_params=pltpu.CompilerParams(
            collective_id=1, has_side_effects=True, vmem_limit_bytes=40 << 20
        ),
        cost_estimate=pl.CostEstimate(
            flops=20_000_000_000, bytes_accessed=8 << 20, transcendentals=0
        ),
    )(d_gate, d_up, out.reshape(4, span, width), stat.reshape(4, span, HEAD_DIM))
    return every_gate, every_up, attended.reshape(tokens, width), stats.reshape(tokens, HEAD_DIM)


def middle_kernel(
    part_ref, residual_ref, rstd_ref, out_grad_ref, gain_ref, w_ref, attended_ref, activated_ref,
    rows_ref, gain_grad_ref, panel_ref, d_attention_ref, every_attended_ref, every_activated,
    residual_rows, out_grad_rows, gain_to, gain_from, gain_all, attended_all,
    from_core, to_side, from_side, to_near, from_near, kept, to_far, from_far, summed,
    da_send, da_own, da_core, da_to_side, da_side, da_to_near, da_near, da_kept, da_to_far, da_far,
    inner_to, inner_from, grad_rows, panels, gathered_ref,
    send_sem, recv_sem, da_send_sem, da_recv_sem, inner_send, inner_recv,
    panel_send, panel_recv, gather_send, gather_recv,
    local_sem, x_send, x_recv, gain_send, gain_recv, attended_send, attended_recv,
):
    place = lax.axis_index("wide")
    x = lax.axis_index("narrow")
    line, group = place // 4, place % 4
    y, core = group // 2, group % 2
    hi, lo = line // 2, line % 2
    span, width = rows_ref.shape
    step = width // PIECES
    block = 2 * core + y

    def flip(bit):
        weight = 1 << bit
        at = (place // weight) % 2
        return (place + weight - 2 * weight * at, x)

    peers = {"core": flip(0), "side": flip(1), "near": flip(2), "far": flip(3), "x": (place, 1 - x)}
    targets = [(8 * x + 2 * block + j, nx) for j in (0, 1) for nx in (0, 1)]
    source_x, source_block = place // 8, (place % 8) // 2
    source_group = 2 * (source_block % 2) + source_block // 2
    sources = [(4 * s + source_group, source_x) for s in range(4)]

    def is_me(device):
        return jnp.logical_and(device[0] == place, device[1] == x)

    def not_me(device):
        return jnp.logical_not(is_me(device))

    barrier = pltpu.get_barrier_semaphore()
    for device in peers.values():
        pl.semaphore_signal(barrier, inc=1, device_id=device, device_id_type=MESH)
    for device in targets + sources:
        @pl.when(not_me(device))
        def _(device=device):
            pl.semaphore_signal(barrier, inc=1, device_id=device, device_id_type=MESH)
    mine = jnp.logical_and(place // 8 == x, source_group == group).astype(jnp.int32)
    pl.semaphore_wait(barrier, 13 - 2 * mine)

    def copy(src, dst, sends, recvs, at, device):
        return pltpu.make_async_remote_copy(
            src_ref=src, dst_ref=dst, send_sem=sends.at[at], recv_sem=recvs.at[at],
            device_id=device, device_id_type=MESH,
        )

    here = (
        pl.ds(pl.multiple_of(line * span, 16), span),
        pl.ds(pl.multiple_of(block * width, HEAD_DIM), width),
    )
    loads = [
        pltpu.make_async_copy(residual_ref.at[here], residual_rows, local_sem.at[0]),
        pltpu.make_async_copy(out_grad_ref.at[here], out_grad_rows, local_sem.at[1]),
    ]
    count = activated_ref.shape[0]
    own_units = every_activated.at[pl.ds(pl.multiple_of(x * count, 16), count)]
    units_local = pltpu.make_async_copy(activated_ref, own_units, local_sem.at[2])
    units_far = pltpu.make_async_remote_copy(
        src_ref=activated_ref, dst_ref=own_units, send_sem=x_send.at[0], recv_sem=x_recv.at[0],
        device_id=peers["x"], device_id_type=MESH,
    )
    for load in loads + [units_local, units_far]:
        load.start()

    def scatter(outgoing, own, bufs, sends, recvs, finish):
        core_buf, side_out, side_in, near_out, near_in, keep, far_out, far_in = bufs

        def cols(p):
            return pl.ds(p * step, step)

        def core_copy(yp, p):
            return copy(
                outgoing(yp, p), core_buf.at[yp, :, :, :, cols(p)], sends, recvs,
                (yp, p), peers["core"],
            )

        def side_copy(p):
            return copy(
                side_out.at[:, :, :, cols(p)], side_in.at[:, :, :, cols(p)], sends, recvs,
                (2, p), peers["side"],
            )

        def near_copy(p):
            return copy(
                near_out.at[:, :, cols(p)], near_in.at[:, :, cols(p)], sends, recvs,
                (3, p), peers["near"],
            )

        def far_copy(p):
            return copy(
                far_out.at[:, cols(p)], far_in.at[:, cols(p)], sends, recvs,
                (4, p), peers["far"],
            )

        def stage(s, p):
            if s == 0:
                core_copy(0, p).start()
                core_copy(1, p).start()
            elif s == 1:
                core_copy(0, p).wait_recv()
                core_copy(1, p).wait_recv()
                for h in range(2):
                    for l in range(2):
                        value = own(1 - y, h, l, p) + core_buf[1 - y, h, l, :, cols(p)].astype(
                            jnp.float32
                        )
                        side_out[h, l, :, cols(p)] = value.astype(jnp.bfloat16)
                side_copy(p).start()
            elif s == 2:
                side_copy(p).wait_recv()

                def total(h, l):
                    return (
                        own(y, h, l, p)
                        + core_buf[y, h, l, :, cols(p)].astype(jnp.float32)
                        + side_in[h, l, :, cols(p)].astype(jnp.float32)
                    )

                for h in range(2):
                    near_out[h, :, cols(p)] = total(h, 1 - lo).astype(jnp.bfloat16)
                near_copy(p).start()
                for h in range(2):
                    keep[h, :, cols(p)] = total(h, lo)
            elif s == 3:
                near_copy(p).wait_recv()

                def total(h):
                    return keep[h, :, cols(p)] + near_in[h, :, cols(p)].astype(jnp.float32)

                far_out[:, cols(p)] = total(1 - hi).astype(jnp.bfloat16)
                far_copy(p).start()
            else:
                far_copy(p).wait_recv()
                finish(
                    p,
                    keep[hi, :, cols(p)]
                    + near_in[hi, :, cols(p)].astype(jnp.float32)
                    + far_in[:, cols(p)].astype(jnp.float32),
                )

        for p in range(PIECES):
            stage(0, p)
        for t in range(-2, PIECES + 2):
            for s, p in ((2, t), (1, t + 2), (3, t - 1), (4, t - 2)):
                if 0 <= p < PIECES:
                    stage(s, p)

        def drain():
            for p in range(PIECES):
                core_copy(0, p).wait_send()
                core_copy(1, p).wait_send()
                side_copy(p).wait_send()
                near_copy(p).wait_send()
                far_copy(p).wait_send()

        return drain

    def part_cols(yp, cp, p):
        return pl.ds(pl.multiple_of((2 * cp + yp) * width + p * step, HEAD_DIM), step)

    def part_finish(p, value):
        summed[:, pl.ds(p * step, step)] = value

    drain_parts = scatter(
        lambda yp, p: part_ref.at[:, :, :, part_cols(yp, 1 - core, p)],
        lambda yp, h, l, p: part_ref[h, l, :, part_cols(yp, core, p)].astype(jnp.float32),
        (from_core, to_side, from_side, to_near, from_near, kept, to_far, from_far),
        send_sem, recv_sem, part_finish,
    )

    attended_all[y, core] = attended_ref[...]
    attended_side = copy(
        attended_all.at[y, core], attended_all.at[y, core], attended_send, attended_recv, 0,
        peers["side"],
    )
    attended_core = copy(
        attended_all.at[:, core], attended_all.at[:, core], attended_send, attended_recv, 1,
        peers["core"],
    )
    for load in loads:
        load.wait()
    d_normed = summed[...]
    scaled = residual_rows[...].astype(jnp.float32) * rstd_ref[:, :1]
    weighted = d_normed * gain_ref[...]
    inner = jnp.sum(weighted * scaled, axis=1, keepdims=True)
    inner = jnp.broadcast_to(inner, inner_to.shape[1:])
    inner_copies = []

    def gain_copy(at):
        return copy(
            gain_to.at[at], gain_from.at[at], gain_send, gain_recv, at, peers[("near", "far")[at]]
        )

    gain_side = copy(
        gain_all.at[core, y], gain_all.at[core, y], gain_send, gain_recv, 2, peers["side"]
    )
    gain_core = copy(
        gain_all.at[core], gain_all.at[core], gain_send, gain_recv, 3, peers["core"]
    )
    for at, name in enumerate(("core", "side", "x")):
        inner_to[at] = inner
        sending = copy(
            inner_to.at[at], inner_from.at[at], inner_send, inner_recv, at, peers[name]
        )
        sending.start()
        inner_copies.append(sending)
        if at == 0:
            gain_to[0] = jnp.broadcast_to(
                jnp.sum(d_normed * scaled, axis=0, keepdims=True), gain_to.shape[1:]
            )
            gain_copy(0).start()
            attended_side.start()
        sending.wait_recv()
        inner = inner + inner_from[at]
    inner = inner[:, :1] * (1.0 / D)
    rows = (
        out_grad_rows[...].astype(jnp.float32) + rstd_ref[:, :1] * (weighted - scaled * inner)
    ).astype(jnp.bfloat16)
    grad_rows[...] = rows
    across = panels.shape[3]
    starts = (0, width - across)

    def panel_copy(at):
        j = at // 2
        return pltpu.make_async_remote_copy(
            src_ref=grad_rows.at[:, pl.ds(starts[j], across)], dst_ref=panels.at[hi, lo],
            send_sem=panel_send.at[at], recv_sem=panel_recv.at[line],
            device_id=targets[at], device_id_type=MESH,
        )

    for at, device in enumerate(targets):
        @pl.when(not_me(device))
        def _(at=at):
            panel_copy(at).start()

        @pl.when(is_me(device))
        def _(at=at):
            begin = starts[at // 2]
            panels[hi, lo] = grad_rows[:, begin : begin + across]
    rows_ref[...] = rows
    gain_copy(0).wait_recv()
    gain_to[1] = gain_to[0] + gain_from[0]
    gain_copy(1).start()
    for s, device in enumerate(sources):
        @pl.when(not_me(device))
        def _(s=s, device=device):
            pltpu.make_async_remote_copy(
                src_ref=grad_rows.at[:, pl.ds(0, across)], dst_ref=panels.at[s // 2, s % 2],
                send_sem=panel_send.at[0], recv_sem=panel_recv.at[s],
                device_id=device, device_id_type=MESH,
            ).wait_recv()

    window = panels[...].reshape(-1, across)
    columns = panel_ref.shape[1]
    panel_ref[...] = jnp.where(
        place % 2 == 0, window[:, :columns], window[:, across - columns :]
    )
    panel = panel_ref[...]
    shape = (2, 2, grad_rows.shape[0], width)

    def product(yp, cp):
        block = w_ref[:, pl.ds(pl.multiple_of((2 * yp + cp) * width, HEAD_DIM), width)]
        return jnp.dot(panel, block, preferred_element_type=jnp.float32).reshape(shape)

    for yp in range(2):
        da_send[yp] = product(yp, 1 - core).astype(jnp.bfloat16)
        da_own[yp] = product(yp, core)
    gain_copy(1).wait_recv()
    gain_all[core, y] = gain_to[1] + gain_from[1]
    gain_side.start()
    attended_side.wait_recv()
    attended_core.start()

    def gather_far(p):
        at = pl.ds(p * step, step)
        return copy(
            gathered_ref.at[hi, lo, :, at], gathered_ref.at[hi, lo, :, at],
            gather_send, gather_recv, (0, p), peers["far"],
        )

    def gather_near(p):
        at = pl.ds(p * step, step)
        return copy(
            gathered_ref.at[:, lo, :, at], gathered_ref.at[:, lo, :, at],
            gather_send, gather_recv, (1, p), peers["near"],
        )

    def da_finish(p, value):
        gathered_ref[hi, lo, :, pl.ds(p * step, step)] = value.astype(jnp.bfloat16)
        gather_far(p).start()
        if p > 0:
            gather_far(p - 1).wait_recv()
            gather_near(p - 1).start()

    drain_da = scatter(
        lambda yp, p: da_send.at[yp, :, :, :, pl.ds(p * step, step)],
        lambda yp, h, l, p: da_own[yp, h, l, :, pl.ds(p * step, step)],
        (da_core, da_to_side, da_side, da_to_near, da_near, da_kept, da_to_far, da_far),
        da_send_sem, da_recv_sem, da_finish,
    )
    gather_far(PIECES - 1).wait_recv()
    gather_near(PIECES - 1).start()
    gain_side.wait_recv()
    gain_core.start()
    attended_core.wait_recv()
    for yp in range(2):
        for cp in range(2):
            at = (2 * yp + cp) * width
            every_attended_ref[:, at : at + width] = attended_all[yp, cp]
    gain_core.wait_recv()
    gain_grad_ref[...] = gain_all[...]
    for p in range(PIECES):
        gather_near(p).wait_recv()
    d_attention_ref[...] = gathered_ref[...]

    drain_parts()
    for sending in inner_copies:
        sending.wait_send()
    for at, device in enumerate(targets):
        @pl.when(not_me(device))
        def _(at=at):
            panel_copy(at).wait_send()
    drain_da()
    for p in range(PIECES):
        gather_far(p).wait_send()
        gather_near(p).wait_send()
    for sending in (gain_copy(0), gain_copy(1), gain_side, gain_core, attended_side, attended_core):
        sending.wait_send()
    units_local.wait()
    units_far.wait()


def middle(part, residual, rstd, out_grad, gain, weights, attended, activated):
    tokens, width = attended.shape
    rows, columns = tokens // 4, weights.shape[0]
    across = -(-columns // HEAD_DIM) * HEAD_DIM
    low, full = jnp.bfloat16, jnp.float32
    chunk = (2, 2, rows, width)
    stages = [
        pltpu.VMEM((2,) + chunk, low),
        pltpu.VMEM(chunk, low),
        pltpu.VMEM(chunk, low),
        pltpu.VMEM((2, rows, width), low),
        pltpu.VMEM((2, rows, width), low),
        pltpu.VMEM((2, rows, width), full),
        pltpu.VMEM((rows, width), low),
        pltpu.VMEM((rows, width), low),
    ]
    hbm = pl.BlockSpec(memory_space=pl.ANY)
    vmem = pl.BlockSpec(memory_space=pltpu.VMEM)
    dma = pltpu.SemaphoreType.DMA
    return pl.pallas_call(
        middle_kernel,
        out_shape=[
            jax.ShapeDtypeStruct((rows, width), low),
            jax.ShapeDtypeStruct((2, 2, 8, width), full),
            jax.ShapeDtypeStruct((tokens, columns), low),
            jax.ShapeDtypeStruct(chunk, low),
            jax.ShapeDtypeStruct((tokens, 4 * width), low),
            jax.ShapeDtypeStruct((2 * activated.shape[0], tokens), low),
        ],
        in_specs=[vmem, hbm, vmem, hbm, vmem, vmem, vmem, hbm],
        out_specs=[vmem] * 5 + [hbm],
        scratch_shapes=[
            pltpu.VMEM((rows, width), low),
            pltpu.VMEM((rows, width), low),
            pltpu.VMEM((2, 8, width), full),
            pltpu.VMEM((2, 8, width), full),
            pltpu.VMEM((2, 2, 8, width), full),
            pltpu.VMEM((2, 2, tokens, width), low),
        ]
        + stages
        + [pltpu.VMEM((rows, width), full)]
        + [pltpu.VMEM((2,) + chunk, low), pltpu.VMEM((2,) + chunk, full)]
        + stages
        + [
            pltpu.VMEM((3, rows, HEAD_DIM), full),
            pltpu.VMEM((3, rows, HEAD_DIM), full),
            pltpu.VMEM((rows, width), low),
            pltpu.VMEM((2, 2, rows, across), low),
            pltpu.VMEM(chunk, low),
            dma((5, PIECES)), dma((5, PIECES)), dma((5, PIECES)), dma((5, PIECES)),
            dma((3,)), dma((3,)), dma((4,)), dma((4,)), dma((2, PIECES)), dma((2, PIECES)),
            dma((3,)), dma((1,)), dma((1,)), dma((4,)), dma((4,)), dma((2,)), dma((2,)),
        ],
        compiler_params=pltpu.CompilerParams(
            collective_id=0, has_side_effects=True, vmem_limit_bytes=40 << 20
        ),
        cost_estimate=pl.CostEstimate(
            flops=60_000_000_000, bytes_accessed=8 << 20, transcendentals=0
        ),
    )(
        part.reshape(2, 2, rows, -1), residual, rstd, out_grad, gain, weights, attended, activated
    )


def per_device(
    residual,
    norm_gain,
    grad_out,
    w_gate,
    w_up,
    w_down,
    w_output,
    query,
    key,
    value,
    cache_key,
    cache_value,
    visible_from,
):
    wide_place = lax.axis_index("wide")
    side = lax.axis_index("narrow")
    line, group = wide_place >> 2, wide_place & 3
    tokens = residual.shape[0]
    cached = cache_key.shape[0]
    hidden = w_down.shape[0]
    scale = 1.0 / math.sqrt(HEAD_DIM)
    base = scale * LOG2E
    heads = query.shape[1] // (8 * HEAD_DIM)
    group_width = heads * HEAD_DIM
    span = tokens // 4

    def for_side(array, place):
        count = array.shape[0] // 2
        return lax.dynamic_slice_in_dim(array, place * count, count, 0)

    def for_heads(array, place):
        width = array.shape[1] // 8
        return lax.dynamic_slice_in_dim(array, (place * 4 + group) * width, width, 1)

    block = 2 * (group & 1) + (group >> 1)

    stream = residual.astype(jnp.float32)
    gain = norm_gain.astype(jnp.float32)
    squares = narrow_sum(jnp.sum(stream * stream, axis=1))

    near = jnp.concatenate([for_heads(array, side) for array in (query, key, value)], axis=1)
    sent = jnp.concatenate([for_heads(array, 1 - side) for array in (query, key, value)], axis=1)
    stretch = placed(near, swapped(sent, "narrow", 1), side)
    queries = stretch[:, :group_width]
    own = lax.dynamic_slice_in_dim(stretch[:, group_width:], line * span, span, 0)
    own = jnp.pad(own, ((0, HEAD_DIM - span), (0, 0)))
    own = jnp.concatenate([own[:, :HEAD_DIM], own[:, HEAD_DIM:]], axis=0)

    def stacked(m):
        at = (group ^ m) * HEAD_DIM
        return jnp.concatenate(
            [
                lax.dynamic_slice_in_dim(cache, at, HEAD_DIM, 1)
                for cache in (cache_key, cache_value)
            ],
            axis=0,
        )

    cache_blocks = [
        stacked(m) if m == 0 else swapped(stacked(m), "wide", m) for m in range(4)
    ]
    position = jnp.arange(tokens, dtype=jnp.int32)[:, None]
    starts = jnp.stack([((line << 2) | (group ^ m)) * cached for m in range(4)])
    bounds = (
        visible_from[:, None] - starts[None, :],
        jnp.minimum(position - line * span, span - 1),
    )

    def halves(part):
        sent = for_side(part, 1 - side).astype(jnp.bfloat16)
        return sent, swapped(sent, "narrow", 1)

    def across(weights, rows, dim):
        return lax.dot_general(
            weights, rows, (((dim,), (1,)), ((), ())), preferred_element_type=jnp.float32
        )

    hidden_part = across(w_down, grad_out, 1)
    rstd = lax.rsqrt(squares / D + EPSILON)[:, None]
    normed = (stream * rstd * gain).astype(jnp.bfloat16)
    gate_part = across(w_gate, normed, 0)
    up_part = across(w_up, normed, 0)
    matmuls = (hidden_part, gate_part, up_part)
    exchanged = [halves(part) for part in matmuls]
    (early_queries,) = after((queries,), *[sent for sent, _ in exchanged])
    early = online_forward(base, 0, heads, early_queries, bounds, cache_blocks[:2], own, ())
    local_out, local_stat = online_forward(
        base, 2, heads, queries, bounds, cache_blocks[2:], None, early
    )
    gots = after([got for _, got in exchanged], local_out)
    hidden_grad, gate, up = [
        for_side(part, side) + got.astype(jnp.float32) for part, got in zip(matmuls, gots)
    ]
    activated_near, d_gate_near, d_up_near = swiglu_back(gate, up, hidden_grad)
    d_gate, d_up, attended, stats = exchange(
        base, d_gate_near, d_up_near, local_out, local_stat
    )
    def back(grads, weights):
        return lax.dot_general(
            grads, weights, (((0,), (1,)), ((), ())), preferred_element_type=jnp.float32
        )

    d_normed_part = (back(d_gate, w_gate) + back(d_up, w_up)).astype(jnp.bfloat16)

    rstd_rows = lax.dynamic_slice_in_dim(rstd, line * span, span, 0)
    grad_rows, gain_rows, panel, d_attention, every_attended, activated = middle(
        d_normed_part,
        residual,
        jnp.broadcast_to(rstd_rows, (span, HEAD_DIM)),
        grad_out,
        lax.dynamic_slice_in_dim(gain, block * group_width, group_width, 0)[None, :],
        w_output.T,
        attended,
        activated_near,
    )
    d_attention = d_attention.reshape(tokens, group_width)
    grad_gain = gain_rows[:, :, 0].reshape(-1)

    def interleaved(pair, other):
        low = (group & 1) == 0
        width = group_width
        first, second = jnp.where(low, pair, other), jnp.where(low, other, pair)
        return jnp.concatenate(
            [first[:, :width], second[:, :width], first[:, width:], second[:, width:]], axis=1
        )

    query_part, grad_residual = query_backward(
        base, scale, heads, queries, d_attention, attended, bounds, cache_blocks, own, stats,
        grad_rows,
    )

    def outer(grads):
        return lax.dot_general(
            normed, grads, (((0,), (1,)), ((), ())), preferred_element_type=jnp.float32
        ).astype(jnp.bfloat16)

    query_low = query_part.astype(jnp.bfloat16)

    def query_rows(array, at):
        return lax.dynamic_slice_in_dim(array, at * span, span, 0)

    d_gate, d_up, activated, panel = after((d_gate, d_up, activated, panel), query_part)
    got = [swapped(query_rows(query_low, line ^ m), "wide", m << 2) for m in (1, 2, 3)]
    grad_w_gate = outer(d_gate)
    got = after(got, grad_w_gate)
    total = query_rows(query_part, line)
    for piece in got:
        total = total + piece.astype(jnp.float32)
    total = total.astype(jnp.bfloat16)
    held = [total] + [swapped(total, "wide", m << 2) for m in (1, 2, 3)]
    (d_up,) = after((d_up,), grad_w_gate)
    grad_w_up = outer(d_up)
    held = after(held, grad_w_up)
    own_query = joined(
        joined(held[0], held[1], line & 1, 0), joined(held[2], held[3], line & 1, 0), line >> 1, 0
    )
    side_query = swapped(own_query, "wide", 2)
    (activated,) = after((activated,), grad_w_up)
    grad_w_down = jnp.dot(
        activated, grad_out, preferred_element_type=jnp.float32
    ).astype(jnp.bfloat16)
    (side_query,) = after((side_query,), grad_w_down)
    pair = joined(own_query, side_query, group >> 1, 1)
    core_query = swapped(pair, "wide", 1)
    (panel,) = after((panel,), grad_w_down)
    grad_w_output = contract_rows(every_attended, panel).astype(jnp.bfloat16)
    (core_query,) = after((core_query,), grad_w_output)
    grad_query = interleaved(pair, core_query)
    return (
        grad_residual,
        grad_gain,
        grad_w_gate,
        grad_w_up,
        grad_w_down,
        grad_w_output,
        grad_query,
    )


def solution(mesh):
    in_specs = (
        P(None, "narrow"),
        P("narrow"),
        P(None, "narrow"),
        P("narrow", "wide"),
        P("narrow", "wide"),
        P("wide", "narrow"),
        P("narrow", "wide"),
        P("narrow", None),
        P("narrow", None),
        P("narrow", None),
        P("wide", "narrow"),
        P("wide", "narrow"),
        P(),
    )
    out_specs = (
        P(None, "narrow"),
        P("narrow"),
        P("narrow", "wide"),
        P("narrow", "wide"),
        P("wide", "narrow"),
        P("narrow", "wide"),
        P(None, "narrow"),
    )
    planes = mesh.shape["wide"] == 16 and mesh.shape["narrow"] == 2
    body = per_device if planes else per_device_general
    return jax.shard_map(
        body, mesh=mesh, in_specs=in_specs, out_specs=out_specs, check_vma=False
    )
```

```python
import functools
import math

import jax
import jax.numpy as jnp
from jax import lax
from jax.experimental import pallas as pl
from jax.experimental.pallas import tpu as pltpu
from jax.sharding import PartitionSpec as P

D = 5120
HEAD_DIM = 128


EPSILON = 1e-06


def contract_rows(left, right):
    return lax.dot_general(
        left, right, (((0,), (0,)), ((), ())), preferred_element_type=jnp.float32
    )


def contract_cols(left, right):
    return lax.dot_general(
        left, right, (((1,), (1,)), ((), ())), preferred_element_type=jnp.float32
    )


def swapped(array, axis, mask):
    size = lax.axis_size(axis)
    return lax.ppermute(array, axis, [(i, i ^ mask) for i in range(size)])


def wide_bits():
    return lax.axis_size("wide").bit_length() - 1


def bit_of(k):
    return (lax.axis_index("wide") >> k) & 1


def as_cube(array):
    count = lax.axis_size("wide")
    return array.reshape((2,) * wide_bits() + (array.shape[0] // count, array.shape[1]))


def masks(stage):
    found = [0]
    for k in stage:
        found += [mask | (1 << k) for mask in found]
    return found


def part_for(cube, stage, mask):
    for k in stage:
        cube = lax.dynamic_slice_in_dim(cube, bit_of(k) ^ ((mask >> k) & 1), 1, k)
    return cube


def scatter_sum(cube, stages):
    for stage in stages:
        low = cube.astype(jnp.bfloat16)
        total = part_for(cube, stage, 0).astype(jnp.float32)
        for mask in masks(stage)[1:]:
            got = swapped(part_for(low, stage, mask), "wide", mask)
            total = total + got.astype(jnp.float32)
        cube = total
    return cube.reshape(cube.shape[-2:])


def gathered(chunk, stages):
    cube = chunk.reshape((1,) * wide_bits() + chunk.shape)
    for stage in reversed(stages):
        held = {0: cube}
        for mask in masks(stage)[1:]:
            held[mask] = swapped(cube, "wide", mask)
        for k in stage:
            first = bit_of(k) == 0
            held = {
                mask: jnp.concatenate(
                    [
                        jnp.where(first, held[mask], held[mask | (1 << k)]),
                        jnp.where(first, held[mask | (1 << k)], held[mask]),
                    ],
                    axis=k,
                )
                for mask in held
                if not mask & (1 << k)
            }
        cube = held[0]
    return cube.reshape(-1, cube.shape[-1])


def own_rows(array):
    bits = wide_bits()
    rows = array.shape[0] // lax.axis_size("wide")
    at = sum(bit_of(k) << (bits - 1 - k) for k in range(bits))
    return lax.dynamic_slice_in_dim(array, at * rows, rows, 0)


def doubled(value, combine):
    for k in range(wide_bits()):
        value = combine(value, swapped(value, "wide", 1 << k))
    return value


def orders():
    core, side, line = (0,), (1,), tuple(range(2, wide_bits()))
    return ([core, side, line], [core, line, side])


def narrow_sum(part):
    if lax.axis_size("narrow") == 2:
        return part + swapped(part, "narrow", 1)
    return lax.psum(part, "narrow")


def narrow_total(part, low):
    if lax.axis_size("narrow") == 2:
        return part + swapped(low, "narrow", 1).astype(jnp.float32)
    return lax.psum(part, "narrow")


def after(arrays, *others):
    return lax.optimization_barrier((tuple(arrays), others))[0]


def to_heads(rows):
    if lax.axis_size("narrow") != 2:
        return lax.all_to_all(rows, "narrow", split_axis=1, concat_axis=0, tiled=True)
    place = lax.axis_index("narrow")
    half = rows.shape[1] // 2
    count = rows.shape[0] // 2
    bit = bit_of(0)
    kept = lax.dynamic_slice_in_dim(rows, place * half, half, 1)
    sent = lax.dynamic_slice(rows, (bit * count, (1 - place) * half), (count, half))
    got = swapped(sent, "narrow", 1)
    other = swapped(got, "wide", 1)
    first = bit == 0
    far = jnp.concatenate([jnp.where(first, got, other), jnp.where(first, other, got)], axis=0)
    low = place == 0
    return jnp.concatenate([jnp.where(low, kept, far), jnp.where(low, far, kept)], axis=0)


def merge_softmax(base, first, second):
    heads = first.shape[1] // 2
    top = jnp.maximum(first[:, :heads], second[:, :heads])
    total = first[:, heads:] * jnp.exp2((first[:, :heads] - top) * base) + second[
        :, heads:
    ] * jnp.exp2((second[:, :heads] - top) * base)
    return jnp.concatenate([top, total], axis=1)


def swiglu_back(gate, up, hidden_grad):
    sigmoid_gate = jax.nn.sigmoid(gate)
    silu_gate = gate * sigmoid_gate
    activated = (silu_gate * up).astype(jnp.bfloat16)
    d_gate = (hidden_grad * up * sigmoid_gate * (1.0 + gate * (1.0 - sigmoid_gate))).astype(
        jnp.bfloat16
    )
    d_up = (hidden_grad * silu_gate).astype(jnp.bfloat16)
    return (activated, d_gate, d_up)


LOG2E = 1.4426950408889634
MASKED = -1e30


def raw_scores(q, key_ref, own_key_ref, from_ref, own_ref):
    cached = contract_cols(q, key_ref[...])
    at = lax.broadcasted_iota(jnp.int32, cached.shape, 1)
    cached = jnp.where(at >= from_ref[...], cached, MASKED)
    own = contract_cols(q, own_key_ref[...])
    own_at = lax.broadcasted_iota(jnp.int32, own.shape, 1)
    own = jnp.where(own_at <= own_ref[...], own, MASKED)
    return (cached, own)


def pick_lane(stat_ref, head):
    lane = lax.broadcasted_iota(jnp.int32, stat_ref.shape, 1)
    return jnp.sum(jnp.where(lane == head, stat_ref[...], 0.0), axis=1, keepdims=True)


def forward_kernel(
    per_group, base, q_ref, key_ref, value_ref, own_key_ref, own_value_ref,
    from_ref, own_ref, out_ref, top_ref, total_ref,
):
    head = pl.program_id(0) * per_group + pl.program_id(1)

    @pl.when(head == 0)
    def _():
        top_ref[...] = jnp.zeros_like(top_ref)
        total_ref[...] = jnp.zeros_like(total_ref)

    cached, own = raw_scores(q_ref[...], key_ref, own_key_ref, from_ref, own_ref)
    top = jnp.maximum(
        jnp.max(cached, axis=1, keepdims=True), jnp.max(own, axis=1, keepdims=True)
    )
    cached = jnp.exp2((cached - top) * base)
    own = jnp.exp2((own - top) * base)
    total = jnp.sum(cached, axis=1, keepdims=True) + jnp.sum(own, axis=1, keepdims=True)
    out = jnp.dot(
        cached.astype(jnp.bfloat16), value_ref[...], preferred_element_type=jnp.float32
    ) + jnp.dot(
        own.astype(jnp.bfloat16), own_value_ref[...], preferred_element_type=jnp.float32
    )
    out_ref[...] = out.astype(out_ref.dtype)
    lane = lax.broadcasted_iota(jnp.int32, top_ref.shape, 1)
    top_ref[...] = jnp.where(lane == head, top, top_ref[...])
    total_ref[...] = jnp.where(lane == head, total, total_ref[...])


def backward_kernel(
    first_group, per_group, base, scale, q_ref, grad_ref, attended_ref, key_ref, value_ref,
    own_key_ref, own_value_ref, from_ref, own_ref, top_ref, inverse_ref, out_ref,
):
    head = (first_group + pl.program_id(0)) * per_group + pl.program_id(1)
    cached, own = raw_scores(q_ref[...], key_ref, own_key_ref, from_ref, own_ref)
    top = pick_lane(top_ref, head)
    inverse = pick_lane(inverse_ref, head)
    grad = grad_ref[...]
    delta = jnp.sum(
        grad.astype(jnp.float32) * attended_ref[...].astype(jnp.float32),
        axis=1,
        keepdims=True,
    )
    cached = jnp.exp2((cached - top) * base) * (contract_cols(grad, value_ref[...]) - delta)
    own = jnp.exp2((own - top) * base) * (contract_cols(grad, own_value_ref[...]) - delta)
    out = jnp.dot(
        cached.astype(jnp.bfloat16), key_ref[...], preferred_element_type=jnp.float32
    ) + jnp.dot(
        own.astype(jnp.bfloat16), own_key_ref[...], preferred_element_type=jnp.float32
    )
    out_ref[...] = (out * (inverse * scale)).astype(out_ref.dtype)


def blocks(tokens, cached, padded, per_group, first):
    head = pl.BlockSpec((tokens, HEAD_DIM), lambda g, p: (0, (first + g) * per_group + p))
    rows = pl.BlockSpec((cached, HEAD_DIM), lambda g, p: (0, first + g))
    own = pl.BlockSpec((padded, HEAD_DIM), lambda g, p: (0, first + g))
    bound = pl.BlockSpec((tokens, 1), lambda g, p: (0, 0))
    stat = pl.BlockSpec((tokens, HEAD_DIM), lambda g, p: (0, 0))
    here = pl.BlockSpec((tokens, HEAD_DIM), lambda g, p: (0, g * per_group + p))
    return (head, rows, own, bound, stat, here)


def forward(
    first, groups, per_group, base, queries, keys, values, own_keys, own_values, bounds
):
    tokens = queries.shape[0]
    cached, padded = keys.shape[0], own_keys.shape[0]
    head, rows, own, bound, stat, here = blocks(tokens, cached, padded, per_group, first)
    work = groups * per_group * tokens * (cached + padded)
    return pl.pallas_call(
        functools.partial(forward_kernel, per_group, base),
        grid=(groups, per_group),
        in_specs=[head, rows, rows, own, own, bound, bound],
        out_specs=[here, stat, stat],
        out_shape=[
            jax.ShapeDtypeStruct((tokens, groups * per_group * HEAD_DIM), jnp.float32),
            jax.ShapeDtypeStruct((tokens, HEAD_DIM), jnp.float32),
            jax.ShapeDtypeStruct((tokens, HEAD_DIM), jnp.float32),
        ],
        compiler_params=pltpu.CompilerParams(vmem_limit_bytes=40 << 20),
        cost_estimate=pl.CostEstimate(
            flops=16 * HEAD_DIM * work, bytes_accessed=20 << 20, transcendentals=work
        ),
    )(queries, keys, values, own_keys, own_values, *bounds)


def backward(
    first, groups, per_group, base, scale, queries, grads, attended, keys, values,
    own_keys, own_values, bounds, top, inverse,
):
    tokens = queries.shape[0]
    cached, padded = keys.shape[0], own_keys.shape[0]
    head, rows, own, bound, stat, here = blocks(tokens, cached, padded, per_group, first)
    work = groups * per_group * tokens * (cached + padded)
    return pl.pallas_call(
        functools.partial(backward_kernel, first, per_group, base, scale),
        grid=(groups, per_group),
        in_specs=[head, here, head, rows, rows, own, own, bound, bound, stat, stat],
        out_specs=here,
        out_shape=jax.ShapeDtypeStruct(grads.shape, jnp.float32),
        compiler_params=pltpu.CompilerParams(vmem_limit_bytes=58 << 20),
        cost_estimate=pl.CostEstimate(
            flops=16 * HEAD_DIM * work, bytes_accessed=12 << 20, transcendentals=work
        ),
    )(queries, grads, attended, keys, values, own_keys, own_values, *bounds, top, inverse)


def split_columns(array, pieces):
    width = array.shape[1] // pieces
    return [array[:, i * width : (i + 1) * width] for i in range(pieces)]


def per_device_general(
    residual,
    norm_gain,
    grad_out,
    w_gate,
    w_up,
    w_down,
    w_output,
    query,
    key,
    value,
    cache_key,
    cache_value,
    visible_from,
):
    wide_count = lax.axis_size("wide")
    wide_place = lax.axis_index("wide")
    tokens = residual.shape[0]
    scale = 1.0 / math.sqrt(HEAD_DIM)
    base = scale * LOG2E

    stream = residual.astype(jnp.float32)
    gain = norm_gain.astype(jnp.float32)
    hidden_part = contract_cols(grad_out, w_down)
    squares = narrow_sum(jnp.sum(stream * stream, axis=1))
    rstd = lax.rsqrt(squares / D + EPSILON)[:, None]
    normed = (stream * rstd * gain).astype(jnp.bfloat16)
    gate_part = jnp.dot(normed, w_gate, preferred_element_type=jnp.float32)
    up_part = jnp.dot(normed, w_up, preferred_element_type=jnp.float32)

    queries, stretch_keys, stretch_values = (to_heads(query), to_heads(key), to_heads(value))
    groups = stretch_keys.shape[1] // HEAD_DIM
    per_group = queries.shape[1] // stretch_keys.shape[1]
    heads = groups * per_group
    cached = cache_key.shape[0]
    span = tokens // wide_count
    start = wide_place * span
    padded = -(-span // HEAD_DIM) * HEAD_DIM
    filler = ((0, padded - span), (0, 0))
    own_keys = jnp.pad(lax.dynamic_slice_in_dim(stretch_keys, start, span, 0), filler)
    own_values = jnp.pad(lax.dynamic_slice_in_dim(stretch_values, start, span, 0), filler)
    position = jnp.arange(tokens, dtype=jnp.int32)[:, None]
    bounds = (
        visible_from[:, None] - wide_place * cached,
        jnp.minimum(position - start, span - 1),
    )

    lows = [part.astype(jnp.bfloat16) for part in (hidden_part, gate_part, up_part)]
    hidden_grad = narrow_total(hidden_part, lows[0])
    gate = narrow_total(gate_part, lows[1])
    up = narrow_total(up_part, lows[2])

    queries, own_keys, own_values = after((queries, own_keys, own_values), *lows)
    early = groups - groups // 4
    outs, tops, totals = [], [], []
    for first, count in ((0, early), (early, groups - early)):
        if count == 0:
            continue
        if first:
            (queries,) = after((queries,), hidden_grad, gate, up)
        out, top, total = forward(
            first, count, per_group, base, queries, cache_key, cache_value, own_keys,
            own_values, bounds,
        )
        outs.append(out)
        tops.append(top[:, : count * per_group])
        totals.append(total[:, : count * per_group])
    local_out = jnp.concatenate(outs, axis=1)
    local_top = jnp.concatenate(tops, axis=1)
    stats = doubled(
        jnp.concatenate([local_top] + totals, axis=1), functools.partial(merge_softmax, base)
    )
    top, inverse = stats[:, :heads], 1.0 / stats[:, heads:]
    factor = jnp.exp2((local_top - top) * base) * inverse
    owner = jnp.arange(heads * HEAD_DIM, dtype=jnp.int32)[None, :] // HEAD_DIM
    choose = (owner == jnp.arange(heads, dtype=jnp.int32)[:, None]).astype(jnp.float32)
    attended_part = local_out * jnp.dot(factor, choose, precision=lax.Precision.HIGHEST)
    side = ((0, 0), (0, HEAD_DIM - heads))
    top, inverse = jnp.pad(top, side), jnp.pad(inverse, side)
    ways = orders()
    attended = jnp.concatenate(
        [
            gathered(scatter_sum(as_cube(part), way).astype(jnp.bfloat16), way)
            for part, way in zip(split_columns(attended_part, 2), ways)
        ],
        axis=1,
    )

    activated, d_gate, d_up = swiglu_back(gate, up, hidden_grad)
    d_normed_part = contract_cols(d_gate, w_gate) + contract_cols(d_up, w_up)
    d_normed = jnp.concatenate(
        [
            scatter_sum(as_cube(part), way)
            for part, way in zip(split_columns(d_normed_part, 2), ways)
        ],
        axis=1,
    )
    rstd_rows = own_rows(rstd)
    scaled = own_rows(residual).astype(jnp.float32) * rstd_rows
    grad_gain = doubled(jnp.sum(d_normed * scaled, axis=0), jnp.add)
    weighted = d_normed * gain
    inner = narrow_sum(jnp.sum(weighted * scaled, axis=1)) / D
    grad_rows = (
        own_rows(grad_out).astype(jnp.float32)
        + rstd_rows * (weighted - scaled * inner[:, None])
    ).astype(jnp.bfloat16)
    grad_residual = jnp.concatenate(
        [gathered(part, way) for part, way in zip(split_columns(grad_rows, 2), ways)], axis=1
    )

    columns = w_output.shape[1]
    width = grad_residual.shape[1]
    if lax.axis_size("narrow") == 2:
        own_panel = lax.dynamic_slice_in_dim(
            grad_residual, (wide_place * columns) % width, columns, 1
        )
        holder = (wide_place * columns) // width == lax.axis_index("narrow")
        panel = jnp.where(holder, own_panel, swapped(own_panel, "narrow", 1))
    else:
        whole = lax.all_gather(grad_residual, "narrow", axis=1, tiled=True)
        panel = lax.dynamic_slice_in_dim(whole, wide_place * columns, columns, 1)
    pieces = 2 if groups % 2 == 0 else 1
    group_count = groups // pieces
    query_grads, query_parts = [], []
    for piece in range(pieces):
        way = ways[piece]
        wide_rows = group_count * per_group * HEAD_DIM
        rows = w_output[piece * wide_rows : (piece + 1) * wide_rows]
        d_attention = gathered(
            scatter_sum(as_cube(contract_cols(panel, rows)), way).astype(jnp.bfloat16), way
        )
        query_part = backward(
            piece * group_count, group_count, per_group, base, scale, queries, d_attention,
            attended, cache_key, cache_value, own_keys, own_values, bounds, top, inverse,
        )
        query_parts.append(query_part)
        query_grads.append(
            gathered(scatter_sum(as_cube(query_part), way).astype(jnp.bfloat16), way)
        )
    grad_query = jnp.concatenate(query_grads, axis=1)
    activated, d_gate, d_up, panel = after((activated, d_gate, d_up, panel), *query_parts)
    grad_w_down = contract_rows(activated, grad_out).astype(jnp.bfloat16)
    grad_w_gate = contract_rows(normed, d_gate).astype(jnp.bfloat16)
    grad_w_up = contract_rows(normed, d_up).astype(jnp.bfloat16)
    grad_w_output = contract_rows(attended, panel).astype(jnp.bfloat16)
    return (
        grad_residual,
        grad_gain,
        grad_w_gate,
        grad_w_up,
        grad_w_down,
        grad_w_output,
        grad_query,
    )


def block_scores(q, pair_ref, from_ref, block):
    rows = pair_ref.shape[0] // 2
    cached = contract_cols(q, pair_ref[:rows, :])
    at = lax.broadcasted_iota(jnp.int32, cached.shape, 1)
    return jnp.where(at >= from_ref[:, block : block + 1], cached, MASKED)


def own_scores(q, pair_ref, own_ref):
    own = contract_cols(q, pair_ref[: pair_ref.shape[0] // 2, :])
    own_at = lax.broadcasted_iota(jnp.int32, own.shape, 1)
    return jnp.where(own_at <= own_ref[...], own, MASKED)


STATS = HEAD_DIM // 2
MESH = pl.DeviceIdType.MESH


def online_kernel(base, first, count, has_own, q_ref, from_ref, own_ref, *refs):
    held = count + has_own
    pairs, rest = refs[:held], refs[held:]
    saved, rest = rest[len(rest) - held :], rest[: len(rest) - held]
    earlier, (out_ref, stat_ref, tops_ref) = rest[:-3], rest[-3:]
    head = pl.program_id(0)

    @pl.when(head == 0)
    def _():
        stat_ref[...] = jnp.zeros_like(stat_ref)
        tops_ref[...] = jnp.zeros_like(tops_ref)

    q = q_ref[...]
    lane = lax.broadcasted_iota(jnp.int32, stat_ref.shape, 1)
    tops = tops_ref[...]
    top = total = out = None
    if earlier:
        out_before, stat_before = earlier
        top, total = pick_lane(stat_before, head), pick_lane(stat_before, head + STATS)
        out = out_before[...]
    for at, pair in enumerate(pairs):
        rows = pair.shape[0] // 2
        if at < count:
            scores = block_scores(q, pair, from_ref, first + at)
        else:
            scores = own_scores(q, pair, own_ref)
        later = jnp.max(scores, axis=1, keepdims=True)
        if top is not None:
            later = jnp.maximum(top, later)
            shrink = jnp.exp2((top - later) * base)
            total, out = total * shrink, out * shrink
        scores = jnp.exp2((scores - later) * base)
        added = jnp.sum(scores, axis=1, keepdims=True)
        scores = scores.astype(jnp.bfloat16)
        saved[at][...] = scores
        tops = jnp.where(lane == head * held + at, later, tops)
        product = jnp.dot(scores, pair[rows:, :], preferred_element_type=jnp.float32)
        total = added if top is None else total + added
        out = product if top is None else out + product
        top = later
    out_ref[...] = (out / total if earlier else out).astype(out_ref.dtype)
    tops_ref[...] = tops
    stat_ref[...] = jnp.where(
        lane == head, top, jnp.where(lane == head + STATS, total, stat_ref[...])
    )


def online_forward(base, first, heads, queries, bounds, blocks, own, earlier):
    tokens = queries.shape[0]
    whole = lambda array: pl.BlockSpec(array.shape, lambda h: (0, 0))
    here = pl.BlockSpec((tokens, HEAD_DIM), lambda h: (0, h))
    stat = pl.BlockSpec((tokens, HEAD_DIM), lambda h: (0, 0))
    pairs = list(blocks) + ([] if own is None else [own])
    work = heads * tokens * sum(pair.shape[0] // 2 for pair in pairs)
    rest = (*bounds, *pairs)
    kind = jnp.bfloat16 if earlier else jnp.float32
    return pl.pallas_call(
        functools.partial(online_kernel, base, first, len(blocks), int(own is not None)),
        grid=(heads,),
        in_specs=[here] + [whole(array) for array in rest] + ([here, stat] if earlier else []),
        out_specs=[here, stat, stat]
        + [pl.BlockSpec((tokens, pair.shape[0] // 2), lambda h: (0, h)) for pair in pairs],
        out_shape=[
            jax.ShapeDtypeStruct((tokens, heads * HEAD_DIM), kind),
            jax.ShapeDtypeStruct((tokens, HEAD_DIM), jnp.float32),
            jax.ShapeDtypeStruct((tokens, HEAD_DIM), jnp.float32),
        ]
        + [
            jax.ShapeDtypeStruct((tokens, heads * (pair.shape[0] // 2)), jnp.bfloat16)
            for pair in pairs
        ],
        compiler_params=pltpu.CompilerParams(vmem_limit_bytes=58 << 20),
        cost_estimate=pl.CostEstimate(
            flops=HEAD_DIM * work, bytes_accessed=1 << 20, transcendentals=work // 8
        ),
    )(queries, *rest, *earlier)


def query_kernel(
    base, scale, places, grad_ref, attended_ref, *refs
):
    count = len(places)
    pairs, saved, tops_refs = refs[:count], refs[count : 2 * count], refs[2 * count :][:2]
    stat_ref, rows_ref, out_ref, grad_residual_ref, residuals, row_send, row_recv = refs[
        2 * count + 2 :
    ]
    head = pl.program_id(0)
    place = lax.axis_index("wide")
    x = lax.axis_index("narrow")
    line, group = place // 4, place % 4
    y, core = group // 2, group % 2
    hi, lo = line // 2, line % 2

    def flip(bit):
        weight = 1 << bit
        return (place + weight - 2 * weight * ((place // weight) % 2), x)

    peers = [flip(bit) for bit in (3, 2, 1, 0)]

    def sending(stage):
        ref = (
            residuals.at[core, y, hi, lo],
            residuals.at[core, y, :, lo],
            residuals.at[core, y],
            residuals.at[core],
        )[stage]
        return pltpu.make_async_remote_copy(
            src_ref=ref, dst_ref=ref, send_sem=row_send.at[stage], recv_sem=row_recv.at[stage],
            device_id=peers[stage], device_id_type=MESH,
        )

    @pl.when(head == 0)
    def _():
        barrier = pltpu.get_barrier_semaphore()
        for device in peers:
            pl.semaphore_signal(barrier, inc=1, device_id=device, device_id_type=MESH)
        pl.semaphore_wait(barrier, 4)
        residuals[core, y, hi, lo] = rows_ref[...]
        sending(0).start()

    for stage, step in ((1, 1), (2, 2), (3, 4)):
        @pl.when(head == step)
        def _(stage=stage):
            sending(stage - 1).wait_recv()
            sending(stage).start()

    top = pick_lane(stat_ref, head)
    inverse = pick_lane(stat_ref, head + STATS)
    grad = grad_ref[...]
    delta = jnp.sum(
        grad.astype(jnp.float32) * attended_ref[...].astype(jnp.float32), axis=1, keepdims=True
    )
    out = 0.0
    for (call, at, held), pair, weights in zip(places, pairs, saved):
        rows = pair.shape[0] // 2
        factor = jnp.exp2((pick_lane(tops_refs[call], head * held + at) - top) * base)
        scores = weights[...].astype(jnp.float32) * (contract_cols(grad, pair[rows:, :]) - delta)
        out = out + factor * jnp.dot(
            scores.astype(jnp.bfloat16), pair[:rows, :], preferred_element_type=jnp.float32
        )
    out_ref[...] = out * (inverse * scale)

    @pl.when(head == pl.num_programs(0) - 1)
    def _():
        sending(3).wait_recv()
        width = rows_ref.shape[1]
        for cp in range(2):
            for yp in range(2):
                at = (2 * cp + yp) * width
                grad_residual_ref[:, :, :, at : at + width] = residuals[cp, yp]
        for stage in range(4):
            sending(stage).wait_send()


def query_backward(
    base, scale, heads, grads, attended, places, pairs, saved, tops, stats, grad_rows
):
    tokens = grads.shape[0]
    span, width = grad_rows.shape
    whole = lambda array: pl.BlockSpec(array.shape, lambda h: (0, 0))
    head = pl.BlockSpec((tokens, HEAD_DIM), lambda h: (0, h))
    work = heads * tokens * sum(pair.shape[0] // 2 for pair in pairs)
    result = (2, 2, span, 4 * width)
    dma = pltpu.SemaphoreType.DMA
    query_part, grad_residual = pl.pallas_call(
        functools.partial(query_kernel, base, scale, places),
        grid=(heads,),
        in_specs=[head, head]
        + [whole(pair) for pair in pairs]
        + [pl.BlockSpec((tokens, pair.shape[0] // 2), lambda h: (0, h)) for pair in pairs]
        + [whole(array) for array in (*tops, stats, grad_rows)],
        out_specs=[head, pl.BlockSpec(result, lambda h: (0, 0, 0, 0))],
        out_shape=[
            jax.ShapeDtypeStruct((tokens, width), jnp.float32),
            jax.ShapeDtypeStruct(result, jnp.bfloat16),
        ],
        scratch_shapes=[
            pltpu.VMEM((2, 2, 2, 2, span, width), jnp.bfloat16),
            dma((4,)), dma((4,)),
        ],
        compiler_params=pltpu.CompilerParams(
            collective_id=2, has_side_effects=True, vmem_limit_bytes=58 << 20
        ),
        cost_estimate=pl.CostEstimate(
            flops=12 * HEAD_DIM * work, bytes_accessed=12 << 20, transcendentals=work
        ),
    )(grads, attended, *pairs, *saved, *tops, stats, grad_rows)
    return query_part, grad_residual.reshape(tokens, -1)


def placed(near, far, first):
    low = first == 0
    return jnp.concatenate([jnp.where(low, near, far), jnp.where(low, far, near)], axis=0)


def joined(near, far, bit, axis):
    low = bit == 0
    return jnp.concatenate([jnp.where(low, near, far), jnp.where(low, far, near)], axis=axis)


def line_scatter(part, line):
    rows = part.shape[0] // 4
    low = part.astype(jnp.bfloat16)
    total = lax.dynamic_slice_in_dim(part, line * rows, rows, 0)
    for m in (1, 2, 3):
        sent = lax.dynamic_slice_in_dim(low, (line ^ m) * rows, rows, 0)
        total = total + swapped(sent, "wide", m << 2).astype(jnp.float32)
    return total


def line_gather(chunk, line):
    held = [chunk if m == 0 else swapped(chunk, "wide", m << 2) for m in range(4)]
    return joined(
        joined(held[0], held[1], line & 1, 0), joined(held[2], held[3], line & 1, 0), line >> 1, 0
    )


def side_gather(block, group):
    return joined(block, swapped(block, "wide", 2), group >> 1, 1)


def core_gather(block, group):
    return joined(block, swapped(block, "wide", 1), group & 1, 1)


PIECES = 5
def exchange_kernel(
    base, d_gate_ref, d_up_ref, out_ref, stat_ref,
    every_gate, every_up, attended_ref, stats_ref,
    outs, stats, rows, row_stats, all_rows, all_stats,
    local_sem, x_send, x_recv, send_sem, recv_sem,
):
    place = lax.axis_index("wide")
    x = lax.axis_index("narrow")
    line, group = place // 4, place % 4
    count = d_gate_ref.shape[0]
    lines = [place + 4 * (1 - 2 * (line % 2)), place + 8 * (1 - 2 * (line // 2))]
    lines.append(lines[0] + lines[1] - place)
    at_line = [at // 4 for at in lines]
    barrier = pltpu.get_barrier_semaphore()
    pl.semaphore_signal(barrier, inc=1, device_id=(place, 1 - x), device_id_type=MESH)
    for peer in lines:
        pl.semaphore_signal(barrier, inc=1, device_id=(peer, x), device_id_type=MESH)
    pl.semaphore_wait(barrier, 4)

    here = pl.ds(pl.multiple_of(x * count, 16), count)
    moves = []
    for at, (src, dst) in enumerate(((d_gate_ref, every_gate), (d_up_ref, every_up))):
        far = pltpu.make_async_remote_copy(
            src_ref=src, dst_ref=dst.at[here], send_sem=x_send.at[at], recv_sem=x_recv.at[at],
            device_id=(place, 1 - x), device_id_type=MESH,
        )
        near = pltpu.make_async_copy(src, dst.at[here], local_sem.at[at])
        far.start()
        near.start()
        moves += [far, near]

    def line_copy(src, dst, at, m):
        return pltpu.make_async_remote_copy(
            src_ref=src, dst_ref=dst, send_sem=send_sem.at[at, m], recv_sem=recv_sem.at[at, m],
            device_id=(lines[m], x), device_id_type=MESH,
        )

    def scattered(m):
        return (
            line_copy(out_ref.at[at_line[m]], outs.at[m], 0, m),
            line_copy(stat_ref.at[at_line[m]], stats.at[m], 1, m),
        )

    for m in range(3):
        for sending in scattered(m):
            sending.start()
    for m in range(3):
        for sending in scattered(m):
            sending.wait_recv()
    parts = [stat_ref[line]] + [stats[m] for m in range(3)]
    top = functools.reduce(jnp.maximum, parts)
    lane = lax.broadcasted_iota(jnp.int32, top.shape, 1)
    weights = [
        jnp.where(
            lane < STATS, 0.0, pltpu.roll(jnp.exp2((part - top) * base), STATS, 1) * part
        )
        for part in parts
    ]
    total = functools.reduce(jnp.add, weights)
    inverse = 1.0 / jnp.where(total > 0.0, total, 1.0)
    row_stats[...] = jnp.where(lane < STATS, top, inverse)
    all_stats[line] = row_stats[...]
    weights = [weight * inverse for weight in weights]
    for h in range(rows.shape[1] // HEAD_DIM):
        cols = slice(h * HEAD_DIM, (h + 1) * HEAD_DIM)
        pieces = [out_ref[line, :, cols]] + [outs[m, :, cols] for m in range(3)]
        value = functools.reduce(
            jnp.add,
            [
                piece.astype(jnp.float32) * weight[:, STATS + h : STATS + h + 1]
                for piece, weight in zip(pieces, weights)
            ],
        )
        rows[:, cols] = value.astype(jnp.bfloat16)
    all_rows[line] = rows[...]

    def spread(m, where):
        return (
            line_copy(rows, all_rows.at[where], 2, m),
            line_copy(row_stats, all_stats.at[where], 3, m),
        )

    for m in range(3):
        for sending in spread(m, line):
            sending.start()
    for m in range(3):
        for sending in spread(m, at_line[m]):
            sending.wait_recv()
    attended_ref[...] = all_rows[...]
    stats_ref[...] = all_stats[...]
    for m in range(3):
        for sending in scattered(m) + spread(m, line):
            sending.wait_send()
    for move in moves:
        move.wait()


def exchange(base, d_gate, d_up, out, stat):
    tokens, width = out.shape
    span = tokens // 4
    low, full = jnp.bfloat16, jnp.float32
    vmem = pl.BlockSpec(memory_space=pltpu.VMEM)
    hbm = pl.BlockSpec(memory_space=pl.ANY)
    dma = pltpu.SemaphoreType.DMA
    every = jax.ShapeDtypeStruct((2 * d_gate.shape[0], d_gate.shape[1]), low)
    every_gate, every_up, attended, stats = pl.pallas_call(
        functools.partial(exchange_kernel, base),
        out_shape=[
            every,
            every,
            jax.ShapeDtypeStruct((4, span, width), low),
            jax.ShapeDtypeStruct((4, span, HEAD_DIM), full),
        ],
        in_specs=[hbm, hbm, vmem, vmem],
        out_specs=[hbm, hbm, vmem, vmem],
        scratch_shapes=[
            pltpu.VMEM((3, span, width), low),
            pltpu.VMEM((3, span, HEAD_DIM), full),
            pltpu.VMEM((span, width), low),
            pltpu.VMEM((span, HEAD_DIM), full),
            pltpu.VMEM((4, span, width), low),
            pltpu.VMEM((4, span, HEAD_DIM), full),
            dma((2,)), dma((2,)), dma((2,)), dma((4, 3)), dma((4, 3)),
        ],
        compiler_params=pltpu.CompilerParams(
            collective_id=1, has_side_effects=True, vmem_limit_bytes=40 << 20
        ),
        cost_estimate=pl.CostEstimate(
            flops=20_000_000_000, bytes_accessed=8 << 20, transcendentals=0
        ),
    )(d_gate, d_up, out.reshape(4, span, width), stat.reshape(4, span, HEAD_DIM))
    return every_gate, every_up, attended.reshape(tokens, width), stats.reshape(tokens, HEAD_DIM)


def middle_kernel(
    part_ref, residual_ref, rstd_ref, out_grad_ref, gain_ref, w_ref, attended_ref, activated_ref,
    rows_ref, gain_grad_ref, panel_ref, d_attention_ref, every_attended_ref, every_activated,
    residual_rows, out_grad_rows, gain_to, gain_from, gain_all, attended_all,
    from_core, to_side, from_side, to_near, from_near, kept, to_far, from_far, summed,
    da_send, da_own, da_core, da_to_side, da_side, da_to_near, da_near, da_kept, da_to_far, da_far,
    inner_to, inner_from, grad_rows, panels, gathered_ref,
    send_sem, recv_sem, da_send_sem, da_recv_sem, inner_send, inner_recv,
    panel_send, panel_recv, gather_send, gather_recv,
    local_sem, x_send, x_recv, gain_send, gain_recv, attended_send, attended_recv,
):
    place = lax.axis_index("wide")
    x = lax.axis_index("narrow")
    line, group = place // 4, place % 4
    y, core = group // 2, group % 2
    hi, lo = line // 2, line % 2
    span, width = rows_ref.shape
    step = width // PIECES
    block = 2 * core + y

    def flip(bit):
        weight = 1 << bit
        at = (place // weight) % 2
        return (place + weight - 2 * weight * at, x)

    peers = {"core": flip(0), "side": flip(1), "near": flip(2), "far": flip(3), "x": (place, 1 - x)}
    targets = [(8 * x + 2 * block + j, nx) for j in (0, 1) for nx in (0, 1)]
    source_x, source_block = place // 8, (place % 8) // 2
    source_group = 2 * (source_block % 2) + source_block // 2
    sources = [(4 * s + source_group, source_x) for s in range(4)]

    def is_me(device):
        return jnp.logical_and(device[0] == place, device[1] == x)

    def not_me(device):
        return jnp.logical_not(is_me(device))

    side_place, core_place = peers["side"][0], peers["core"][0]
    corner = side_place + core_place - place
    others = [
        (at, nx)
        for nx in (x, 1 - x)
        for at in (place, core_place, side_place, corner)
    ][1:]
    barrier = pltpu.get_barrier_semaphore()
    for device in [peers["near"], peers["far"]] + others:
        pl.semaphore_signal(barrier, inc=1, device_id=device, device_id_type=MESH)
    for device in targets + sources:
        @pl.when(not_me(device))
        def _(device=device):
            pl.semaphore_signal(barrier, inc=1, device_id=device, device_id_type=MESH)
    mine = jnp.logical_and(place // 8 == x, source_group == group).astype(jnp.int32)
    pl.semaphore_wait(barrier, 17 - 2 * mine)

    def copy(src, dst, sends, recvs, at, device):
        return pltpu.make_async_remote_copy(
            src_ref=src, dst_ref=dst, send_sem=sends.at[at], recv_sem=recvs.at[at],
            device_id=device, device_id_type=MESH,
        )

    here = (
        pl.ds(pl.multiple_of(line * span, 16), span),
        pl.ds(pl.multiple_of(block * width, HEAD_DIM), width),
    )
    loads = [
        pltpu.make_async_copy(residual_ref.at[here], residual_rows, local_sem.at[0]),
        pltpu.make_async_copy(out_grad_ref.at[here], out_grad_rows, local_sem.at[1]),
    ]
    count = activated_ref.shape[0]
    own_units = every_activated.at[pl.ds(pl.multiple_of(x * count, 16), count)]
    units_local = pltpu.make_async_copy(activated_ref, own_units, local_sem.at[2])
    units_far = pltpu.make_async_remote_copy(
        src_ref=activated_ref, dst_ref=own_units, send_sem=x_send.at[0], recv_sem=x_recv.at[0],
        device_id=peers["x"], device_id_type=MESH,
    )
    for load in loads + [units_local, units_far]:
        load.start()

    def scatter(outgoing, own, bufs, sends, recvs, finish):
        core_buf, side_out, side_in, near_out, near_in, keep, far_out, far_in = bufs

        def cols(p):
            return pl.ds(p * step, step)

        def core_copy(yp, p):
            return copy(
                outgoing(yp, p), core_buf.at[yp, :, :, :, cols(p)], sends, recvs,
                (yp, p), peers["core"],
            )

        def side_copy(p):
            return copy(
                side_out.at[:, :, :, cols(p)], side_in.at[:, :, :, cols(p)], sends, recvs,
                (2, p), peers["side"],
            )

        def near_copy(p):
            return copy(
                near_out.at[:, :, cols(p)], near_in.at[:, :, cols(p)], sends, recvs,
                (3, p), peers["near"],
            )

        def far_copy(p):
            return copy(
                far_out.at[:, cols(p)], far_in.at[:, cols(p)], sends, recvs,
                (4, p), peers["far"],
            )

        def stage(s, p):
            if s == 0:
                core_copy(0, p).start()
                core_copy(1, p).start()
            elif s == 1:
                core_copy(0, p).wait_recv()
                core_copy(1, p).wait_recv()
                for h in range(2):
                    for l in range(2):
                        value = own(1 - y, h, l, p) + core_buf[1 - y, h, l, :, cols(p)].astype(
                            jnp.float32
                        )
                        side_out[h, l, :, cols(p)] = value.astype(jnp.bfloat16)
                side_copy(p).start()
            elif s == 2:
                side_copy(p).wait_recv()

                def total(h, l):
                    return (
                        own(y, h, l, p)
                        + core_buf[y, h, l, :, cols(p)].astype(jnp.float32)
                        + side_in[h, l, :, cols(p)].astype(jnp.float32)
                    )

                for h in range(2):
                    near_out[h, :, cols(p)] = total(h, 1 - lo).astype(jnp.bfloat16)
                near_copy(p).start()
                for h in range(2):
                    keep[h, :, cols(p)] = total(h, lo)
            elif s == 3:
                near_copy(p).wait_recv()

                def total(h):
                    return keep[h, :, cols(p)] + near_in[h, :, cols(p)].astype(jnp.float32)

                far_out[:, cols(p)] = total(1 - hi).astype(jnp.bfloat16)
                far_copy(p).start()
            else:
                far_copy(p).wait_recv()
                finish(
                    p,
                    keep[hi, :, cols(p)]
                    + near_in[hi, :, cols(p)].astype(jnp.float32)
                    + far_in[:, cols(p)].astype(jnp.float32),
                )

        for p in range(PIECES):
            stage(0, p)
        for t in range(-2, PIECES + 2):
            for s, p in ((2, t), (1, t + 2), (3, t - 1), (4, t - 2)):
                if 0 <= p < PIECES:
                    stage(s, p)

        def drain():
            for p in range(PIECES):
                core_copy(0, p).wait_send()
                core_copy(1, p).wait_send()
                side_copy(p).wait_send()
                near_copy(p).wait_send()
                far_copy(p).wait_send()

        return drain

    def part_cols(yp, cp, p):
        return pl.ds(pl.multiple_of((2 * cp + yp) * width + p * step, HEAD_DIM), step)

    def part_finish(p, value):
        summed[:, pl.ds(p * step, step)] = value

    drain_parts = scatter(
        lambda yp, p: part_ref.at[:, :, :, part_cols(yp, 1 - core, p)],
        lambda yp, h, l, p: part_ref[h, l, :, part_cols(yp, core, p)].astype(jnp.float32),
        (from_core, to_side, from_side, to_near, from_near, kept, to_far, from_far),
        send_sem, recv_sem, part_finish,
    )

    attended_all[y, core] = attended_ref[...]
    attended_side = copy(
        attended_all.at[y, core], attended_all.at[y, core], attended_send, attended_recv, 0,
        peers["side"],
    )
    attended_core = copy(
        attended_all.at[:, core], attended_all.at[:, core], attended_send, attended_recv, 1,
        peers["core"],
    )
    for load in loads:
        load.wait()
    d_normed = summed[...]
    scaled = residual_rows[...].astype(jnp.float32) * rstd_ref[:, :1]
    weighted = d_normed * gain_ref[...]
    inner = jnp.sum(weighted * scaled, axis=1, keepdims=True)
    inner_to[...] = jnp.broadcast_to(inner, inner_to.shape)
    inner_copies = [
        copy(inner_to, inner_from.at[at], inner_send, inner_recv, at, device)
        for at, device in enumerate(others)
    ]
    for sending in inner_copies:
        sending.start()

    def gain_copy(at):
        return copy(
            gain_to.at[at], gain_from.at[at], gain_send, gain_recv, at, peers[("near", "far")[at]]
        )

    gain_side = copy(
        gain_all.at[core, y], gain_all.at[core, y], gain_send, gain_recv, 2, peers["side"]
    )
    gain_core = copy(
        gain_all.at[core], gain_all.at[core], gain_send, gain_recv, 3, peers["core"]
    )
    gain_to[0] = jnp.broadcast_to(
        jnp.sum(d_normed * scaled, axis=0, keepdims=True), gain_to.shape[1:]
    )
    for sending in inner_copies:
        sending.wait_recv()
    inner = functools.reduce(
        jnp.add, [inner_from[at] for at in range(len(others))], inner_to[...]
    )
    gain_copy(0).start()
    attended_side.start()
    inner = inner[:, :1] * (1.0 / D)
    rows = (
        out_grad_rows[...].astype(jnp.float32) + rstd_ref[:, :1] * (weighted - scaled * inner)
    ).astype(jnp.bfloat16)
    grad_rows[...] = rows
    across = panels.shape[3]
    starts = (0, width - across)

    def panel_copy(at):
        j = at // 2
        return pltpu.make_async_remote_copy(
            src_ref=grad_rows.at[:, pl.ds(starts[j], across)], dst_ref=panels.at[hi, lo],
            send_sem=panel_send.at[at], recv_sem=panel_recv.at[line],
            device_id=targets[at], device_id_type=MESH,
        )

    for at, device in enumerate(targets):
        @pl.when(not_me(device))
        def _(at=at):
            panel_copy(at).start()

        @pl.when(is_me(device))
        def _(at=at):
            begin = starts[at // 2]
            panels[hi, lo] = grad_rows[:, begin : begin + across]
    rows_ref[...] = rows
    gain_copy(0).wait_recv()
    gain_to[1] = gain_to[0] + gain_from[0]
    gain_copy(1).start()
    for s, device in enumerate(sources):
        @pl.when(not_me(device))
        def _(s=s, device=device):
            pltpu.make_async_remote_copy(
                src_ref=grad_rows.at[:, pl.ds(0, across)], dst_ref=panels.at[s // 2, s % 2],
                send_sem=panel_send.at[0], recv_sem=panel_recv.at[s],
                device_id=device, device_id_type=MESH,
            ).wait_recv()

    window = panels[...].reshape(-1, across)
    columns = panel_ref.shape[1]
    panel_ref[...] = jnp.where(
        place % 2 == 0, window[:, :columns], window[:, across - columns :]
    )
    panel = panel_ref[...]
    shape = (2, 2, grad_rows.shape[0], width)

    def product(yp, cp):
        block = w_ref[:, pl.ds(pl.multiple_of((2 * yp + cp) * width, HEAD_DIM), width)]
        return jnp.dot(panel, block, preferred_element_type=jnp.float32).reshape(shape)

    for yp in range(2):
        da_send[yp] = product(yp, 1 - core).astype(jnp.bfloat16)
        da_own[yp] = product(yp, core)
    gain_copy(1).wait_recv()
    gain_all[core, y] = gain_to[1] + gain_from[1]
    gain_side.start()
    attended_side.wait_recv()
    attended_core.start()

    def gather_far(p):
        at = pl.ds(p * step, step)
        return copy(
            gathered_ref.at[hi, lo, :, at], gathered_ref.at[hi, lo, :, at],
            gather_send, gather_recv, (0, p), peers["far"],
        )

    def gather_near(p):
        at = pl.ds(p * step, step)
        return copy(
            gathered_ref.at[:, lo, :, at], gathered_ref.at[:, lo, :, at],
            gather_send, gather_recv, (1, p), peers["near"],
        )

    def da_finish(p, value):
        gathered_ref[hi, lo, :, pl.ds(p * step, step)] = value.astype(jnp.bfloat16)
        gather_far(p).start()
        if p > 0:
            gather_far(p - 1).wait_recv()
            gather_near(p - 1).start()

    drain_da = scatter(
        lambda yp, p: da_send.at[yp, :, :, :, pl.ds(p * step, step)],
        lambda yp, h, l, p: da_own[yp, h, l, :, pl.ds(p * step, step)],
        (da_core, da_to_side, da_side, da_to_near, da_near, da_kept, da_to_far, da_far),
        da_send_sem, da_recv_sem, da_finish,
    )
    gather_far(PIECES - 1).wait_recv()
    gather_near(PIECES - 1).start()
    gain_side.wait_recv()
    gain_core.start()
    attended_core.wait_recv()
    for yp in range(2):
        for cp in range(2):
            at = (2 * yp + cp) * width
            every_attended_ref[:, at : at + width] = attended_all[yp, cp]
    gain_core.wait_recv()
    gain_grad_ref[...] = gain_all[...]
    for p in range(PIECES):
        gather_near(p).wait_recv()
    d_attention_ref[...] = gathered_ref[...]

    drain_parts()
    for sending in inner_copies:
        sending.wait_send()
    for at, device in enumerate(targets):
        @pl.when(not_me(device))
        def _(at=at):
            panel_copy(at).wait_send()
    drain_da()
    for p in range(PIECES):
        gather_far(p).wait_send()
        gather_near(p).wait_send()
    for sending in (gain_copy(0), gain_copy(1), gain_side, gain_core, attended_side, attended_core):
        sending.wait_send()
    units_local.wait()
    units_far.wait()


def middle(part, residual, rstd, out_grad, gain, weights, attended, activated):
    tokens, width = attended.shape
    rows, columns = tokens // 4, weights.shape[0]
    across = -(-columns // HEAD_DIM) * HEAD_DIM
    low, full = jnp.bfloat16, jnp.float32
    chunk = (2, 2, rows, width)
    stages = [
        pltpu.VMEM((2,) + chunk, low),
        pltpu.VMEM(chunk, low),
        pltpu.VMEM(chunk, low),
        pltpu.VMEM((2, rows, width), low),
        pltpu.VMEM((2, rows, width), low),
        pltpu.VMEM((2, rows, width), full),
        pltpu.VMEM((rows, width), low),
        pltpu.VMEM((rows, width), low),
    ]
    hbm = pl.BlockSpec(memory_space=pl.ANY)
    vmem = pl.BlockSpec(memory_space=pltpu.VMEM)
    dma = pltpu.SemaphoreType.DMA
    return pl.pallas_call(
        middle_kernel,
        out_shape=[
            jax.ShapeDtypeStruct((rows, width), low),
            jax.ShapeDtypeStruct((2, 2, 8, width), full),
            jax.ShapeDtypeStruct((tokens, columns), low),
            jax.ShapeDtypeStruct(chunk, low),
            jax.ShapeDtypeStruct((tokens, 4 * width), low),
            jax.ShapeDtypeStruct((2 * activated.shape[0], tokens), low),
        ],
        in_specs=[vmem, hbm, vmem, hbm, vmem, vmem, vmem, hbm],
        out_specs=[vmem] * 5 + [hbm],
        scratch_shapes=[
            pltpu.VMEM((rows, width), low),
            pltpu.VMEM((rows, width), low),
            pltpu.VMEM((2, 8, width), full),
            pltpu.VMEM((2, 8, width), full),
            pltpu.VMEM((2, 2, 8, width), full),
            pltpu.VMEM((2, 2, tokens, width), low),
        ]
        + stages
        + [pltpu.VMEM((rows, width), full)]
        + [pltpu.VMEM((2,) + chunk, low), pltpu.VMEM((2,) + chunk, full)]
        + stages
        + [
            pltpu.VMEM((rows, HEAD_DIM), full),
            pltpu.VMEM((7, rows, HEAD_DIM), full),
            pltpu.VMEM((rows, width), low),
            pltpu.VMEM((2, 2, rows, across), low),
            pltpu.VMEM(chunk, low),
            dma((5, PIECES)), dma((5, PIECES)), dma((5, PIECES)), dma((5, PIECES)),
            dma((7,)), dma((7,)), dma((4,)), dma((4,)), dma((2, PIECES)), dma((2, PIECES)),
            dma((3,)), dma((1,)), dma((1,)), dma((4,)), dma((4,)), dma((2,)), dma((2,)),
        ],
        compiler_params=pltpu.CompilerParams(
            collective_id=0, has_side_effects=True, vmem_limit_bytes=40 << 20
        ),
        cost_estimate=pl.CostEstimate(
            flops=60_000_000_000, bytes_accessed=8 << 20, transcendentals=0
        ),
    )(
        part.reshape(2, 2, rows, -1), residual, rstd, out_grad, gain, weights, attended, activated
    )


def per_device(
    residual,
    norm_gain,
    grad_out,
    w_gate,
    w_up,
    w_down,
    w_output,
    query,
    key,
    value,
    cache_key,
    cache_value,
    visible_from,
):
    wide_place = lax.axis_index("wide")
    side = lax.axis_index("narrow")
    line, group = wide_place >> 2, wide_place & 3
    tokens = residual.shape[0]
    cached = cache_key.shape[0]
    hidden = w_down.shape[0]
    scale = 1.0 / math.sqrt(HEAD_DIM)
    base = scale * LOG2E
    heads = query.shape[1] // (8 * HEAD_DIM)
    group_width = heads * HEAD_DIM
    span = tokens // 4

    def for_side(array, place):
        count = array.shape[0] // 2
        return lax.dynamic_slice_in_dim(array, place * count, count, 0)

    def for_heads(array, place):
        width = array.shape[1] // 8
        return lax.dynamic_slice_in_dim(array, (place * 4 + group) * width, width, 1)

    block = 2 * (group & 1) + (group >> 1)

    stream = residual.astype(jnp.float32)
    gain = norm_gain.astype(jnp.float32)
    squares = narrow_sum(jnp.sum(stream * stream, axis=1))

    near = jnp.concatenate([for_heads(array, side) for array in (query, key, value)], axis=1)
    sent = jnp.concatenate([for_heads(array, 1 - side) for array in (query, key, value)], axis=1)
    stretch = placed(near, swapped(sent, "narrow", 1), side)
    queries = stretch[:, :group_width]
    own = lax.dynamic_slice_in_dim(stretch[:, group_width:], line * span, span, 0)
    own = jnp.pad(own, ((0, HEAD_DIM - span), (0, 0)))
    own = jnp.concatenate([own[:, :HEAD_DIM], own[:, HEAD_DIM:]], axis=0)

    def stacked(m):
        at = (group ^ m) * HEAD_DIM
        return jnp.concatenate(
            [
                lax.dynamic_slice_in_dim(cache, at, HEAD_DIM, 1)
                for cache in (cache_key, cache_value)
            ],
            axis=0,
        )

    cache_blocks = [
        stacked(m) if m == 0 else swapped(stacked(m), "wide", m) for m in range(4)
    ]
    position = jnp.arange(tokens, dtype=jnp.int32)[:, None]
    starts = jnp.stack([((line << 2) | (group ^ m)) * cached for m in range(4)])
    bounds = (
        visible_from[:, None] - starts[None, :],
        jnp.minimum(position - line * span, span - 1),
    )

    def halves(part):
        sent = for_side(part, 1 - side).astype(jnp.bfloat16)
        return sent, swapped(sent, "narrow", 1)

    def across(weights, rows, dim):
        return lax.dot_general(
            weights, rows, (((dim,), (1,)), ((), ())), preferred_element_type=jnp.float32
        )

    hidden_part = across(w_down, grad_out, 1)
    rstd = lax.rsqrt(squares / D + EPSILON)[:, None]
    normed = (stream * rstd * gain).astype(jnp.bfloat16)
    gate_part = across(w_gate, normed, 0)
    up_part = across(w_up, normed, 0)
    matmuls = (hidden_part, gate_part, up_part)
    exchanged = [halves(part) for part in matmuls]
    (early_queries,) = after((queries,), *[sent for sent, _ in exchanged])
    early = online_forward(base, 0, heads, early_queries, bounds, cache_blocks[:2], own, ())
    late = online_forward(
        base, 2, heads, queries, bounds, cache_blocks[2:], None, tuple(early[:2])
    )
    local_out, local_stat = late[:2]
    pairs = cache_blocks[:2] + [own] + cache_blocks[2:]
    places = [(0, 0, 3), (0, 1, 3), (0, 2, 3), (1, 0, 2), (1, 1, 2)]
    gots = after([got for _, got in exchanged], local_out)
    hidden_grad, gate, up = [
        for_side(part, side) + got.astype(jnp.float32) for part, got in zip(matmuls, gots)
    ]
    activated_near, d_gate_near, d_up_near = swiglu_back(gate, up, hidden_grad)
    d_gate, d_up, attended, stats = exchange(
        base, d_gate_near, d_up_near, local_out, local_stat
    )
    def back(grads, weights):
        return lax.dot_general(
            grads, weights, (((0,), (1,)), ((), ())), preferred_element_type=jnp.float32
        )

    d_normed_part = (back(d_gate, w_gate) + back(d_up, w_up)).astype(jnp.bfloat16)

    rstd_rows = lax.dynamic_slice_in_dim(rstd, line * span, span, 0)
    grad_rows, gain_rows, panel, d_attention, every_attended, activated = middle(
        d_normed_part,
        residual,
        jnp.broadcast_to(rstd_rows, (span, HEAD_DIM)),
        grad_out,
        lax.dynamic_slice_in_dim(gain, block * group_width, group_width, 0)[None, :],
        w_output.T,
        attended,
        activated_near,
    )
    d_attention = d_attention.reshape(tokens, group_width)
    grad_gain = gain_rows[:, :, 0].reshape(-1)

    def interleaved(pair, other):
        low = (group & 1) == 0
        width = group_width
        first, second = jnp.where(low, pair, other), jnp.where(low, other, pair)
        return jnp.concatenate(
            [first[:, :width], second[:, :width], first[:, width:], second[:, width:]], axis=1
        )

    query_part, grad_residual = query_backward(
        base, scale, heads, d_attention, attended, places, pairs, early[3:] + late[3:],
        (early[2], late[2]), stats, grad_rows,
    )

    def outer(grads):
        return lax.dot_general(
            normed, grads, (((0,), (1,)), ((), ())), preferred_element_type=jnp.float32
        ).astype(jnp.bfloat16)

    query_low = query_part.astype(jnp.bfloat16)

    def query_rows(array, at):
        return lax.dynamic_slice_in_dim(array, at * span, span, 0)

    d_gate, d_up, activated, panel = after((d_gate, d_up, activated, panel), query_part)
    got = [swapped(query_rows(query_low, line ^ m), "wide", m << 2) for m in (1, 2, 3)]
    grad_w_gate = outer(d_gate)
    got = after(got, grad_w_gate)
    total = query_rows(query_part, line)
    for piece in got:
        total = total + piece.astype(jnp.float32)
    total = total.astype(jnp.bfloat16)
    held = [total] + [swapped(total, "wide", m << 2) for m in (1, 2, 3)]
    (d_up,) = after((d_up,), grad_w_gate)
    grad_w_up = outer(d_up)
    held = after(held, grad_w_up)
    own_query = joined(
        joined(held[0], held[1], line & 1, 0), joined(held[2], held[3], line & 1, 0), line >> 1, 0
    )
    side_query = swapped(own_query, "wide", 2)
    (activated,) = after((activated,), grad_w_up)
    grad_w_down = jnp.dot(
        activated, grad_out, preferred_element_type=jnp.float32
    ).astype(jnp.bfloat16)
    (side_query,) = after((side_query,), grad_w_down)
    pair = joined(own_query, side_query, group >> 1, 1)
    core_query = swapped(pair, "wide", 1)
    (panel,) = after((panel,), grad_w_down)
    grad_w_output = contract_rows(every_attended, panel).astype(jnp.bfloat16)
    (core_query,) = after((core_query,), grad_w_output)
    grad_query = interleaved(pair, core_query)
    return (
        grad_residual,
        grad_gain,
        grad_w_gate,
        grad_w_up,
        grad_w_down,
        grad_w_output,
        grad_query,
    )


def solution(mesh):
    in_specs = (
        P(None, "narrow"),
        P("narrow"),
        P(None, "narrow"),
        P("narrow", "wide"),
        P("narrow", "wide"),
        P("wide", "narrow"),
        P("narrow", "wide"),
        P("narrow", None),
        P("narrow", None),
        P("narrow", None),
        P("wide", "narrow"),
        P("wide", "narrow"),
        P(),
    )
    out_specs = (
        P(None, "narrow"),
        P("narrow"),
        P("narrow", "wide"),
        P("narrow", "wide"),
        P("wide", "narrow"),
        P("narrow", "wide"),
        P(None, "narrow"),
    )
    planes = mesh.shape["wide"] == 16 and mesh.shape["narrow"] == 2
    body = per_device if planes else per_device_general
    return jax.shard_map(
        body, mesh=mesh, in_specs=in_specs, out_specs=out_specs, check_vma=False
    )
```

```python
import functools
import math

import jax
import jax.numpy as jnp
from jax import lax
from jax.experimental import pallas as pl
from jax.experimental.pallas import tpu as pltpu
from jax.sharding import PartitionSpec as P

D = 5120
HEAD_DIM = 128


EPSILON = 1e-06


def contract_rows(left, right):
    return lax.dot_general(
        left, right, (((0,), (0,)), ((), ())), preferred_element_type=jnp.float32
    )


def contract_cols(left, right):
    return lax.dot_general(
        left, right, (((1,), (1,)), ((), ())), preferred_element_type=jnp.float32
    )


def swapped(array, axis, mask):
    size = lax.axis_size(axis)
    return lax.ppermute(array, axis, [(i, i ^ mask) for i in range(size)])


def wide_bits():
    return lax.axis_size("wide").bit_length() - 1


def bit_of(k):
    return (lax.axis_index("wide") >> k) & 1


def as_cube(array):
    count = lax.axis_size("wide")
    return array.reshape((2,) * wide_bits() + (array.shape[0] // count, array.shape[1]))


def masks(stage):
    found = [0]
    for k in stage:
        found += [mask | (1 << k) for mask in found]
    return found


def part_for(cube, stage, mask):
    for k in stage:
        cube = lax.dynamic_slice_in_dim(cube, bit_of(k) ^ ((mask >> k) & 1), 1, k)
    return cube


def scatter_sum(cube, stages):
    for stage in stages:
        low = cube.astype(jnp.bfloat16)
        total = part_for(cube, stage, 0).astype(jnp.float32)
        for mask in masks(stage)[1:]:
            got = swapped(part_for(low, stage, mask), "wide", mask)
            total = total + got.astype(jnp.float32)
        cube = total
    return cube.reshape(cube.shape[-2:])


def gathered(chunk, stages):
    cube = chunk.reshape((1,) * wide_bits() + chunk.shape)
    for stage in reversed(stages):
        held = {0: cube}
        for mask in masks(stage)[1:]:
            held[mask] = swapped(cube, "wide", mask)
        for k in stage:
            first = bit_of(k) == 0
            held = {
                mask: jnp.concatenate(
                    [
                        jnp.where(first, held[mask], held[mask | (1 << k)]),
                        jnp.where(first, held[mask | (1 << k)], held[mask]),
                    ],
                    axis=k,
                )
                for mask in held
                if not mask & (1 << k)
            }
        cube = held[0]
    return cube.reshape(-1, cube.shape[-1])


def own_rows(array):
    bits = wide_bits()
    rows = array.shape[0] // lax.axis_size("wide")
    at = sum(bit_of(k) << (bits - 1 - k) for k in range(bits))
    return lax.dynamic_slice_in_dim(array, at * rows, rows, 0)


def doubled(value, combine):
    for k in range(wide_bits()):
        value = combine(value, swapped(value, "wide", 1 << k))
    return value


def orders():
    core, side, line = (0,), (1,), tuple(range(2, wide_bits()))
    return ([core, side, line], [core, line, side])


def narrow_sum(part):
    if lax.axis_size("narrow") == 2:
        return part + swapped(part, "narrow", 1)
    return lax.psum(part, "narrow")


def narrow_total(part, low):
    if lax.axis_size("narrow") == 2:
        return part + swapped(low, "narrow", 1).astype(jnp.float32)
    return lax.psum(part, "narrow")


def after(arrays, *others):
    return lax.optimization_barrier((tuple(arrays), others))[0]


def to_heads(rows):
    if lax.axis_size("narrow") != 2:
        return lax.all_to_all(rows, "narrow", split_axis=1, concat_axis=0, tiled=True)
    place = lax.axis_index("narrow")
    half = rows.shape[1] // 2
    count = rows.shape[0] // 2
    bit = bit_of(0)
    kept = lax.dynamic_slice_in_dim(rows, place * half, half, 1)
    sent = lax.dynamic_slice(rows, (bit * count, (1 - place) * half), (count, half))
    got = swapped(sent, "narrow", 1)
    other = swapped(got, "wide", 1)
    first = bit == 0
    far = jnp.concatenate([jnp.where(first, got, other), jnp.where(first, other, got)], axis=0)
    low = place == 0
    return jnp.concatenate([jnp.where(low, kept, far), jnp.where(low, far, kept)], axis=0)


def merge_softmax(base, first, second):
    heads = first.shape[1] // 2
    top = jnp.maximum(first[:, :heads], second[:, :heads])
    total = first[:, heads:] * jnp.exp2((first[:, :heads] - top) * base) + second[
        :, heads:
    ] * jnp.exp2((second[:, :heads] - top) * base)
    return jnp.concatenate([top, total], axis=1)


def swiglu_back(gate, up, hidden_grad):
    sigmoid_gate = jax.nn.sigmoid(gate)
    silu_gate = gate * sigmoid_gate
    activated = (silu_gate * up).astype(jnp.bfloat16)
    d_gate = (hidden_grad * up * sigmoid_gate * (1.0 + gate * (1.0 - sigmoid_gate))).astype(
        jnp.bfloat16
    )
    d_up = (hidden_grad * silu_gate).astype(jnp.bfloat16)
    return (activated, d_gate, d_up)


LOG2E = 1.4426950408889634
MASKED = -1e30


def raw_scores(q, key_ref, own_key_ref, from_ref, own_ref):
    cached = contract_cols(q, key_ref[...])
    at = lax.broadcasted_iota(jnp.int32, cached.shape, 1)
    cached = jnp.where(at >= from_ref[...], cached, MASKED)
    own = contract_cols(q, own_key_ref[...])
    own_at = lax.broadcasted_iota(jnp.int32, own.shape, 1)
    own = jnp.where(own_at <= own_ref[...], own, MASKED)
    return (cached, own)


def pick_lane(stat_ref, head):
    lane = lax.broadcasted_iota(jnp.int32, stat_ref.shape, 1)
    return jnp.sum(jnp.where(lane == head, stat_ref[...], 0.0), axis=1, keepdims=True)


def forward_kernel(
    per_group, base, q_ref, key_ref, value_ref, own_key_ref, own_value_ref,
    from_ref, own_ref, out_ref, top_ref, total_ref,
):
    head = pl.program_id(0) * per_group + pl.program_id(1)

    @pl.when(head == 0)
    def _():
        top_ref[...] = jnp.zeros_like(top_ref)
        total_ref[...] = jnp.zeros_like(total_ref)

    cached, own = raw_scores(q_ref[...], key_ref, own_key_ref, from_ref, own_ref)
    top = jnp.maximum(
        jnp.max(cached, axis=1, keepdims=True), jnp.max(own, axis=1, keepdims=True)
    )
    cached = jnp.exp2((cached - top) * base)
    own = jnp.exp2((own - top) * base)
    total = jnp.sum(cached, axis=1, keepdims=True) + jnp.sum(own, axis=1, keepdims=True)
    out = jnp.dot(
        cached.astype(jnp.bfloat16), value_ref[...], preferred_element_type=jnp.float32
    ) + jnp.dot(
        own.astype(jnp.bfloat16), own_value_ref[...], preferred_element_type=jnp.float32
    )
    out_ref[...] = out.astype(out_ref.dtype)
    lane = lax.broadcasted_iota(jnp.int32, top_ref.shape, 1)
    top_ref[...] = jnp.where(lane == head, top, top_ref[...])
    total_ref[...] = jnp.where(lane == head, total, total_ref[...])


def backward_kernel(
    first_group, per_group, base, scale, q_ref, grad_ref, attended_ref, key_ref, value_ref,
    own_key_ref, own_value_ref, from_ref, own_ref, top_ref, inverse_ref, out_ref,
):
    head = (first_group + pl.program_id(0)) * per_group + pl.program_id(1)
    cached, own = raw_scores(q_ref[...], key_ref, own_key_ref, from_ref, own_ref)
    top = pick_lane(top_ref, head)
    inverse = pick_lane(inverse_ref, head)
    grad = grad_ref[...]
    delta = jnp.sum(
        grad.astype(jnp.float32) * attended_ref[...].astype(jnp.float32),
        axis=1,
        keepdims=True,
    )
    cached = jnp.exp2((cached - top) * base) * (contract_cols(grad, value_ref[...]) - delta)
    own = jnp.exp2((own - top) * base) * (contract_cols(grad, own_value_ref[...]) - delta)
    out = jnp.dot(
        cached.astype(jnp.bfloat16), key_ref[...], preferred_element_type=jnp.float32
    ) + jnp.dot(
        own.astype(jnp.bfloat16), own_key_ref[...], preferred_element_type=jnp.float32
    )
    out_ref[...] = (out * (inverse * scale)).astype(out_ref.dtype)


def blocks(tokens, cached, padded, per_group, first):
    head = pl.BlockSpec((tokens, HEAD_DIM), lambda g, p: (0, (first + g) * per_group + p))
    rows = pl.BlockSpec((cached, HEAD_DIM), lambda g, p: (0, first + g))
    own = pl.BlockSpec((padded, HEAD_DIM), lambda g, p: (0, first + g))
    bound = pl.BlockSpec((tokens, 1), lambda g, p: (0, 0))
    stat = pl.BlockSpec((tokens, HEAD_DIM), lambda g, p: (0, 0))
    here = pl.BlockSpec((tokens, HEAD_DIM), lambda g, p: (0, g * per_group + p))
    return (head, rows, own, bound, stat, here)


def forward(
    first, groups, per_group, base, queries, keys, values, own_keys, own_values, bounds
):
    tokens = queries.shape[0]
    cached, padded = keys.shape[0], own_keys.shape[0]
    head, rows, own, bound, stat, here = blocks(tokens, cached, padded, per_group, first)
    work = groups * per_group * tokens * (cached + padded)
    return pl.pallas_call(
        functools.partial(forward_kernel, per_group, base),
        grid=(groups, per_group),
        in_specs=[head, rows, rows, own, own, bound, bound],
        out_specs=[here, stat, stat],
        out_shape=[
            jax.ShapeDtypeStruct((tokens, groups * per_group * HEAD_DIM), jnp.float32),
            jax.ShapeDtypeStruct((tokens, HEAD_DIM), jnp.float32),
            jax.ShapeDtypeStruct((tokens, HEAD_DIM), jnp.float32),
        ],
        compiler_params=pltpu.CompilerParams(vmem_limit_bytes=40 << 20),
        cost_estimate=pl.CostEstimate(
            flops=16 * HEAD_DIM * work, bytes_accessed=20 << 20, transcendentals=work
        ),
    )(queries, keys, values, own_keys, own_values, *bounds)


def backward(
    first, groups, per_group, base, scale, queries, grads, attended, keys, values,
    own_keys, own_values, bounds, top, inverse,
):
    tokens = queries.shape[0]
    cached, padded = keys.shape[0], own_keys.shape[0]
    head, rows, own, bound, stat, here = blocks(tokens, cached, padded, per_group, first)
    work = groups * per_group * tokens * (cached + padded)
    return pl.pallas_call(
        functools.partial(backward_kernel, first, per_group, base, scale),
        grid=(groups, per_group),
        in_specs=[head, here, head, rows, rows, own, own, bound, bound, stat, stat],
        out_specs=here,
        out_shape=jax.ShapeDtypeStruct(grads.shape, jnp.float32),
        compiler_params=pltpu.CompilerParams(vmem_limit_bytes=58 << 20),
        cost_estimate=pl.CostEstimate(
            flops=16 * HEAD_DIM * work, bytes_accessed=12 << 20, transcendentals=work
        ),
    )(queries, grads, attended, keys, values, own_keys, own_values, *bounds, top, inverse)


def split_columns(array, pieces):
    width = array.shape[1] // pieces
    return [array[:, i * width : (i + 1) * width] for i in range(pieces)]


def per_device_general(
    residual,
    norm_gain,
    grad_out,
    w_gate,
    w_up,
    w_down,
    w_output,
    query,
    key,
    value,
    cache_key,
    cache_value,
    visible_from,
):
    wide_count = lax.axis_size("wide")
    wide_place = lax.axis_index("wide")
    tokens = residual.shape[0]
    scale = 1.0 / math.sqrt(HEAD_DIM)
    base = scale * LOG2E

    stream = residual.astype(jnp.float32)
    gain = norm_gain.astype(jnp.float32)
    hidden_part = contract_cols(grad_out, w_down)
    squares = narrow_sum(jnp.sum(stream * stream, axis=1))
    rstd = lax.rsqrt(squares / D + EPSILON)[:, None]
    normed = (stream * rstd * gain).astype(jnp.bfloat16)
    gate_part = jnp.dot(normed, w_gate, preferred_element_type=jnp.float32)
    up_part = jnp.dot(normed, w_up, preferred_element_type=jnp.float32)

    queries, stretch_keys, stretch_values = (to_heads(query), to_heads(key), to_heads(value))
    groups = stretch_keys.shape[1] // HEAD_DIM
    per_group = queries.shape[1] // stretch_keys.shape[1]
    heads = groups * per_group
    cached = cache_key.shape[0]
    span = tokens // wide_count
    start = wide_place * span
    padded = -(-span // HEAD_DIM) * HEAD_DIM
    filler = ((0, padded - span), (0, 0))
    own_keys = jnp.pad(lax.dynamic_slice_in_dim(stretch_keys, start, span, 0), filler)
    own_values = jnp.pad(lax.dynamic_slice_in_dim(stretch_values, start, span, 0), filler)
    position = jnp.arange(tokens, dtype=jnp.int32)[:, None]
    bounds = (
        visible_from[:, None] - wide_place * cached,
        jnp.minimum(position - start, span - 1),
    )

    lows = [part.astype(jnp.bfloat16) for part in (hidden_part, gate_part, up_part)]
    hidden_grad = narrow_total(hidden_part, lows[0])
    gate = narrow_total(gate_part, lows[1])
    up = narrow_total(up_part, lows[2])

    queries, own_keys, own_values = after((queries, own_keys, own_values), *lows)
    early = groups - groups // 4
    outs, tops, totals = [], [], []
    for first, count in ((0, early), (early, groups - early)):
        if count == 0:
            continue
        if first:
            (queries,) = after((queries,), hidden_grad, gate, up)
        out, top, total = forward(
            first, count, per_group, base, queries, cache_key, cache_value, own_keys,
            own_values, bounds,
        )
        outs.append(out)
        tops.append(top[:, : count * per_group])
        totals.append(total[:, : count * per_group])
    local_out = jnp.concatenate(outs, axis=1)
    local_top = jnp.concatenate(tops, axis=1)
    stats = doubled(
        jnp.concatenate([local_top] + totals, axis=1), functools.partial(merge_softmax, base)
    )
    top, inverse = stats[:, :heads], 1.0 / stats[:, heads:]
    factor = jnp.exp2((local_top - top) * base) * inverse
    owner = jnp.arange(heads * HEAD_DIM, dtype=jnp.int32)[None, :] // HEAD_DIM
    choose = (owner == jnp.arange(heads, dtype=jnp.int32)[:, None]).astype(jnp.float32)
    attended_part = local_out * jnp.dot(factor, choose, precision=lax.Precision.HIGHEST)
    side = ((0, 0), (0, HEAD_DIM - heads))
    top, inverse = jnp.pad(top, side), jnp.pad(inverse, side)
    ways = orders()
    attended = jnp.concatenate(
        [
            gathered(scatter_sum(as_cube(part), way).astype(jnp.bfloat16), way)
            for part, way in zip(split_columns(attended_part, 2), ways)
        ],
        axis=1,
    )

    activated, d_gate, d_up = swiglu_back(gate, up, hidden_grad)
    d_normed_part = contract_cols(d_gate, w_gate) + contract_cols(d_up, w_up)
    d_normed = jnp.concatenate(
        [
            scatter_sum(as_cube(part), way)
            for part, way in zip(split_columns(d_normed_part, 2), ways)
        ],
        axis=1,
    )
    rstd_rows = own_rows(rstd)
    scaled = own_rows(residual).astype(jnp.float32) * rstd_rows
    grad_gain = doubled(jnp.sum(d_normed * scaled, axis=0), jnp.add)
    weighted = d_normed * gain
    inner = narrow_sum(jnp.sum(weighted * scaled, axis=1)) / D
    grad_rows = (
        own_rows(grad_out).astype(jnp.float32)
        + rstd_rows * (weighted - scaled * inner[:, None])
    ).astype(jnp.bfloat16)
    grad_residual = jnp.concatenate(
        [gathered(part, way) for part, way in zip(split_columns(grad_rows, 2), ways)], axis=1
    )

    columns = w_output.shape[1]
    width = grad_residual.shape[1]
    if lax.axis_size("narrow") == 2:
        own_panel = lax.dynamic_slice_in_dim(
            grad_residual, (wide_place * columns) % width, columns, 1
        )
        holder = (wide_place * columns) // width == lax.axis_index("narrow")
        panel = jnp.where(holder, own_panel, swapped(own_panel, "narrow", 1))
    else:
        whole = lax.all_gather(grad_residual, "narrow", axis=1, tiled=True)
        panel = lax.dynamic_slice_in_dim(whole, wide_place * columns, columns, 1)
    pieces = 2 if groups % 2 == 0 else 1
    group_count = groups // pieces
    query_grads, query_parts = [], []
    for piece in range(pieces):
        way = ways[piece]
        wide_rows = group_count * per_group * HEAD_DIM
        rows = w_output[piece * wide_rows : (piece + 1) * wide_rows]
        d_attention = gathered(
            scatter_sum(as_cube(contract_cols(panel, rows)), way).astype(jnp.bfloat16), way
        )
        query_part = backward(
            piece * group_count, group_count, per_group, base, scale, queries, d_attention,
            attended, cache_key, cache_value, own_keys, own_values, bounds, top, inverse,
        )
        query_parts.append(query_part)
        query_grads.append(
            gathered(scatter_sum(as_cube(query_part), way).astype(jnp.bfloat16), way)
        )
    grad_query = jnp.concatenate(query_grads, axis=1)
    activated, d_gate, d_up, panel = after((activated, d_gate, d_up, panel), *query_parts)
    grad_w_down = contract_rows(activated, grad_out).astype(jnp.bfloat16)
    grad_w_gate = contract_rows(normed, d_gate).astype(jnp.bfloat16)
    grad_w_up = contract_rows(normed, d_up).astype(jnp.bfloat16)
    grad_w_output = contract_rows(attended, panel).astype(jnp.bfloat16)
    return (
        grad_residual,
        grad_gain,
        grad_w_gate,
        grad_w_up,
        grad_w_down,
        grad_w_output,
        grad_query,
    )


def block_scores(q, pair_ref, from_ref, block):
    rows = pair_ref.shape[0] // 2
    cached = contract_cols(q, pair_ref[:rows, :])
    at = lax.broadcasted_iota(jnp.int32, cached.shape, 1)
    return jnp.where(at >= from_ref[:, block : block + 1], cached, MASKED)


def own_scores(q, pair_ref, own_ref):
    own = contract_cols(q, pair_ref[: pair_ref.shape[0] // 2, :])
    own_at = lax.broadcasted_iota(jnp.int32, own.shape, 1)
    return jnp.where(own_at <= own_ref[...], own, MASKED)


STATS = HEAD_DIM // 2
MESH = pl.DeviceIdType.MESH


def online_kernel(base, first, count, has_own, q_ref, from_ref, own_ref, *refs):
    pairs = refs[: count + has_own]
    rest = refs[count + has_own :]
    earlier, (out_ref, stat_ref) = rest[:-2], rest[-2:]
    head = pl.program_id(0)

    @pl.when(head == 0)
    def _():
        stat_ref[...] = jnp.zeros_like(stat_ref)

    q = q_ref[...]
    top = total = out = None
    if earlier:
        out_before, stat_before = earlier
        top, total = pick_lane(stat_before, head), pick_lane(stat_before, head + STATS)
        out = out_before[...]
    for at, pair in enumerate(pairs):
        rows = pair.shape[0] // 2
        if at < count:
            scores = block_scores(q, pair, from_ref, first + at)
        else:
            scores = own_scores(q, pair, own_ref)
        later = jnp.max(scores, axis=1, keepdims=True)
        if top is not None:
            later = jnp.maximum(top, later)
            shrink = jnp.exp2((top - later) * base)
            total, out = total * shrink, out * shrink
        scores = jnp.exp2((scores - later) * base)
        added = jnp.sum(scores, axis=1, keepdims=True)
        product = jnp.dot(
            scores.astype(jnp.bfloat16), pair[rows:, :], preferred_element_type=jnp.float32
        )
        total = added if top is None else total + added
        out = product if top is None else out + product
        top = later
    out_ref[...] = (out / total if earlier else out).astype(out_ref.dtype)
    lane = lax.broadcasted_iota(jnp.int32, stat_ref.shape, 1)
    stat_ref[...] = jnp.where(
        lane == head, top, jnp.where(lane == head + STATS, total, stat_ref[...])
    )


def online_forward(base, first, heads, queries, bounds, blocks, own, earlier):
    tokens = queries.shape[0]
    whole = lambda array: pl.BlockSpec(array.shape, lambda h: (0, 0))
    here = pl.BlockSpec((tokens, HEAD_DIM), lambda h: (0, h))
    stat = pl.BlockSpec((tokens, HEAD_DIM), lambda h: (0, 0))
    pairs = list(blocks) + ([] if own is None else [own])
    work = heads * tokens * sum(pair.shape[0] // 2 for pair in pairs)
    rest = (*bounds, *pairs)
    kind = jnp.bfloat16 if earlier else jnp.float32
    return pl.pallas_call(
        functools.partial(online_kernel, base, first, len(blocks), int(own is not None)),
        grid=(heads,),
        in_specs=[here] + [whole(array) for array in rest] + ([here, stat] if earlier else []),
        out_specs=[here, stat],
        out_shape=[
            jax.ShapeDtypeStruct((tokens, heads * HEAD_DIM), kind),
            jax.ShapeDtypeStruct((tokens, HEAD_DIM), jnp.float32),
        ],
        compiler_params=pltpu.CompilerParams(vmem_limit_bytes=58 << 20),
        cost_estimate=pl.CostEstimate(
            flops=HEAD_DIM * work, bytes_accessed=1 << 20, transcendentals=work // 8
        ),
    )(queries, *rest, *earlier)


def query_kernel(
    base, scale, count, q_ref, grad_ref, attended_ref, from_ref, own_ref, *refs
):
    pairs = refs[: count + 1]
    stat_ref, rows_ref, out_ref, grad_residual_ref, residuals, row_send, row_recv = refs[
        count + 1 :
    ]
    head = pl.program_id(0)
    place = lax.axis_index("wide")
    x = lax.axis_index("narrow")
    line, group = place // 4, place % 4
    y, core = group // 2, group % 2
    hi, lo = line // 2, line % 2

    def flip(bit):
        weight = 1 << bit
        return (place + weight - 2 * weight * ((place // weight) % 2), x)

    peers = [flip(bit) for bit in (3, 2, 1, 0)]

    def sending(stage):
        ref = (
            residuals.at[core, y, hi, lo],
            residuals.at[core, y, :, lo],
            residuals.at[core, y],
            residuals.at[core],
        )[stage]
        return pltpu.make_async_remote_copy(
            src_ref=ref, dst_ref=ref, send_sem=row_send.at[stage], recv_sem=row_recv.at[stage],
            device_id=peers[stage], device_id_type=MESH,
        )

    @pl.when(head == 0)
    def _():
        barrier = pltpu.get_barrier_semaphore()
        for device in peers:
            pl.semaphore_signal(barrier, inc=1, device_id=device, device_id_type=MESH)
        pl.semaphore_wait(barrier, 4)
        residuals[core, y, hi, lo] = rows_ref[...]
        sending(0).start()

    for stage, step in ((1, 1), (2, 2), (3, 4)):
        @pl.when(head == step)
        def _(stage=stage):
            sending(stage - 1).wait_recv()
            sending(stage).start()

    top = pick_lane(stat_ref, head)
    inverse = pick_lane(stat_ref, head + STATS)
    q, grad = q_ref[...], grad_ref[...]
    delta = jnp.sum(
        grad.astype(jnp.float32) * attended_ref[...].astype(jnp.float32), axis=1, keepdims=True
    )
    out = None
    for at, pair in enumerate(pairs):
        rows = pair.shape[0] // 2
        if at < count:
            scores = block_scores(q, pair, from_ref, at)
        else:
            scores = own_scores(q, pair, own_ref)
        scores = jnp.exp2((scores - top) * base) * (contract_cols(grad, pair[rows:, :]) - delta)
        product = jnp.dot(
            scores.astype(jnp.bfloat16), pair[:rows, :], preferred_element_type=jnp.float32
        )
        out = out + product if at else product
    out_ref[...] = out * (inverse * scale)

    @pl.when(head == pl.num_programs(0) - 1)
    def _():
        sending(3).wait_recv()
        width = rows_ref.shape[1]
        for cp in range(2):
            for yp in range(2):
                at = (2 * cp + yp) * width
                grad_residual_ref[:, :, :, at : at + width] = residuals[cp, yp]
        for stage in range(4):
            sending(stage).wait_send()


def query_backward(
    base, scale, heads, queries, grads, attended, bounds, blocks, own, stats, grad_rows
):
    tokens = queries.shape[0]
    span, width = grad_rows.shape
    whole = lambda array: pl.BlockSpec(array.shape, lambda h: (0, 0))
    head = pl.BlockSpec((tokens, HEAD_DIM), lambda h: (0, h))
    pairs = list(blocks) + [own]
    work = heads * tokens * sum(pair.shape[0] // 2 for pair in pairs)
    rest = (*bounds, *pairs, stats, grad_rows)
    result = (2, 2, span, 4 * width)
    dma = pltpu.SemaphoreType.DMA
    query_part, grad_residual = pl.pallas_call(
        functools.partial(query_kernel, base, scale, len(blocks)),
        grid=(heads,),
        in_specs=[head, head, head] + [whole(array) for array in rest],
        out_specs=[head, pl.BlockSpec(result, lambda h: (0, 0, 0, 0))],
        out_shape=[
            jax.ShapeDtypeStruct((tokens, width), jnp.float32),
            jax.ShapeDtypeStruct(result, jnp.bfloat16),
        ],
        scratch_shapes=[
            pltpu.VMEM((2, 2, 2, 2, span, width), jnp.bfloat16),
            dma((4,)), dma((4,)),
        ],
        compiler_params=pltpu.CompilerParams(
            collective_id=2, has_side_effects=True, vmem_limit_bytes=58 << 20
        ),
        cost_estimate=pl.CostEstimate(
            flops=12 * HEAD_DIM * work, bytes_accessed=12 << 20, transcendentals=work
        ),
    )(queries, grads, attended, *rest)
    return query_part, grad_residual.reshape(tokens, -1)


def placed(near, far, first):
    low = first == 0
    return jnp.concatenate([jnp.where(low, near, far), jnp.where(low, far, near)], axis=0)


def joined(near, far, bit, axis):
    low = bit == 0
    return jnp.concatenate([jnp.where(low, near, far), jnp.where(low, far, near)], axis=axis)


def line_scatter(part, line):
    rows = part.shape[0] // 4
    low = part.astype(jnp.bfloat16)
    total = lax.dynamic_slice_in_dim(part, line * rows, rows, 0)
    for m in (1, 2, 3):
        sent = lax.dynamic_slice_in_dim(low, (line ^ m) * rows, rows, 0)
        total = total + swapped(sent, "wide", m << 2).astype(jnp.float32)
    return total


def line_gather(chunk, line):
    held = [chunk if m == 0 else swapped(chunk, "wide", m << 2) for m in range(4)]
    return joined(
        joined(held[0], held[1], line & 1, 0), joined(held[2], held[3], line & 1, 0), line >> 1, 0
    )


def side_gather(block, group):
    return joined(block, swapped(block, "wide", 2), group >> 1, 1)


def core_gather(block, group):
    return joined(block, swapped(block, "wide", 1), group & 1, 1)


PIECES = 5
def exchange_kernel(
    base, d_gate_ref, d_up_ref, out_ref, stat_ref,
    every_gate, every_up, attended_ref, stats_ref,
    outs, stats, rows, row_stats, all_rows, all_stats,
    local_sem, x_send, x_recv, send_sem, recv_sem,
):
    place = lax.axis_index("wide")
    x = lax.axis_index("narrow")
    line, group = place // 4, place % 4
    count = d_gate_ref.shape[0]
    lines = [place + 4 * (1 - 2 * (line % 2)), place + 8 * (1 - 2 * (line // 2))]
    lines.append(lines[0] + lines[1] - place)
    at_line = [at // 4 for at in lines]
    barrier = pltpu.get_barrier_semaphore()
    pl.semaphore_signal(barrier, inc=1, device_id=(place, 1 - x), device_id_type=MESH)
    for peer in lines:
        pl.semaphore_signal(barrier, inc=1, device_id=(peer, x), device_id_type=MESH)
    pl.semaphore_wait(barrier, 4)

    here = pl.ds(pl.multiple_of(x * count, 16), count)
    moves = []
    for at, (src, dst) in enumerate(((d_gate_ref, every_gate), (d_up_ref, every_up))):
        far = pltpu.make_async_remote_copy(
            src_ref=src, dst_ref=dst.at[here], send_sem=x_send.at[at], recv_sem=x_recv.at[at],
            device_id=(place, 1 - x), device_id_type=MESH,
        )
        near = pltpu.make_async_copy(src, dst.at[here], local_sem.at[at])
        far.start()
        near.start()
        moves += [far, near]

    def line_copy(src, dst, at, m):
        return pltpu.make_async_remote_copy(
            src_ref=src, dst_ref=dst, send_sem=send_sem.at[at, m], recv_sem=recv_sem.at[at, m],
            device_id=(lines[m], x), device_id_type=MESH,
        )

    def scattered(m):
        return (
            line_copy(out_ref.at[at_line[m]], outs.at[m], 0, m),
            line_copy(stat_ref.at[at_line[m]], stats.at[m], 1, m),
        )

    for m in range(3):
        for sending in scattered(m):
            sending.start()
    for m in range(3):
        for sending in scattered(m):
            sending.wait_recv()
    parts = [stat_ref[line]] + [stats[m] for m in range(3)]
    top = functools.reduce(jnp.maximum, parts)
    lane = lax.broadcasted_iota(jnp.int32, top.shape, 1)
    weights = [
        jnp.where(
            lane < STATS, 0.0, pltpu.roll(jnp.exp2((part - top) * base), STATS, 1) * part
        )
        for part in parts
    ]
    total = functools.reduce(jnp.add, weights)
    inverse = 1.0 / jnp.where(total > 0.0, total, 1.0)
    row_stats[...] = jnp.where(lane < STATS, top, inverse)
    all_stats[line] = row_stats[...]
    weights = [weight * inverse for weight in weights]
    for h in range(rows.shape[1] // HEAD_DIM):
        cols = slice(h * HEAD_DIM, (h + 1) * HEAD_DIM)
        pieces = [out_ref[line, :, cols]] + [outs[m, :, cols] for m in range(3)]
        value = functools.reduce(
            jnp.add,
            [
                piece.astype(jnp.float32) * weight[:, STATS + h : STATS + h + 1]
                for piece, weight in zip(pieces, weights)
            ],
        )
        rows[:, cols] = value.astype(jnp.bfloat16)
    all_rows[line] = rows[...]

    def spread(m, where):
        return (
            line_copy(rows, all_rows.at[where], 2, m),
            line_copy(row_stats, all_stats.at[where], 3, m),
        )

    for m in range(3):
        for sending in spread(m, line):
            sending.start()
    for m in range(3):
        for sending in spread(m, at_line[m]):
            sending.wait_recv()
    attended_ref[...] = all_rows[...]
    stats_ref[...] = all_stats[...]
    for m in range(3):
        for sending in scattered(m) + spread(m, line):
            sending.wait_send()
    for move in moves:
        move.wait()


def exchange(base, d_gate, d_up, out, stat):
    tokens, width = out.shape
    span = tokens // 4
    low, full = jnp.bfloat16, jnp.float32
    vmem = pl.BlockSpec(memory_space=pltpu.VMEM)
    hbm = pl.BlockSpec(memory_space=pl.ANY)
    dma = pltpu.SemaphoreType.DMA
    every = jax.ShapeDtypeStruct((2 * d_gate.shape[0], d_gate.shape[1]), low)
    every_gate, every_up, attended, stats = pl.pallas_call(
        functools.partial(exchange_kernel, base),
        out_shape=[
            every,
            every,
            jax.ShapeDtypeStruct((4, span, width), low),
            jax.ShapeDtypeStruct((4, span, HEAD_DIM), full),
        ],
        in_specs=[hbm, hbm, vmem, vmem],
        out_specs=[hbm, hbm, vmem, vmem],
        scratch_shapes=[
            pltpu.VMEM((3, span, width), low),
            pltpu.VMEM((3, span, HEAD_DIM), full),
            pltpu.VMEM((span, width), low),
            pltpu.VMEM((span, HEAD_DIM), full),
            pltpu.VMEM((4, span, width), low),
            pltpu.VMEM((4, span, HEAD_DIM), full),
            dma((2,)), dma((2,)), dma((2,)), dma((4, 3)), dma((4, 3)),
        ],
        compiler_params=pltpu.CompilerParams(
            collective_id=1, has_side_effects=True, vmem_limit_bytes=40 << 20
        ),
        cost_estimate=pl.CostEstimate(
            flops=20_000_000_000, bytes_accessed=8 << 20, transcendentals=0
        ),
    )(d_gate, d_up, out.reshape(4, span, width), stat.reshape(4, span, HEAD_DIM))
    return every_gate, every_up, attended.reshape(tokens, width), stats.reshape(tokens, HEAD_DIM)


def middle_kernel(
    part_ref, residual_ref, rstd_ref, out_grad_ref, gain_ref, w_ref, attended_ref, activated_ref,
    rows_ref, gain_grad_ref, panel_ref, d_attention_ref, every_attended_ref, every_activated,
    residual_rows, out_grad_rows, gain_to, gain_from, gain_all, attended_all,
    from_core, to_side, from_side, to_near, from_near, kept, to_far, from_far, summed,
    da_send, da_own, da_core, da_to_side, da_side, da_to_near, da_near, da_kept, da_to_far, da_far,
    inner_to, inner_from, grad_rows, panels, gathered_ref,
    send_sem, recv_sem, da_send_sem, da_recv_sem, inner_send, inner_recv,
    panel_send, panel_recv, gather_send, gather_recv,
    local_sem, x_send, x_recv, gain_send, gain_recv, attended_send, attended_recv,
):
    place = lax.axis_index("wide")
    x = lax.axis_index("narrow")
    line, group = place // 4, place % 4
    y, core = group // 2, group % 2
    hi, lo = line // 2, line % 2
    span, width = rows_ref.shape
    step = width // PIECES
    block = 2 * core + y

    def flip(bit):
        weight = 1 << bit
        at = (place // weight) % 2
        return (place + weight - 2 * weight * at, x)

    peers = {"core": flip(0), "side": flip(1), "near": flip(2), "far": flip(3), "x": (place, 1 - x)}
    targets = [(8 * x + 2 * block + j, nx) for j in (0, 1) for nx in (0, 1)]
    source_x, source_block = place // 8, (place % 8) // 2
    source_group = 2 * (source_block % 2) + source_block // 2
    sources = [(4 * s + source_group, source_x) for s in range(4)]

    def is_me(device):
        return jnp.logical_and(device[0] == place, device[1] == x)

    def not_me(device):
        return jnp.logical_not(is_me(device))

    side_place, core_place = peers["side"][0], peers["core"][0]
    corner = side_place + core_place - place
    others = [
        (at, nx)
        for nx in (x, 1 - x)
        for at in (place, core_place, side_place, corner)
    ][1:]
    barrier = pltpu.get_barrier_semaphore()
    for device in [peers["near"], peers["far"]] + others:
        pl.semaphore_signal(barrier, inc=1, device_id=device, device_id_type=MESH)
    for device in targets + sources:
        @pl.when(not_me(device))
        def _(device=device):
            pl.semaphore_signal(barrier, inc=1, device_id=device, device_id_type=MESH)
    mine = jnp.logical_and(place // 8 == x, source_group == group).astype(jnp.int32)
    pl.semaphore_wait(barrier, 17 - 2 * mine)

    def copy(src, dst, sends, recvs, at, device):
        return pltpu.make_async_remote_copy(
            src_ref=src, dst_ref=dst, send_sem=sends.at[at], recv_sem=recvs.at[at],
            device_id=device, device_id_type=MESH,
        )

    here = (
        pl.ds(pl.multiple_of(line * span, 16), span),
        pl.ds(pl.multiple_of(block * width, HEAD_DIM), width),
    )
    loads = [
        pltpu.make_async_copy(residual_ref.at[here], residual_rows, local_sem.at[0]),
        pltpu.make_async_copy(out_grad_ref.at[here], out_grad_rows, local_sem.at[1]),
    ]
    count = activated_ref.shape[0]
    own_units = every_activated.at[pl.ds(pl.multiple_of(x * count, 16), count)]
    units_local = pltpu.make_async_copy(activated_ref, own_units, local_sem.at[2])
    units_far = pltpu.make_async_remote_copy(
        src_ref=activated_ref, dst_ref=own_units, send_sem=x_send.at[0], recv_sem=x_recv.at[0],
        device_id=peers["x"], device_id_type=MESH,
    )
    for load in loads + [units_local, units_far]:
        load.start()

    def scatter(outgoing, own, bufs, sends, recvs, finish):
        core_buf, side_out, side_in, near_out, near_in, keep, far_out, far_in = bufs

        def cols(p):
            return pl.ds(p * step, step)

        def core_copy(yp, p):
            return copy(
                outgoing(yp, p), core_buf.at[yp, :, :, :, cols(p)], sends, recvs,
                (yp, p), peers["core"],
            )

        def side_copy(p):
            return copy(
                side_out.at[:, :, :, cols(p)], side_in.at[:, :, :, cols(p)], sends, recvs,
                (2, p), peers["side"],
            )

        def near_copy(p):
            return copy(
                near_out.at[:, :, cols(p)], near_in.at[:, :, cols(p)], sends, recvs,
                (3, p), peers["near"],
            )

        def far_copy(p):
            return copy(
                far_out.at[:, cols(p)], far_in.at[:, cols(p)], sends, recvs,
                (4, p), peers["far"],
            )

        def stage(s, p):
            if s == 0:
                core_copy(0, p).start()
                core_copy(1, p).start()
            elif s == 1:
                core_copy(0, p).wait_recv()
                core_copy(1, p).wait_recv()
                for h in range(2):
                    for l in range(2):
                        value = own(1 - y, h, l, p) + core_buf[1 - y, h, l, :, cols(p)].astype(
                            jnp.float32
                        )
                        side_out[h, l, :, cols(p)] = value.astype(jnp.bfloat16)
                side_copy(p).start()
            elif s == 2:
                side_copy(p).wait_recv()

                def total(h, l):
                    return (
                        own(y, h, l, p)
                        + core_buf[y, h, l, :, cols(p)].astype(jnp.float32)
                        + side_in[h, l, :, cols(p)].astype(jnp.float32)
                    )

                for h in range(2):
                    near_out[h, :, cols(p)] = total(h, 1 - lo).astype(jnp.bfloat16)
                near_copy(p).start()
                for h in range(2):
                    keep[h, :, cols(p)] = total(h, lo)
            elif s == 3:
                near_copy(p).wait_recv()

                def total(h):
                    return keep[h, :, cols(p)] + near_in[h, :, cols(p)].astype(jnp.float32)

                far_out[:, cols(p)] = total(1 - hi).astype(jnp.bfloat16)
                far_copy(p).start()
            else:
                far_copy(p).wait_recv()
                finish(
                    p,
                    keep[hi, :, cols(p)]
                    + near_in[hi, :, cols(p)].astype(jnp.float32)
                    + far_in[:, cols(p)].astype(jnp.float32),
                )

        for p in range(PIECES):
            stage(0, p)
        for t in range(-2, PIECES + 2):
            for s, p in ((2, t), (1, t + 2), (3, t - 1), (4, t - 2)):
                if 0 <= p < PIECES:
                    stage(s, p)

        def drain():
            for p in range(PIECES):
                core_copy(0, p).wait_send()
                core_copy(1, p).wait_send()
                side_copy(p).wait_send()
                near_copy(p).wait_send()
                far_copy(p).wait_send()

        return drain

    def part_cols(yp, cp, p):
        return pl.ds(pl.multiple_of((2 * cp + yp) * width + p * step, HEAD_DIM), step)

    def part_finish(p, value):
        summed[:, pl.ds(p * step, step)] = value

    drain_parts = scatter(
        lambda yp, p: part_ref.at[:, :, :, part_cols(yp, 1 - core, p)],
        lambda yp, h, l, p: part_ref[h, l, :, part_cols(yp, core, p)].astype(jnp.float32),
        (from_core, to_side, from_side, to_near, from_near, kept, to_far, from_far),
        send_sem, recv_sem, part_finish,
    )

    attended_all[y, core] = attended_ref[...]
    attended_side = copy(
        attended_all.at[y, core], attended_all.at[y, core], attended_send, attended_recv, 0,
        peers["side"],
    )
    attended_core = copy(
        attended_all.at[:, core], attended_all.at[:, core], attended_send, attended_recv, 1,
        peers["core"],
    )
    for load in loads:
        load.wait()
    d_normed = summed[...]
    scaled = residual_rows[...].astype(jnp.float32) * rstd_ref[:, :1]
    weighted = d_normed * gain_ref[...]
    inner = jnp.sum(weighted * scaled, axis=1, keepdims=True)
    inner_to[...] = jnp.broadcast_to(inner, inner_to.shape)
    inner_copies = [
        copy(inner_to, inner_from.at[at], inner_send, inner_recv, at, device)
        for at, device in enumerate(others)
    ]
    for sending in inner_copies:
        sending.start()

    def gain_copy(at):
        return copy(
            gain_to.at[at], gain_from.at[at], gain_send, gain_recv, at, peers[("near", "far")[at]]
        )

    gain_side = copy(
        gain_all.at[core, y], gain_all.at[core, y], gain_send, gain_recv, 2, peers["side"]
    )
    gain_core = copy(
        gain_all.at[core], gain_all.at[core], gain_send, gain_recv, 3, peers["core"]
    )
    gain_to[0] = jnp.broadcast_to(
        jnp.sum(d_normed * scaled, axis=0, keepdims=True), gain_to.shape[1:]
    )
    for sending in inner_copies:
        sending.wait_recv()
    inner = functools.reduce(
        jnp.add, [inner_from[at] for at in range(len(others))], inner_to[...]
    )
    gain_copy(0).start()
    attended_side.start()
    inner = inner[:, :1] * (1.0 / D)
    rows = (
        out_grad_rows[...].astype(jnp.float32) + rstd_ref[:, :1] * (weighted - scaled * inner)
    ).astype(jnp.bfloat16)
    grad_rows[...] = rows
    across = panels.shape[3]
    starts = (0, width - across)

    def panel_copy(at):
        j = at // 2
        return pltpu.make_async_remote_copy(
            src_ref=grad_rows.at[:, pl.ds(starts[j], across)], dst_ref=panels.at[hi, lo],
            send_sem=panel_send.at[at], recv_sem=panel_recv.at[line],
            device_id=targets[at], device_id_type=MESH,
        )

    for at, device in enumerate(targets):
        @pl.when(not_me(device))
        def _(at=at):
            panel_copy(at).start()

        @pl.when(is_me(device))
        def _(at=at):
            begin = starts[at // 2]
            panels[hi, lo] = grad_rows[:, begin : begin + across]
    rows_ref[...] = rows
    gain_copy(0).wait_recv()
    gain_to[1] = gain_to[0] + gain_from[0]
    gain_copy(1).start()
    for s, device in enumerate(sources):
        @pl.when(not_me(device))
        def _(s=s, device=device):
            pltpu.make_async_remote_copy(
                src_ref=grad_rows.at[:, pl.ds(0, across)], dst_ref=panels.at[s // 2, s % 2],
                send_sem=panel_send.at[0], recv_sem=panel_recv.at[s],
                device_id=device, device_id_type=MESH,
            ).wait_recv()

    window = panels[...].reshape(-1, across)
    columns = panel_ref.shape[1]
    panel_ref[...] = jnp.where(
        place % 2 == 0, window[:, :columns], window[:, across - columns :]
    )
    panel = panel_ref[...]
    shape = (2, 2, grad_rows.shape[0], width)

    def product(yp, cp):
        block = w_ref[:, pl.ds(pl.multiple_of((2 * yp + cp) * width, HEAD_DIM), width)]
        return jnp.dot(panel, block, preferred_element_type=jnp.float32).reshape(shape)

    for yp in range(2):
        da_send[yp] = product(yp, 1 - core).astype(jnp.bfloat16)
        da_own[yp] = product(yp, core)
    gain_copy(1).wait_recv()
    gain_all[core, y] = gain_to[1] + gain_from[1]
    gain_side.start()
    attended_side.wait_recv()
    attended_core.start()

    def gather_far(p):
        at = pl.ds(p * step, step)
        return copy(
            gathered_ref.at[hi, lo, :, at], gathered_ref.at[hi, lo, :, at],
            gather_send, gather_recv, (0, p), peers["far"],
        )

    def gather_near(p):
        at = pl.ds(p * step, step)
        return copy(
            gathered_ref.at[:, lo, :, at], gathered_ref.at[:, lo, :, at],
            gather_send, gather_recv, (1, p), peers["near"],
        )

    def da_finish(p, value):
        gathered_ref[hi, lo, :, pl.ds(p * step, step)] = value.astype(jnp.bfloat16)
        gather_far(p).start()
        if p > 0:
            gather_far(p - 1).wait_recv()
            gather_near(p - 1).start()

    drain_da = scatter(
        lambda yp, p: da_send.at[yp, :, :, :, pl.ds(p * step, step)],
        lambda yp, h, l, p: da_own[yp, h, l, :, pl.ds(p * step, step)],
        (da_core, da_to_side, da_side, da_to_near, da_near, da_kept, da_to_far, da_far),
        da_send_sem, da_recv_sem, da_finish,
    )
    gather_far(PIECES - 1).wait_recv()
    gather_near(PIECES - 1).start()
    gain_side.wait_recv()
    gain_core.start()
    attended_core.wait_recv()
    for yp in range(2):
        for cp in range(2):
            at = (2 * yp + cp) * width
            every_attended_ref[:, at : at + width] = attended_all[yp, cp]
    gain_core.wait_recv()
    gain_grad_ref[...] = gain_all[...]
    for p in range(PIECES):
        gather_near(p).wait_recv()
    d_attention_ref[...] = gathered_ref[...]

    drain_parts()
    for sending in inner_copies:
        sending.wait_send()
    for at, device in enumerate(targets):
        @pl.when(not_me(device))
        def _(at=at):
            panel_copy(at).wait_send()
    drain_da()
    for p in range(PIECES):
        gather_far(p).wait_send()
        gather_near(p).wait_send()
    for sending in (gain_copy(0), gain_copy(1), gain_side, gain_core, attended_side, attended_core):
        sending.wait_send()
    units_local.wait()
    units_far.wait()


def middle(part, residual, rstd, out_grad, gain, weights, attended, activated):
    tokens, width = attended.shape
    rows, columns = tokens // 4, weights.shape[0]
    across = -(-columns // HEAD_DIM) * HEAD_DIM
    low, full = jnp.bfloat16, jnp.float32
    chunk = (2, 2, rows, width)
    stages = [
        pltpu.VMEM((2,) + chunk, low),
        pltpu.VMEM(chunk, low),
        pltpu.VMEM(chunk, low),
        pltpu.VMEM((2, rows, width), low),
        pltpu.VMEM((2, rows, width), low),
        pltpu.VMEM((2, rows, width), full),
        pltpu.VMEM((rows, width), low),
        pltpu.VMEM((rows, width), low),
    ]
    hbm = pl.BlockSpec(memory_space=pl.ANY)
    vmem = pl.BlockSpec(memory_space=pltpu.VMEM)
    dma = pltpu.SemaphoreType.DMA
    return pl.pallas_call(
        middle_kernel,
        out_shape=[
            jax.ShapeDtypeStruct((rows, width), low),
            jax.ShapeDtypeStruct((2, 2, 8, width), full),
            jax.ShapeDtypeStruct((tokens, columns), low),
            jax.ShapeDtypeStruct(chunk, low),
            jax.ShapeDtypeStruct((tokens, 4 * width), low),
            jax.ShapeDtypeStruct((2 * activated.shape[0], tokens), low),
        ],
        in_specs=[vmem, hbm, vmem, hbm, vmem, vmem, vmem, hbm],
        out_specs=[vmem] * 5 + [hbm],
        scratch_shapes=[
            pltpu.VMEM((rows, width), low),
            pltpu.VMEM((rows, width), low),
            pltpu.VMEM((2, 8, width), full),
            pltpu.VMEM((2, 8, width), full),
            pltpu.VMEM((2, 2, 8, width), full),
            pltpu.VMEM((2, 2, tokens, width), low),
        ]
        + stages
        + [pltpu.VMEM((rows, width), full)]
        + [pltpu.VMEM((2,) + chunk, low), pltpu.VMEM((2,) + chunk, full)]
        + stages
        + [
            pltpu.VMEM((rows, HEAD_DIM), full),
            pltpu.VMEM((7, rows, HEAD_DIM), full),
            pltpu.VMEM((rows, width), low),
            pltpu.VMEM((2, 2, rows, across), low),
            pltpu.VMEM(chunk, low),
            dma((5, PIECES)), dma((5, PIECES)), dma((5, PIECES)), dma((5, PIECES)),
            dma((7,)), dma((7,)), dma((4,)), dma((4,)), dma((2, PIECES)), dma((2, PIECES)),
            dma((3,)), dma((1,)), dma((1,)), dma((4,)), dma((4,)), dma((2,)), dma((2,)),
        ],
        compiler_params=pltpu.CompilerParams(
            collective_id=0, has_side_effects=True, vmem_limit_bytes=40 << 20
        ),
        cost_estimate=pl.CostEstimate(
            flops=60_000_000_000, bytes_accessed=8 << 20, transcendentals=0
        ),
    )(
        part.reshape(2, 2, rows, -1), residual, rstd, out_grad, gain, weights, attended, activated
    )


def per_device(
    residual,
    norm_gain,
    grad_out,
    w_gate,
    w_up,
    w_down,
    w_output,
    query,
    key,
    value,
    cache_key,
    cache_value,
    visible_from,
):
    wide_place = lax.axis_index("wide")
    side = lax.axis_index("narrow")
    line, group = wide_place >> 2, wide_place & 3
    tokens = residual.shape[0]
    cached = cache_key.shape[0]
    hidden = w_down.shape[0]
    scale = 1.0 / math.sqrt(HEAD_DIM)
    base = scale * LOG2E
    heads = query.shape[1] // (8 * HEAD_DIM)
    group_width = heads * HEAD_DIM
    span = tokens // 4

    def for_side(array, place):
        count = array.shape[0] // 2
        return lax.dynamic_slice_in_dim(array, place * count, count, 0)

    def for_heads(array, place):
        width = array.shape[1] // 8
        return lax.dynamic_slice_in_dim(array, (place * 4 + group) * width, width, 1)

    block = 2 * (group & 1) + (group >> 1)

    stream = residual.astype(jnp.float32)
    gain = norm_gain.astype(jnp.float32)
    squares = narrow_sum(jnp.sum(stream * stream, axis=1))

    near = jnp.concatenate([for_heads(array, side) for array in (query, key, value)], axis=1)
    sent = jnp.concatenate([for_heads(array, 1 - side) for array in (query, key, value)], axis=1)
    stretch = placed(near, swapped(sent, "narrow", 1), side)
    queries = stretch[:, :group_width]
    own = lax.dynamic_slice_in_dim(stretch[:, group_width:], line * span, span, 0)
    own = jnp.pad(own, ((0, HEAD_DIM - span), (0, 0)))
    own = jnp.concatenate([own[:, :HEAD_DIM], own[:, HEAD_DIM:]], axis=0)

    def stacked(m):
        at = (group ^ m) * HEAD_DIM
        return jnp.concatenate(
            [
                lax.dynamic_slice_in_dim(cache, at, HEAD_DIM, 1)
                for cache in (cache_key, cache_value)
            ],
            axis=0,
        )

    cache_blocks = [
        stacked(m) if m == 0 else swapped(stacked(m), "wide", m) for m in range(4)
    ]
    position = jnp.arange(tokens, dtype=jnp.int32)[:, None]
    starts = jnp.stack([((line << 2) | (group ^ m)) * cached for m in range(4)])
    bounds = (
        visible_from[:, None] - starts[None, :],
        jnp.minimum(position - line * span, span - 1),
    )

    def halves(part):
        sent = for_side(part, 1 - side).astype(jnp.bfloat16)
        return sent, swapped(sent, "narrow", 1)

    def across(weights, rows, dim):
        return lax.dot_general(
            weights, rows, (((dim,), (1,)), ((), ())), preferred_element_type=jnp.float32
        )

    hidden_part = across(w_down, grad_out, 1)
    rstd = lax.rsqrt(squares / D + EPSILON)[:, None]
    normed = (stream * rstd * gain).astype(jnp.bfloat16)
    gate_part = across(w_gate, normed, 0)
    up_part = across(w_up, normed, 0)
    matmuls = (hidden_part, gate_part, up_part)
    exchanged = [halves(part) for part in matmuls]
    (early_queries,) = after((queries,), *[sent for sent, _ in exchanged])
    early = online_forward(base, 0, heads, early_queries, bounds, cache_blocks[:2], own, ())
    local_out, local_stat = online_forward(
        base, 2, heads, queries, bounds, cache_blocks[2:], None, early
    )
    gots = after([got for _, got in exchanged], local_out)
    hidden_grad, gate, up = [
        for_side(part, side) + got.astype(jnp.float32) for part, got in zip(matmuls, gots)
    ]
    activated_near, d_gate_near, d_up_near = swiglu_back(gate, up, hidden_grad)
    d_gate, d_up, attended, stats = exchange(
        base, d_gate_near, d_up_near, local_out, local_stat
    )
    def back(grads, weights):
        return lax.dot_general(
            grads, weights, (((0,), (1,)), ((), ())), preferred_element_type=jnp.float32
        )

    d_normed_part = (back(d_gate, w_gate) + back(d_up, w_up)).astype(jnp.bfloat16)

    rstd_rows = lax.dynamic_slice_in_dim(rstd, line * span, span, 0)
    grad_rows, gain_rows, panel, d_attention, every_attended, activated = middle(
        d_normed_part,
        residual,
        jnp.broadcast_to(rstd_rows, (span, HEAD_DIM)),
        grad_out,
        lax.dynamic_slice_in_dim(gain, block * group_width, group_width, 0)[None, :],
        w_output.T,
        attended,
        activated_near,
    )
    d_attention = d_attention.reshape(tokens, group_width)
    grad_gain = gain_rows[:, :, 0].reshape(-1)

    def interleaved(pair, other):
        low = (group & 1) == 0
        width = group_width
        first, second = jnp.where(low, pair, other), jnp.where(low, other, pair)
        return jnp.concatenate(
            [first[:, :width], second[:, :width], first[:, width:], second[:, width:]], axis=1
        )

    query_part, grad_residual = query_backward(
        base, scale, heads, queries, d_attention, attended, bounds, cache_blocks, own, stats,
        grad_rows,
    )

    def outer(grads):
        return lax.dot_general(
            normed, grads, (((0,), (1,)), ((), ())), preferred_element_type=jnp.float32
        ).astype(jnp.bfloat16)

    query_low = query_part.astype(jnp.bfloat16)

    def query_rows(array, at):
        return lax.dynamic_slice_in_dim(array, at * span, span, 0)

    d_gate, d_up, activated, panel = after((d_gate, d_up, activated, panel), query_part)
    got = [swapped(query_rows(query_low, line ^ m), "wide", m << 2) for m in (1, 2, 3)]
    grad_w_gate = outer(d_gate)
    got = after(got, grad_w_gate)
    total = query_rows(query_part, line)
    for piece in got:
        total = total + piece.astype(jnp.float32)
    total = total.astype(jnp.bfloat16)
    held = [total] + [swapped(total, "wide", m << 2) for m in (1, 2, 3)]
    (d_up,) = after((d_up,), grad_w_gate)
    grad_w_up = outer(d_up)
    held = after(held, grad_w_up)
    own_query = joined(
        joined(held[0], held[1], line & 1, 0), joined(held[2], held[3], line & 1, 0), line >> 1, 0
    )
    side_query = swapped(own_query, "wide", 2)
    (activated,) = after((activated,), grad_w_up)
    grad_w_down = jnp.dot(
        activated, grad_out, preferred_element_type=jnp.float32
    ).astype(jnp.bfloat16)
    (side_query,) = after((side_query,), grad_w_down)
    pair = joined(own_query, side_query, group >> 1, 1)
    core_query = swapped(pair, "wide", 1)
    (panel,) = after((panel,), grad_w_down)
    grad_w_output = contract_rows(every_attended, panel).astype(jnp.bfloat16)
    (core_query,) = after((core_query,), grad_w_output)
    grad_query = interleaved(pair, core_query)
    return (
        grad_residual,
        grad_gain,
        grad_w_gate,
        grad_w_up,
        grad_w_down,
        grad_w_output,
        grad_query,
    )


def solution(mesh):
    in_specs = (
        P(None, "narrow"),
        P("narrow"),
        P(None, "narrow"),
        P("narrow", "wide"),
        P("narrow", "wide"),
        P("wide", "narrow"),
        P("narrow", "wide"),
        P("narrow", None),
        P("narrow", None),
        P("narrow", None),
        P("wide", "narrow"),
        P("wide", "narrow"),
        P(),
    )
    out_specs = (
        P(None, "narrow"),
        P("narrow"),
        P("narrow", "wide"),
        P("narrow", "wide"),
        P("wide", "narrow"),
        P("narrow", "wide"),
        P(None, "narrow"),
    )
    planes = mesh.shape["wide"] == 16 and mesh.shape["narrow"] == 2
    body = per_device if planes else per_device_general
    return jax.shard_map(
        body, mesh=mesh, in_specs=in_specs, out_specs=out_specs, check_vma=False
    )
```
